512 devices in a mesh: slab: 128 (over x, z, core), sub: 4 (over y).
Axes of the slice: x: 4, y: 4, z: 16, core: 2. Of those that a mesh axis runs over, the one named last changes fastest.
Arguments:
- ensemble: float32 [2, 15, 80, 65536], P(None, None, None, ('slab', 'sub')), may hold values from -6 to 6
- obs_value: float32 [2, 256], replicated, may hold values from -6 to 6
- obs_var: float32 [2, 256], replicated, may hold values from 0.5 to 4
- obs_owner: int32 [2, 256, 1], replicated, may hold values from 0 to 127; in each aligned block of 256 rows (0 to 255, 256 to 511, ..., all dimensions but the last counted through in order) at most 8 rows name the same one
- obs_column: int32 [2, 256], replicated, may hold values from 0 to 511
- home_block: int32 [2, 256], replicated, may hold values from -1 to 1
- batch_order: int32 [2], replicated, may hold values from 0 to 1, each once
Outputs:
- analysis: float32 [2, 15, 80, 65536], P(None, None, None, ('slab', 'sub'))
- assimilated_priors: float32 [2, 256, 160], replicated
The draws below stay inside these ranges and needn't reach their ends.
Inputs may be any that keep to these rules, and one draw needn't show every extreme that they name: `obs_owner`: in each batch no slab owns more than 8 observations; in some batch one slab owns exactly 8. `batch_order`: each batch appears once.
All inputs are finite; a program needn't handle non-finite values.
Results may differ from the reference program's by a relative error of at most 0.00012.
Values sent between devices are 32-bit elements; how exact they have to be, the bound alone decides.
A program may use at most 64 MiB of HBM per device.

```python
import math
import jax
import jax.numpy as jnp
import numpy as np
from jax import lax

M = 80
LV = 15
BANDS = 2
BLK = 16
BATCHES = 2
CAP = 8
OBS_BATCH = 256
COLS_SLAB = 512
COLS_TOTAL = 65536
NBLK = 4096
SPAN_BROAD = 8
SPAN_NARROW = 2
N_SLAB = 128


def plant(result, stream_key, least, top_value):
    longest = result.shape.index(max(result.shape))
    spots = []
    for shift in (0, 1):
        where = [jax.random.randint(jax.random.fold_in(stream_key, axis), (), 0, length) for axis, length in enumerate(result.shape)]
        where[longest] = (where[longest] + shift) % result.shape[longest]
        spots.append(tuple(where))
    return result.at[spots[0]].set(least).at[spots[1]].set(top_value)


def steps_of(stream_key, shape, shards, least, top_value):
    loudness, own = 1.0, jax.random.fold_in(stream_key, 6)
    for axis_at, parts in shards:
        steps = jnp.exp(jax.random.uniform(jax.random.fold_in(own, axis_at), (parts,), jnp.float32, least / len(shards), top_value / len(shards)))
        loudness = loudness * jnp.repeat(steps, shape[axis_at] // parts).reshape([-1 if axis == axis_at else 1 for axis in range(len(shape))])
    return loudness


def shared_out(own_key, own, number, rows, count, top, limit, slope):
    order = jax.random.permutation(own_key, count)
    packed, ordinary = shares(count, rows * top, limit, slope, True), shares(count, rows * top, limit, slope, False)
    places = jnp.arange(count)

    def named(sizes, offset_by):
        used = int((sizes > 0).sum())
        fixed = max(1, used // 4)
        passed = fixed + (places - fixed + offset_by * (used - fixed)) % max(1, count - fixed)
        return jnp.zeros((count,), jnp.int32).at[order[jnp.where(places < fixed, places, passed)]].set(jnp.asarray(sizes, jnp.int32))

    sizes = jnp.where(number % 4 == 0, named(packed, number // 4), named(ordinary, number - number // 4 - 1))
    mixed = jax.random.permutation(jax.random.fold_in(own, 3), count)
    source_of, sink = mixed[0:count // 2 * 2:2], mixed[1:count // 2 * 2:2]
    slack = jnp.minimum(sizes[source_of] - 1, limit - sizes[sink]) // 2
    slack = jnp.where((source_of == order[0]) | (sink == order[0]) | (sizes[sink] == 0), 0, jnp.maximum(slack, 0))
    passed = jax.random.randint(jax.random.fold_in(own, 4), (count // 2,), 0, 1 << 20) % (slack + 1)
    sizes = sizes.at[source_of].add(-passed).at[sink].add(passed)
    items = jnp.searchsorted(jnp.cumsum(sizes), jnp.arange(rows * top), side="right").astype(jnp.int32)
    grid = items.reshape(top, rows).T
    grid = grid[jax.random.permutation(jax.random.fold_in(own, 1), rows)]
    offset_by = jax.random.randint(jax.random.fold_in(own, 2), (rows, 1), 0, top)
    return jnp.take_along_axis(grid, (jnp.arange(top)[None, :] + offset_by) % top, axis=1)


def shares(count, total, reach, slope, full):
    weights = [(1 << 20) // math.isqrt(rank ** slope) + 1 for rank in range(1, count + 1)]
    largest = reach if full else min(reach, max(-(-total // count), total * weights[0] // sum(weights)))
    least = 1 if total - largest >= count - 1 else 0
    holding, rest = [largest] + [least] * (count - 1), total - largest - least * (count - 1)
    while rest > 0:
        movable = [i for i in range(1, count) if holding[i] < largest] or [i for i in range(1, count) if holding[i] < reach]
        whole, remaining = sum([weights[i] for i in movable]), rest
        for i in movable:
            more = min(reach - holding[i], max(1, remaining * weights[i] // whole), rest)
            holding[i] = holding[i] + more
            rest = rest - more
    return np.array(holding)


def bell_draw(own_key, dims, scale, bound, shards=(), held_as=jnp.bfloat16):
    result = scale * jax.random.normal(own_key, dims, jnp.float32)
    if shards:
        result = result * steps_of(own_key, dims, shards, -0.22, 0.18)
    return jnp.clip(result, -bound, bound).astype(held_as)


def setup_inputs(seed: int = 0) -> dict:
    arg_keys = jax.random.split(jax.random.key(seed), 8)
    ensemble = bell_draw(arg_keys[0], (BANDS, LV, M, COLS_TOTAL), 1.0, 6.0, ((3, 512),), jnp.float32)
    obs_value = bell_draw(arg_keys[1], (BATCHES, OBS_BATCH), 1.5, 6.0, (), jnp.float32)
    obs_var = jnp.clip(jnp.exp(jax.random.uniform(arg_keys[2], (BATCHES, OBS_BATCH), jnp.float32, math.log(0.5), math.log(4.0))), 0.5, 4.0)
    obs_owner_keys = jax.random.split(jax.random.fold_in(arg_keys[3], 1), BATCHES * OBS_BATCH // OBS_BATCH)
    obs_owner_turns = jax.random.permutation(jax.random.fold_in(arg_keys[3], 3), BATCHES * OBS_BATCH // OBS_BATCH)
    obs_owner = jax.vmap(lambda own, number: shared_out(jax.random.fold_in(arg_keys[3], 2), own, number, OBS_BATCH, N_SLAB, 1, CAP, 2))(obs_owner_keys, obs_owner_turns).reshape((BATCHES, OBS_BATCH, 1))
    obs_column = plant(jax.random.randint(arg_keys[4], (BATCHES, OBS_BATCH), 0, COLS_SLAB), jax.random.fold_in(arg_keys[4], 1), 0, COLS_SLAB - 1).astype(jnp.int32)
    home_block = plant(jax.random.randint(arg_keys[5], (BATCHES, OBS_BATCH), -1, 2), jax.random.fold_in(arg_keys[5], 1), -1, 1).astype(jnp.int32)
    batch_order = jax.random.permutation(arg_keys[6], BATCHES).astype(jnp.int32)
    return dict(ensemble=ensemble, obs_value=obs_value, obs_var=obs_var, obs_owner=obs_owner, obs_column=obs_column, home_block=home_block, batch_order=batch_order)


HIGHEST = lax.Precision.HIGHEST

def gc_weight(first, second, nblocks, length):
    block_gap = jnp.abs(first - second)
    block_gap = jnp.minimum(block_gap, nblocks - block_gap)
    scaled_gap = block_gap.astype(jnp.float32) / length
    near_part = ((-0.25 * scaled_gap + 0.5) * scaled_gap + 0.625) * scaled_gap ** 3 - 5.0 / 3.0 * scaled_gap ** 2 + 1.0
    floored = jnp.maximum(scaled_gap, 1.0)
    far_part = ((((scaled_gap / 12.0 - 0.5) * scaled_gap + 0.625) * scaled_gap + 5.0 / 3.0) * scaled_gap - 5.0) * scaled_gap + 4.0 - 2.0 / (3.0 * floored)
    return jnp.where(scaled_gap <= 1.0, near_part, jnp.where(scaled_gap < 2.0, far_part, 0.0))

def obs_statistics(current, values, variances, members):
    banded = current.reshape(current.shape[0], BANDS, members)
    whole_obs = lax.optimization_barrier(jnp.sum(banded, axis=1))
    centre = lax.optimization_barrier(jnp.mean(whole_obs, axis=1, keepdims=True))
    spread = lax.optimization_barrier(jnp.sum((whole_obs - centre) ** 2, axis=1)) / (members - 1) + 1e-06
    post_var = 1.0 / (1.0 / spread + 1.0 / variances)
    post_mean = post_var * (centre[:, 0] / spread + values / variances)
    increments = (post_mean - centre[:, 0])[:, None] + (jnp.sqrt(post_var / spread) - 1.0)[:, None] * (whole_obs - centre)
    deviations = banded - lax.optimization_barrier(jnp.mean(banded, axis=2, keepdims=True))
    return (deviations, spread, increments)

def update_pool(prior_pool, pool_homes, deviations, spread, increments, obs_homes, nblocks, decays):
    members = deviations.shape[2]
    banded = prior_pool.reshape(prior_pool.shape[0], prior_pool.shape[1], BANDS, members)
    new_bands = []
    for band_no in range(BANDS):
        pool_band = banded[:, :, band_no, :]
        pool_dev = pool_band - lax.optimization_barrier(jnp.mean(pool_band, axis=2, keepdims=True))
        weights = gc_weight(pool_homes[:, :, None], obs_homes[None, None, :], nblocks, decays[band_no]) / ((members - 1) * spread)[None, None, :]
        crossed = jnp.einsum('bpm,km->bpk', pool_dev, deviations[:, band_no, :], precision=HIGHEST)
        change = jnp.einsum('bpk,km->bpm', crossed * weights, increments, precision=HIGHEST)
        new_bands.append(pool_band + change)
    return jnp.stack(new_bands, axis=2).reshape(prior_pool.shape)

def update_state(ensemble, col_blocks, deviations, spread, increments, obs_homes, nblocks, decays):
    members = ensemble.shape[2]
    new_bands = []
    for band_no in range(BANDS):
        band_layer = ensemble[band_no]
        layer_dev = band_layer - lax.optimization_barrier(jnp.mean(band_layer, axis=1, keepdims=True))
        obs_dev = deviations[:, band_no, :]
        weights = gc_weight(col_blocks[:, None], obs_homes[None, :], nblocks, decays[band_no]) / ((members - 1) * spread)[None, :]

        def one_level(level_dev):
            crossed = jnp.einsum('mc,km->ck', level_dev, obs_dev, precision=HIGHEST)
            return jnp.einsum('ck,km->mc', crossed * weights, increments, precision=HIGHEST)
        change = lax.map(one_level, layer_dev)
        new_bands.append(band_layer + change)
    return jnp.stack(new_bands, axis=0)

def reference(ensemble, obs_value, obs_var, obs_owner, obs_column, home_block, batch_order):
    members = ensemble.shape[2]
    level_of = jnp.arange(OBS_BATCH, dtype=jnp.int32) % LV
    global_col = (obs_owner[:, :, 0] * COLS_SLAB + obs_column).astype(jnp.int32)
    obs_home = jnp.mod(global_col // BLK + home_block, NBLK).astype(jnp.int32)
    levels = jnp.broadcast_to(level_of[None, :], global_col.shape)
    picked = ensemble[:, levels, :, global_col]
    priors = picked.reshape(BATCHES, OBS_BATCH, BANDS * members)
    col_blocks = (jnp.arange(COLS_TOTAL, dtype=jnp.int32) // BLK).astype(jnp.int32)
    decays = (float(SPAN_BROAD), float(SPAN_NARROW))
    recorded = jnp.zeros((BATCHES, OBS_BATCH, BANDS * members), jnp.float32)
    for step_no in range(BATCHES):
        batch_id = batch_order[step_no]
        current = priors[batch_id]
        recorded = recorded.at[batch_id].set(current)
        deviations, spread, increments = obs_statistics(current, obs_value[batch_id], obs_var[batch_id], members)
        obs_homes = obs_home[batch_id]
        ensemble = update_state(ensemble, col_blocks, deviations, spread, increments, obs_homes, NBLK, decays)
        priors = update_pool(priors, obs_home, deviations, spread, increments, obs_homes, NBLK, decays)
    return (ensemble, recorded)
```

```python
import jax
import jax.numpy as jnp
from jax import lax
from jax.sharding import PartitionSpec as P

BANDS = 2
BLK = 16
BATCHES = 2
CAP = 8


HIGHEST = lax.Precision.HIGHEST


def gc_weight(first, second, nblocks, length):
    block_gap = jnp.abs(first - second)
    block_gap = jnp.minimum(block_gap, nblocks - block_gap)
    scaled_gap = block_gap.astype(jnp.float32) / length
    near_part = (
        ((-0.25 * scaled_gap + 0.5) * scaled_gap + 0.625) * scaled_gap**3
        - 5.0 / 3.0 * scaled_gap**2
        + 1.0
    )
    floored = jnp.maximum(scaled_gap, 1.0)
    far_part = (
        (
            (((scaled_gap / 12.0 - 0.5) * scaled_gap + 0.625) * scaled_gap + 5.0 / 3.0) * scaled_gap
            - 5.0
        )
        * scaled_gap
        + 4.0
        - 2.0 / (3.0 * floored)
    )
    return jnp.where(scaled_gap <= 1.0, near_part, jnp.where(scaled_gap < 2.0, far_part, 0.0))


def obs_statistics(current, values, variances, members):
    banded = current.reshape(current.shape[0], BANDS, members)
    whole_obs = jnp.sum(banded, axis=1)
    centre = jnp.mean(whole_obs, axis=1, keepdims=True)
    spread = jnp.sum((whole_obs - centre) ** 2, axis=1) / (members - 1) + 1e-06
    post_var = 1.0 / (1.0 / spread + 1.0 / variances)
    post_mean = post_var * (centre[:, 0] / spread + values / variances)
    increments = (post_mean - centre[:, 0])[:, None] + (jnp.sqrt(post_var / spread) - 1.0)[
        :, None
    ] * (whole_obs - centre)
    deviations = banded - jnp.mean(banded, axis=2, keepdims=True)
    return (deviations, spread, increments)


def update_pool(pool, pool_homes, deviations, spread, increments, obs_homes, nblocks, decays):
    members = deviations.shape[2]
    banded = pool.reshape(pool.shape[0], BANDS, members)
    new_bands = []
    for band_no in range(BANDS):
        pool_band = banded[:, band_no, :]
        pool_dev = pool_band - jnp.mean(pool_band, axis=1, keepdims=True)
        weights = (
            gc_weight(pool_homes[:, None], obs_homes[None, :], nblocks, decays[band_no])
            / ((members - 1) * spread)[None, :]
        )
        crossed = jnp.einsum("pm,km->pk", pool_dev, deviations[:, band_no, :], precision=HIGHEST)
        change = jnp.einsum("pk,km->pm", crossed * weights, increments, precision=HIGHEST)
        new_bands.append(pool_band + change)
    return jnp.stack(new_bands, axis=1).reshape(pool.shape)


def update_state(ensemble, my_cols, deviations, spread, increments, obs_homes, valid, nblocks, decays):
    members = ensemble.shape[2]
    new_bands = []
    for band_no in range(BANDS):
        band_layer = ensemble[band_no]
        layer_dev = band_layer - jnp.mean(band_layer, axis=1, keepdims=True)
        obs_dev = deviations[:, band_no, :]
        weights = (
            gc_weight((my_cols // BLK)[:, None], obs_homes[None, :], nblocks, decays[band_no])
            / ((members - 1) * spread)[None, :]
        )
        weights = jnp.where(valid[None, :], weights, 0.0)
        crossed = jnp.einsum("lmc,km->lck", layer_dev, obs_dev, precision=HIGHEST)
        change = jnp.einsum("lck,km->lmc", crossed * weights[None], increments, precision=HIGHEST)
        new_bands.append(band_layer + change)
    return jnp.stack(new_bands, axis=0)


def slot_table(owners, slot_rank, slab_number, capacity):
    obs_count = owners.shape[1]
    matches = (owners == slab_number)[:, None, :] & (
        slot_rank[:, None, :] == jnp.arange(capacity, dtype=jnp.int32)[None, :, None]
    )
    slot_obs = jnp.sum(
        jnp.where(matches, jnp.arange(obs_count, dtype=jnp.int32)[None, None, :], 0), axis=2
    )
    slot_valid = jnp.any(matches, axis=2)
    return (slot_obs, slot_valid)


def per_device(ensemble, obs_value, obs_var, obs_owner, obs_column, home_block, batch_order):
    members = ensemble.shape[2]
    levels_count = ensemble.shape[1]
    cols_dev = ensemble.shape[3]
    slab_count = lax.axis_size("slab")
    sub_count = lax.axis_size("sub")
    slab_index = lax.axis_index("slab")
    sub_index = lax.axis_index("sub")
    capacity = CAP
    cols_slab = cols_dev * sub_count
    nblocks = cols_slab * slab_count // BLK
    span_broad = cols_slab // (4 * BLK)
    span_narrow = max(span_broad // 4, 1)
    decays = (float(span_broad), float(span_narrow))
    assert 2 * span_broad + 1 <= cols_slab // BLK and slab_count >= 3
    owners = obs_owner[:, :, 0]
    obs_home = jnp.mod((owners * cols_slab + obs_column) // BLK + home_block, nblocks)
    onehot = (owners[:, :, None] == jnp.arange(slab_count, dtype=jnp.int32)[None, None, :]).astype(
        jnp.int32
    )
    running = jnp.cumsum(onehot, axis=1) - 1
    slot_rank = jnp.sum(onehot * running, axis=2)
    slot_global = owners * capacity + slot_rank
    slot_obs, slot_valid = slot_table(owners, slot_rank, slab_index, capacity)
    slot_column = jnp.take_along_axis(obs_column, slot_obs, axis=1)
    slot_level = slot_obs % levels_count
    holder = slot_column // cols_dev
    local_col = slot_column % cols_dev
    picked = ensemble[:, slot_level, :, local_col]
    retain = slot_valid & (holder == sub_index)
    picked = jnp.where(retain[:, :, None, None], picked, 0.0).reshape(
        BATCHES, capacity, BANDS * members
    )
    slab_slots = jnp.sum(lax.all_gather(picked, "sub", axis=0), axis=0)
    gathered = lax.all_gather(slab_slots, "slab", axis=1, tiled=True)
    priors = jnp.take_along_axis(gathered, slot_global[:, :, None], axis=1)

    first, second = batch_order[0], batch_order[1]
    y0 = priors[first]
    stats0 = obs_statistics(y0, obs_value[first], obs_var[first], members)
    y1 = update_pool(priors[second], obs_home[second], *stats0, obs_home[first], nblocks, decays)
    stats1 = obs_statistics(y1, obs_value[second], obs_var[second], members)
    recorded = jnp.zeros_like(priors).at[first].set(y0).at[second].set(y1)

    my_cols = (slab_index * sub_count + sub_index) * cols_dev + jnp.arange(
        cols_dev, dtype=jnp.int32
    )
    near = [jnp.mod(slab_index + d, slab_count) for d in (-1, 0, 1)]
    for batch_id, stats in ((first, stats0), (second, stats1)):
        deviations, spread, increments = stats
        b_owners = lax.dynamic_index_in_dim(owners, batch_id, keepdims=True)
        b_rank = lax.dynamic_index_in_dim(slot_rank, batch_id, keepdims=True)
        tables = [slot_table(b_owners, b_rank, n, capacity) for n in near]
        idx = jnp.concatenate([t[0][0] for t in tables])
        valid = jnp.concatenate([t[1][0] for t in tables])
        ensemble = update_state(
            ensemble,
            my_cols,
            deviations[idx],
            spread[idx],
            increments[idx],
            obs_home[batch_id][idx],
            valid,
            nblocks,
            decays,
        )
    return (ensemble, recorded)


def solution(mesh):
    placed = (P(None, None, None, ("slab", "sub")), P(), P(), P(), P(), P(), P())
    return jax.shard_map(
        per_device,
        mesh=mesh,
        in_specs=placed,
        out_specs=(P(None, None, None, ("slab", "sub")), P()),
        check_vma=False,
    )
```

```python
import functools

import jax
import jax.numpy as jnp
from jax import lax
from jax.experimental import pallas as pl
from jax.experimental.pallas import tpu as pltpu
from jax.sharding import PartitionSpec as P

MESH = pl.DeviceIdType.MESH

BANDS = 2
BLK = 16
BATCHES = 2
CAP = 8


HIGHEST = lax.Precision.HIGHEST


def gc_weight(first, second, nblocks, length):
    block_gap = jnp.abs(first - second)
    block_gap = jnp.minimum(block_gap, nblocks - block_gap)
    scaled_gap = block_gap.astype(jnp.float32) / length
    near_part = (
        ((-0.25 * scaled_gap + 0.5) * scaled_gap + 0.625) * scaled_gap**3
        - 5.0 / 3.0 * scaled_gap**2
        + 1.0
    )
    floored = jnp.maximum(scaled_gap, 1.0)
    far_part = (
        (
            (((scaled_gap / 12.0 - 0.5) * scaled_gap + 0.625) * scaled_gap + 5.0 / 3.0) * scaled_gap
            - 5.0
        )
        * scaled_gap
        + 4.0
        - 2.0 / (3.0 * floored)
    )
    return jnp.where(scaled_gap <= 1.0, near_part, jnp.where(scaled_gap < 2.0, far_part, 0.0))


def obs_statistics(current, values, variances, members):
    banded = current.reshape(current.shape[0], BANDS, members)
    whole_obs = jnp.sum(banded, axis=1)
    centre = jnp.mean(whole_obs, axis=1, keepdims=True)
    spread = jnp.sum((whole_obs - centre) ** 2, axis=1) / (members - 1) + 1e-06
    post_var = 1.0 / (1.0 / spread + 1.0 / variances)
    post_mean = post_var * (centre[:, 0] / spread + values / variances)
    increments = (post_mean - centre[:, 0])[:, None] + (jnp.sqrt(post_var / spread) - 1.0)[
        :, None
    ] * (whole_obs - centre)
    deviations = banded - jnp.mean(banded, axis=2, keepdims=True)
    return (deviations, spread, increments)


def update_pool(pool, pool_homes, deviations, spread, increments, obs_homes, nblocks, decays):
    members = deviations.shape[2]
    banded = pool.reshape(pool.shape[0], BANDS, members)
    new_bands = []
    for band_no in range(BANDS):
        pool_band = banded[:, band_no, :]
        pool_dev = pool_band - jnp.mean(pool_band, axis=1, keepdims=True)
        weights = (
            gc_weight(pool_homes[:, None], obs_homes[None, :], nblocks, decays[band_no])
            / ((members - 1) * spread)[None, :]
        )
        crossed = jnp.einsum("pm,km->pk", pool_dev, deviations[:, band_no, :], precision=HIGHEST)
        change = jnp.einsum("pk,km->pm", crossed * weights, increments, precision=HIGHEST)
        new_bands.append(pool_band + change)
    return jnp.stack(new_bands, axis=1).reshape(pool.shape)


def update_state(ensemble, my_cols, deviations, spread, increments, obs_homes, valid, nblocks, decays):
    members = ensemble.shape[2]
    new_bands = []
    for band_no in range(BANDS):
        band_layer = ensemble[band_no]
        layer_dev = band_layer - jnp.mean(band_layer, axis=1, keepdims=True)
        obs_dev = deviations[:, band_no, :]
        weights = (
            gc_weight((my_cols // BLK)[:, None], obs_homes[None, :], nblocks, decays[band_no])
            / ((members - 1) * spread)[None, :]
        )
        weights = jnp.where(valid[None, :], weights, 0.0)
        crossed = jnp.einsum("lmc,km->lck", layer_dev, obs_dev, precision=HIGHEST)
        change = jnp.einsum("lck,km->lmc", crossed * weights[None], increments, precision=HIGHEST)
        new_bands.append(band_layer + change)
    return jnp.stack(new_bands, axis=0)


def slot_table(owners, slot_rank, slab_number, capacity):
    obs_count = owners.shape[1]
    matches = (owners == slab_number)[:, None, :] & (
        slot_rank[:, None, :] == jnp.arange(capacity, dtype=jnp.int32)[None, :, None]
    )
    slot_obs = jnp.sum(
        jnp.where(matches, jnp.arange(obs_count, dtype=jnp.int32)[None, None, :], 0), axis=2
    )
    slot_valid = jnp.any(matches, axis=2)
    return (slot_obs, slot_valid)


def gather_kernel(n_row, picked_ref, out_ref, part_ref, sem0, send0, sem_a, send_a, sem_b, send_b, sem_c, send_c):
    n_slab = lax.axis_size("slab")
    n_sub = lax.axis_size("sub")
    s = lax.axis_index("slab")
    u = lax.axis_index("sub")
    n_rows = n_slab // n_row
    row, loc = s // n_row, s % n_row
    q_rows = out_ref.shape[2]

    def copy(src, dst, send, recv, dev):
        return pltpu.make_async_remote_copy(
            src_ref=src, dst_ref=dst, send_sem=send, recv_sem=recv, device_id=dev, device_id_type=MESH
        )

    def to_sub(d):
        q = (u + d) % n_sub
        return copy(
            picked_ref.at[q], part_ref.at[u], send0.at[q], sem0.at[u], (s, q)
        )

    def from_sub(d):
        q = (u + d) % n_sub
        return copy(
            picked_ref.at[q], part_ref.at[q], send0.at[q], sem0.at[q], (s, q)
        )

    for d in range(1, n_sub):
        to_sub(d).start()
    total = picked_ref[u]
    for d in range(1, n_sub):
        from_sub(d).wait_recv()
        total = total + part_ref[(u + d) % n_sub]
    out_ref[u, s] = total

    def to_a(d):
        j = (loc + d) % n_row
        return copy(out_ref.at[u, s], out_ref.at[u, s], send_a.at[j], sem_a.at[loc], (row * n_row + j, u))

    def from_a(d):
        j = (loc + d) % n_row
        src = row * n_row + j
        return copy(out_ref.at[u, src], out_ref.at[u, src], send_a.at[j], sem_a.at[j], (src, u))

    def start_a(d, c):
        to_a(d).start()
        return c

    def wait_a(d, c):
        from_a(d).wait_recv()
        return c

    lax.fori_loop(1, n_row, start_a, 0)
    lax.fori_loop(1, n_row, wait_a, 0)

    def block(r):
        return out_ref.at[u, pl.ds(r * n_row, n_row)]

    def to_b(d):
        r = (row + d) % n_rows
        return copy(block(row), block(row), send_b.at[r], sem_b.at[row], (r * n_row + loc, u))

    def from_b(d):
        r = (row + d) % n_rows
        return copy(block(r), block(r), send_b.at[r], sem_b.at[r], (r * n_row + loc, u))

    for d in range(1, n_rows):
        to_b(d).start()
    for d in range(1, n_rows):
        from_b(d).wait_recv()

    def to_c(d):
        q = (u + d) % n_sub
        return copy(out_ref.at[u], out_ref.at[u], send_c.at[q], sem_c.at[u], (s, q))

    def from_c(d):
        q = (u + d) % n_sub
        return copy(out_ref.at[q], out_ref.at[q], send_c.at[q], sem_c.at[q], (s, q))

    for d in range(1, n_sub):
        to_c(d).start()
    for d in range(1, n_sub):
        from_c(d).wait_recv()

    for d in range(1, n_sub):
        to_sub(d).wait_send()
    lax.fori_loop(1, n_row, lambda d, c: (to_a(d).wait_send(), c)[1], 0)
    for d in range(1, n_rows):
        to_b(d).wait_send()
    for d in range(1, n_sub):
        to_c(d).wait_send()


def gather_slots(picked, n_slab, n_sub, n_row):
    rows, width = picked.shape
    q_rows = rows // n_sub
    n_rows = n_slab // n_row
    return pl.pallas_call(
        functools.partial(gather_kernel, n_row),
        out_shape=jax.ShapeDtypeStruct((n_sub, n_slab, q_rows, width), jnp.float32),
        in_specs=[pl.BlockSpec(memory_space=pltpu.VMEM)],
        out_specs=pl.BlockSpec(memory_space=pltpu.VMEM),
        scratch_shapes=[
            pltpu.VMEM((n_sub, q_rows, width), jnp.float32),
            pltpu.SemaphoreType.DMA((n_sub,)),
            pltpu.SemaphoreType.DMA((n_sub,)),
            pltpu.SemaphoreType.DMA((n_row,)),
            pltpu.SemaphoreType.DMA((n_row,)),
            pltpu.SemaphoreType.DMA((n_rows,)),
            pltpu.SemaphoreType.DMA((n_rows,)),
            pltpu.SemaphoreType.DMA((n_sub,)),
            pltpu.SemaphoreType.DMA((n_sub,)),
        ],
        compiler_params=pltpu.CompilerParams(has_side_effects=True),
    )(picked.reshape(n_sub, q_rows, width))


def per_device(ensemble, obs_value, obs_var, obs_owner, obs_column, home_block, batch_order):
    members = ensemble.shape[2]
    levels_count = ensemble.shape[1]
    cols_dev = ensemble.shape[3]
    slab_count = lax.axis_size("slab")
    sub_count = lax.axis_size("sub")
    slab_index = lax.axis_index("slab")
    sub_index = lax.axis_index("sub")
    capacity = CAP
    cols_slab = cols_dev * sub_count
    nblocks = cols_slab * slab_count // BLK
    span_broad = cols_slab // (4 * BLK)
    span_narrow = max(span_broad // 4, 1)
    decays = (float(span_broad), float(span_narrow))
    assert 2 * span_broad + 1 <= cols_slab // BLK and slab_count >= 3
    owners = obs_owner[:, :, 0]
    obs_home = jnp.mod((owners * cols_slab + obs_column) // BLK + home_block, nblocks)
    onehot = (owners[:, :, None] == jnp.arange(slab_count, dtype=jnp.int32)[None, None, :]).astype(
        jnp.int32
    )
    running = jnp.cumsum(onehot, axis=1) - 1
    slot_rank = jnp.sum(onehot * running, axis=2)
    slot_global = owners * capacity + slot_rank
    slot_obs, slot_valid = slot_table(owners, slot_rank, slab_index, capacity)
    slot_column = jnp.take_along_axis(obs_column, slot_obs, axis=1)
    slot_level = slot_obs % levels_count
    holder = slot_column // cols_dev
    local_col = slot_column % cols_dev
    picked = ensemble[:, slot_level, :, local_col]
    retain = slot_valid & (holder == sub_index)
    picked = jnp.where(retain[:, :, None, None], picked, 0.0).reshape(
        BATCHES * capacity, BANDS * members
    )
    n_row = 32 if slab_count % 32 == 0 else slab_count
    gathered = gather_slots(picked, slab_count, sub_count, n_row)
    q_rows = gathered.shape[2]
    row_of = jnp.arange(BATCHES, dtype=jnp.int32)[:, None] * capacity + slot_rank
    flat = (row_of // q_rows) * (slab_count * q_rows) + owners * q_rows + row_of % q_rows
    priors = jnp.take(gathered.reshape(-1, BANDS * members), flat, axis=0)

    first, second = batch_order[0], batch_order[1]
    y0 = priors[first]
    stats0 = obs_statistics(y0, obs_value[first], obs_var[first], members)
    y1 = update_pool(priors[second], obs_home[second], *stats0, obs_home[first], nblocks, decays)
    stats1 = obs_statistics(y1, obs_value[second], obs_var[second], members)
    recorded = jnp.zeros_like(priors).at[first].set(y0).at[second].set(y1)

    my_cols = (slab_index * sub_count + sub_index) * cols_dev + jnp.arange(
        cols_dev, dtype=jnp.int32
    )
    near = [jnp.mod(slab_index + d, slab_count) for d in (-1, 0, 1)]
    for batch_id, stats in ((first, stats0), (second, stats1)):
        deviations, spread, increments = stats
        b_owners = lax.dynamic_index_in_dim(owners, batch_id, keepdims=True)
        b_rank = lax.dynamic_index_in_dim(slot_rank, batch_id, keepdims=True)
        tables = [slot_table(b_owners, b_rank, n, capacity) for n in near]
        idx = jnp.concatenate([t[0][0] for t in tables])
        valid = jnp.concatenate([t[1][0] for t in tables])
        ensemble = update_state(
            ensemble,
            my_cols,
            deviations[idx],
            spread[idx],
            increments[idx],
            obs_home[batch_id][idx],
            valid,
            nblocks,
            decays,
        )
    return (ensemble, recorded)


def solution(mesh):
    placed = (P(None, None, None, ("slab", "sub")), P(), P(), P(), P(), P(), P())
    return jax.shard_map(
        per_device,
        mesh=mesh,
        in_specs=placed,
        out_specs=(P(None, None, None, ("slab", "sub")), P()),
        check_vma=False,
    )
```

```python
import functools

import jax
import jax.numpy as jnp
from jax import lax
from jax.experimental import pallas as pl
from jax.experimental.pallas import tpu as pltpu
from jax.sharding import PartitionSpec as P

MESH = pl.DeviceIdType.MESH

BANDS = 2
BLK = 16
BATCHES = 2
CAP = 8


HIGHEST = lax.Precision.HIGHEST


def gc_weight(first, second, nblocks, length):
    block_gap = jnp.abs(first - second)
    block_gap = jnp.minimum(block_gap, nblocks - block_gap)
    scaled_gap = block_gap.astype(jnp.float32) / length
    near_part = (
        ((-0.25 * scaled_gap + 0.5) * scaled_gap + 0.625) * scaled_gap**3
        - 5.0 / 3.0 * scaled_gap**2
        + 1.0
    )
    floored = jnp.maximum(scaled_gap, 1.0)
    far_part = (
        (
            (((scaled_gap / 12.0 - 0.5) * scaled_gap + 0.625) * scaled_gap + 5.0 / 3.0) * scaled_gap
            - 5.0
        )
        * scaled_gap
        + 4.0
        - 2.0 / (3.0 * floored)
    )
    return jnp.where(scaled_gap <= 1.0, near_part, jnp.where(scaled_gap < 2.0, far_part, 0.0))


def obs_statistics(current, values, variances, members):
    banded = current.reshape(current.shape[0], BANDS, members)
    whole_obs = jnp.sum(banded, axis=1)
    centre = jnp.mean(whole_obs, axis=1, keepdims=True)
    spread = jnp.sum((whole_obs - centre) ** 2, axis=1) / (members - 1) + 1e-06
    post_var = 1.0 / (1.0 / spread + 1.0 / variances)
    post_mean = post_var * (centre[:, 0] / spread + values / variances)
    increments = (post_mean - centre[:, 0])[:, None] + (jnp.sqrt(post_var / spread) - 1.0)[
        :, None
    ] * (whole_obs - centre)
    deviations = banded - jnp.mean(banded, axis=2, keepdims=True)
    return (deviations, spread, increments)


def update_pool(pool, pool_homes, deviations, spread, increments, obs_homes, nblocks, decays):
    members = deviations.shape[2]
    banded = pool.reshape(pool.shape[0], BANDS, members)
    new_bands = []
    for band_no in range(BANDS):
        pool_band = banded[:, band_no, :]
        pool_dev = pool_band - jnp.mean(pool_band, axis=1, keepdims=True)
        weights = (
            gc_weight(pool_homes[:, None], obs_homes[None, :], nblocks, decays[band_no])
            / ((members - 1) * spread)[None, :]
        )
        crossed = jnp.einsum("pm,km->pk", pool_dev, deviations[:, band_no, :], precision=HIGHEST)
        change = jnp.einsum("pk,km->pm", crossed * weights, increments, precision=HIGHEST)
        new_bands.append(pool_band + change)
    return jnp.stack(new_bands, axis=1).reshape(pool.shape)


def update_state(ensemble, my_cols, deviations, spread, increments, obs_homes, valid, nblocks, decays):
    members = ensemble.shape[2]
    new_bands = []
    for band_no in range(BANDS):
        band_layer = ensemble[band_no]
        layer_dev = band_layer - jnp.mean(band_layer, axis=1, keepdims=True)
        obs_dev = deviations[:, band_no, :]
        weights = (
            gc_weight((my_cols // BLK)[:, None], obs_homes[None, :], nblocks, decays[band_no])
            / ((members - 1) * spread)[None, :]
        )
        weights = jnp.where(valid[None, :], weights, 0.0)
        crossed = jnp.einsum("lmc,km->lck", layer_dev, obs_dev, precision=HIGHEST)
        change = jnp.einsum("lck,km->lmc", crossed * weights[None], increments, precision=HIGHEST)
        new_bands.append(band_layer + change)
    return jnp.stack(new_bands, axis=0)


def slot_table(owners, slot_rank, slab_number, capacity):
    obs_count = owners.shape[1]
    matches = (owners == slab_number)[:, None, :] & (
        slot_rank[:, None, :] == jnp.arange(capacity, dtype=jnp.int32)[None, :, None]
    )
    slot_obs = jnp.sum(
        jnp.where(matches, jnp.arange(obs_count, dtype=jnp.int32)[None, None, :], 0), axis=2
    )
    slot_valid = jnp.any(matches, axis=2)
    return (slot_obs, slot_valid)


def gather_kernel(n_row, picked_ref, out_ref, part_ref, sem0, send0, sem_a, send_a, sem_b, send_b, sem_c, send_c):
    n_slab = lax.axis_size("slab")
    n_sub = lax.axis_size("sub")
    s = lax.axis_index("slab")
    u = lax.axis_index("sub")
    n_rows = n_slab // n_row
    row, loc = s // n_row, s % n_row

    def copy(src, dst, send, recv, dev):
        return pltpu.make_async_remote_copy(
            src_ref=src, dst_ref=dst, send_sem=send, recv_sem=recv, device_id=dev, device_id_type=MESH
        )

    def to_sub(d):
        q = (u + d) % n_sub
        return copy(picked_ref.at[q], part_ref.at[u], send0.at[q], sem0.at[u], (s, q))

    def from_sub(d):
        q = (u + d) % n_sub
        return copy(picked_ref.at[q], part_ref.at[q], send0.at[q], sem0.at[q], (s, q))

    for d in range(1, n_sub):
        to_sub(d).start()
    total = picked_ref[pl.ds(u, 1), :]
    for d in range(1, n_sub):
        from_sub(d).wait_recv()
        total = total + part_ref[pl.ds((u + d) % n_sub, 1), :]
    out_ref[u, pl.ds(s, 1), :] = total

    def own(r):
        return out_ref.at[u, pl.ds(r, 1)]

    def to_a(d):
        j = (loc + d) % n_row
        return copy(own(s), own(s), send_a.at[j], sem_a.at[loc], (row * n_row + j, u))

    def from_a(d):
        j = (loc + d) % n_row
        src = row * n_row + j
        return copy(own(src), own(src), send_a.at[j], sem_a.at[j], (src, u))

    def start_a(d, c):
        to_a(d).start()
        return c

    def wait_a(d, c):
        from_a(d).wait_recv()
        return c

    lax.fori_loop(1, n_row, start_a, 0)
    lax.fori_loop(1, n_row, wait_a, 0)

    def block(r):
        return out_ref.at[u, pl.ds(r * n_row, n_row)]

    def to_b(d):
        r = (row + d) % n_rows
        return copy(block(row), block(row), send_b.at[r], sem_b.at[row], (r * n_row + loc, u))

    def from_b(d):
        r = (row + d) % n_rows
        return copy(block(r), block(r), send_b.at[r], sem_b.at[r], (r * n_row + loc, u))

    for d in range(1, n_rows):
        to_b(d).start()
    for d in range(1, n_rows):
        from_b(d).wait_recv()

    def to_c(d):
        q = (u + d) % n_sub
        return copy(out_ref.at[u], out_ref.at[u], send_c.at[q], sem_c.at[u], (s, q))

    def from_c(d):
        q = (u + d) % n_sub
        return copy(out_ref.at[q], out_ref.at[q], send_c.at[q], sem_c.at[q], (s, q))

    for d in range(1, n_sub):
        to_c(d).start()
    for d in range(1, n_sub):
        from_c(d).wait_recv()

    for d in range(1, n_sub):
        to_sub(d).wait_send()
    lax.fori_loop(1, n_row, lambda d, c: (to_a(d).wait_send(), c)[1], 0)
    for d in range(1, n_rows):
        to_b(d).wait_send()
    for d in range(1, n_sub):
        to_c(d).wait_send()


def gather_slots(picked, n_slab, n_sub, n_row):
    rows, width = picked.shape
    lanes = rows // n_sub * width
    n_rows = n_slab // n_row
    return pl.pallas_call(
        functools.partial(gather_kernel, n_row),
        out_shape=jax.ShapeDtypeStruct((n_sub, n_slab, lanes), jnp.float32),
        in_specs=[pl.BlockSpec(memory_space=pltpu.VMEM)],
        out_specs=pl.BlockSpec(memory_space=pltpu.VMEM),
        scratch_shapes=[
            pltpu.VMEM((n_sub, lanes), jnp.float32),
            pltpu.SemaphoreType.DMA((n_sub,)),
            pltpu.SemaphoreType.DMA((n_sub,)),
            pltpu.SemaphoreType.DMA((n_row,)),
            pltpu.SemaphoreType.DMA((n_row,)),
            pltpu.SemaphoreType.DMA((n_rows,)),
            pltpu.SemaphoreType.DMA((n_rows,)),
            pltpu.SemaphoreType.DMA((n_sub,)),
            pltpu.SemaphoreType.DMA((n_sub,)),
        ],
        compiler_params=pltpu.CompilerParams(has_side_effects=True),
    )(picked.reshape(n_sub, lanes))


def per_device(ensemble, obs_value, obs_var, obs_owner, obs_column, home_block, batch_order):
    members = ensemble.shape[2]
    levels_count = ensemble.shape[1]
    cols_dev = ensemble.shape[3]
    slab_count = lax.axis_size("slab")
    sub_count = lax.axis_size("sub")
    slab_index = lax.axis_index("slab")
    sub_index = lax.axis_index("sub")
    capacity = CAP
    cols_slab = cols_dev * sub_count
    nblocks = cols_slab * slab_count // BLK
    span_broad = cols_slab // (4 * BLK)
    span_narrow = max(span_broad // 4, 1)
    decays = (float(span_broad), float(span_narrow))
    assert 2 * span_broad + 1 <= cols_slab // BLK and slab_count >= 3
    owners = obs_owner[:, :, 0]
    obs_home = jnp.mod((owners * cols_slab + obs_column) // BLK + home_block, nblocks)
    onehot = (owners[:, :, None] == jnp.arange(slab_count, dtype=jnp.int32)[None, None, :]).astype(
        jnp.int32
    )
    running = jnp.cumsum(onehot, axis=1) - 1
    slot_rank = jnp.sum(onehot * running, axis=2)
    slot_global = owners * capacity + slot_rank
    slot_obs, slot_valid = slot_table(owners, slot_rank, slab_index, capacity)
    slot_column = jnp.take_along_axis(obs_column, slot_obs, axis=1)
    slot_level = slot_obs % levels_count
    holder = slot_column // cols_dev
    local_col = slot_column % cols_dev
    picked = ensemble[:, slot_level, :, local_col]
    retain = slot_valid & (holder == sub_index)
    picked = jnp.where(retain[:, :, None, None], picked, 0.0).reshape(
        BATCHES * capacity, BANDS * members
    )
    n_row = 32 if slab_count % 32 == 0 else slab_count
    gathered = gather_slots(picked, slab_count, sub_count, n_row)
    q_rows = BATCHES * capacity // sub_count
    row_of = jnp.arange(BATCHES, dtype=jnp.int32)[:, None] * capacity + slot_rank
    flat = (row_of // q_rows) * (slab_count * q_rows) + owners * q_rows + row_of % q_rows
    priors = jnp.take(gathered.reshape(-1, BANDS * members), flat, axis=0)

    first, second = batch_order[0], batch_order[1]
    y0 = priors[first]
    stats0 = obs_statistics(y0, obs_value[first], obs_var[first], members)
    y1 = update_pool(priors[second], obs_home[second], *stats0, obs_home[first], nblocks, decays)
    stats1 = obs_statistics(y1, obs_value[second], obs_var[second], members)
    recorded = jnp.zeros_like(priors).at[first].set(y0).at[second].set(y1)

    my_cols = (slab_index * sub_count + sub_index) * cols_dev + jnp.arange(
        cols_dev, dtype=jnp.int32
    )
    near = [jnp.mod(slab_index + d, slab_count) for d in (-1, 0, 1)]
    for batch_id, stats in ((first, stats0), (second, stats1)):
        deviations, spread, increments = stats
        b_owners = lax.dynamic_index_in_dim(owners, batch_id, keepdims=True)
        b_rank = lax.dynamic_index_in_dim(slot_rank, batch_id, keepdims=True)
        tables = [slot_table(b_owners, b_rank, n, capacity) for n in near]
        idx = jnp.concatenate([t[0][0] for t in tables])
        valid = jnp.concatenate([t[1][0] for t in tables])
        ensemble = update_state(
            ensemble,
            my_cols,
            deviations[idx],
            spread[idx],
            increments[idx],
            obs_home[batch_id][idx],
            valid,
            nblocks,
            decays,
        )
    return (ensemble, recorded)


def solution(mesh):
    placed = (P(None, None, None, ("slab", "sub")), P(), P(), P(), P(), P(), P())
    return jax.shard_map(
        per_device,
        mesh=mesh,
        in_specs=placed,
        out_specs=(P(None, None, None, ("slab", "sub")), P()),
        check_vma=False,
    )
```

```python
import functools

import jax
import jax.numpy as jnp
from jax import lax
from jax.experimental import pallas as pl
from jax.experimental.pallas import tpu as pltpu
from jax.sharding import PartitionSpec as P

MESH = pl.DeviceIdType.MESH

BANDS = 2
BLK = 16
BATCHES = 2
CAP = 8


HIGHEST = lax.Precision.HIGHEST


def gc_weight(first, second, nblocks, length):
    block_gap = jnp.abs(first - second)
    block_gap = jnp.minimum(block_gap, nblocks - block_gap)
    scaled_gap = block_gap.astype(jnp.float32) / length
    near_part = (
        ((-0.25 * scaled_gap + 0.5) * scaled_gap + 0.625) * scaled_gap**3
        - 5.0 / 3.0 * scaled_gap**2
        + 1.0
    )
    floored = jnp.maximum(scaled_gap, 1.0)
    far_part = (
        (
            (((scaled_gap / 12.0 - 0.5) * scaled_gap + 0.625) * scaled_gap + 5.0 / 3.0) * scaled_gap
            - 5.0
        )
        * scaled_gap
        + 4.0
        - 2.0 / (3.0 * floored)
    )
    return jnp.where(scaled_gap <= 1.0, near_part, jnp.where(scaled_gap < 2.0, far_part, 0.0))


def obs_statistics(current, values, variances, members):
    banded = current.reshape(current.shape[0], BANDS, members)
    whole_obs = jnp.sum(banded, axis=1)
    centre = jnp.mean(whole_obs, axis=1, keepdims=True)
    spread = jnp.sum((whole_obs - centre) ** 2, axis=1) / (members - 1) + 1e-06
    post_var = 1.0 / (1.0 / spread + 1.0 / variances)
    post_mean = post_var * (centre[:, 0] / spread + values / variances)
    increments = (post_mean - centre[:, 0])[:, None] + (jnp.sqrt(post_var / spread) - 1.0)[
        :, None
    ] * (whole_obs - centre)
    deviations = banded - jnp.mean(banded, axis=2, keepdims=True)
    return (deviations, spread, increments)


def update_pool(pool, pool_homes, deviations, spread, increments, obs_homes, nblocks, decays):
    members = deviations.shape[2]
    banded = pool.reshape(pool.shape[0], BANDS, members)
    new_bands = []
    for band_no in range(BANDS):
        pool_band = banded[:, band_no, :]
        pool_dev = pool_band - jnp.mean(pool_band, axis=1, keepdims=True)
        weights = (
            gc_weight(pool_homes[:, None], obs_homes[None, :], nblocks, decays[band_no])
            / ((members - 1) * spread)[None, :]
        )
        crossed = jnp.einsum("pm,km->pk", pool_dev, deviations[:, band_no, :], precision=HIGHEST)
        change = jnp.einsum("pk,km->pm", crossed * weights, increments, precision=HIGHEST)
        new_bands.append(pool_band + change)
    return jnp.stack(new_bands, axis=1).reshape(pool.shape)


def update_state(ensemble, my_cols, deviations, spread, increments, obs_homes, valid, nblocks, decays):
    members = ensemble.shape[2]
    new_bands = []
    for band_no in range(BANDS):
        band_layer = ensemble[band_no]
        layer_dev = band_layer - jnp.mean(band_layer, axis=1, keepdims=True)
        obs_dev = deviations[:, band_no, :]
        weights = (
            gc_weight((my_cols // BLK)[:, None], obs_homes[None, :], nblocks, decays[band_no])
            / ((members - 1) * spread)[None, :]
        )
        weights = jnp.where(valid[None, :], weights, 0.0)
        crossed = jnp.einsum("lmc,km->lck", layer_dev, obs_dev, precision=HIGHEST)
        change = jnp.einsum("lck,km->lmc", crossed * weights[None], increments, precision=HIGHEST)
        new_bands.append(band_layer + change)
    return jnp.stack(new_bands, axis=0)


def slot_table(owners, slot_rank, slab_number, capacity):
    obs_count = owners.shape[1]
    matches = (owners == slab_number)[:, None, :] & (
        slot_rank[:, None, :] == jnp.arange(capacity, dtype=jnp.int32)[None, :, None]
    )
    slot_obs = jnp.sum(
        jnp.where(matches, jnp.arange(obs_count, dtype=jnp.int32)[None, None, :], 0), axis=2
    )
    slot_valid = jnp.any(matches, axis=2)
    return (slot_obs, slot_valid)


def gather_kernel(n_row, picked_ref, out_ref, part_ref, sem0, send0, sem_a, send_a, sem_b, send_b):
    n_slab = lax.axis_size("slab")
    n_sub = lax.axis_size("sub")
    s = lax.axis_index("slab")
    u = lax.axis_index("sub")
    n_rows = n_slab // n_row
    row, loc = s // n_row, s % n_row

    def copy(src, dst, send, recv, dev):
        return pltpu.make_async_remote_copy(
            src_ref=src, dst_ref=dst, send_sem=send, recv_sem=recv, device_id=dev, device_id_type=MESH
        )

    def part(q):
        return part_ref.at[pl.ds(q, 1)]

    def to_sub(d):
        q = (u + d) % n_sub
        return copy(picked_ref, part(u), send0.at[q], sem0.at[u], (s, q))

    def from_sub(d):
        q = (u + d) % n_sub
        return copy(picked_ref, part(q), send0.at[q], sem0.at[q], (s, q))

    for d in range(1, n_sub):
        to_sub(d).start()
    total = picked_ref[...]
    for d in range(1, n_sub):
        from_sub(d).wait_recv()
        total = total + part_ref[pl.ds((u + d) % n_sub, 1), :]
    out_ref[pl.ds(s, 1), :] = total

    def own(r):
        return out_ref.at[pl.ds(r, 1)]

    def to_a(d):
        j = (loc + d) % n_row
        return copy(own(s), own(s), send_a.at[j], sem_a.at[loc], (row * n_row + j, u))

    def from_a(d):
        j = (loc + d) % n_row
        src = row * n_row + j
        return copy(own(src), own(src), send_a.at[j], sem_a.at[j], (src, u))

    def start_a(d, c):
        to_a(d).start()
        return c

    def wait_a(d, c):
        from_a(d).wait_recv()
        return c

    lax.fori_loop(1, n_row, start_a, 0)
    lax.fori_loop(1, n_row, wait_a, 0)

    def block(r):
        return out_ref.at[pl.ds(r * n_row, n_row)]

    def to_b(d):
        r = (row + d) % n_rows
        return copy(block(row), block(row), send_b.at[r], sem_b.at[row], (r * n_row + loc, u))

    def from_b(d):
        r = (row + d) % n_rows
        return copy(block(r), block(r), send_b.at[r], sem_b.at[r], (r * n_row + loc, u))

    for d in range(1, n_rows):
        to_b(d).start()
    for d in range(1, n_rows):
        from_b(d).wait_recv()

    for d in range(1, n_sub):
        to_sub(d).wait_send()
    lax.fori_loop(1, n_row, lambda d, c: (to_a(d).wait_send(), c)[1], 0)
    for d in range(1, n_rows):
        to_b(d).wait_send()


def gather_slots(picked, n_slab, n_sub, n_row):
    rows, width = picked.shape
    lanes = rows * width
    n_rows = n_slab // n_row
    return pl.pallas_call(
        functools.partial(gather_kernel, n_row),
        out_shape=jax.ShapeDtypeStruct((n_slab, lanes), jnp.float32),
        in_specs=[pl.BlockSpec(memory_space=pltpu.VMEM)],
        out_specs=pl.BlockSpec(memory_space=pltpu.VMEM),
        scratch_shapes=[
            pltpu.VMEM((n_sub, lanes), jnp.float32),
            pltpu.SemaphoreType.DMA((n_sub,)),
            pltpu.SemaphoreType.DMA((n_sub,)),
            pltpu.SemaphoreType.DMA((n_row,)),
            pltpu.SemaphoreType.DMA((n_row,)),
            pltpu.SemaphoreType.DMA((n_rows,)),
            pltpu.SemaphoreType.DMA((n_rows,)),
        ],
        compiler_params=pltpu.CompilerParams(has_side_effects=True),
    )(picked.reshape(1, lanes))


def per_device(ensemble, obs_value, obs_var, obs_owner, obs_column, home_block, batch_order):
    members = ensemble.shape[2]
    levels_count = ensemble.shape[1]
    cols_dev = ensemble.shape[3]
    slab_count = lax.axis_size("slab")
    sub_count = lax.axis_size("sub")
    slab_index = lax.axis_index("slab")
    sub_index = lax.axis_index("sub")
    capacity = CAP
    cols_slab = cols_dev * sub_count
    nblocks = cols_slab * slab_count // BLK
    span_broad = cols_slab // (4 * BLK)
    span_narrow = max(span_broad // 4, 1)
    decays = (float(span_broad), float(span_narrow))
    assert 2 * span_broad + 1 <= cols_slab // BLK and slab_count >= 3
    owners = obs_owner[:, :, 0]
    obs_home = jnp.mod((owners * cols_slab + obs_column) // BLK + home_block, nblocks)
    onehot = (owners[:, :, None] == jnp.arange(slab_count, dtype=jnp.int32)[None, None, :]).astype(
        jnp.int32
    )
    running = jnp.cumsum(onehot, axis=1) - 1
    slot_rank = jnp.sum(onehot * running, axis=2)
    slot_global = owners * capacity + slot_rank
    slot_obs, slot_valid = slot_table(owners, slot_rank, slab_index, capacity)
    slot_column = jnp.take_along_axis(obs_column, slot_obs, axis=1)
    slot_level = slot_obs % levels_count
    holder = slot_column // cols_dev
    local_col = slot_column % cols_dev
    picked = ensemble[:, slot_level, :, local_col]
    retain = slot_valid & (holder == sub_index)
    picked = jnp.where(retain[:, :, None, None], picked, 0.0).reshape(
        BATCHES * capacity, BANDS * members
    )
    n_row = 32 if slab_count % 32 == 0 else slab_count
    gathered = gather_slots(picked, slab_count, sub_count, n_row)
    flat = (owners * BATCHES + jnp.arange(BATCHES, dtype=jnp.int32)[:, None]) * capacity + slot_rank
    priors = jnp.take(gathered.reshape(-1, BANDS * members), flat, axis=0)

    first, second = batch_order[0], batch_order[1]
    y0 = priors[first]
    stats0 = obs_statistics(y0, obs_value[first], obs_var[first], members)
    y1 = update_pool(priors[second], obs_home[second], *stats0, obs_home[first], nblocks, decays)
    stats1 = obs_statistics(y1, obs_value[second], obs_var[second], members)
    recorded = jnp.zeros_like(priors).at[first].set(y0).at[second].set(y1)

    my_cols = (slab_index * sub_count + sub_index) * cols_dev + jnp.arange(
        cols_dev, dtype=jnp.int32
    )
    near = [jnp.mod(slab_index + d, slab_count) for d in (-1, 0, 1)]
    for batch_id, stats in ((first, stats0), (second, stats1)):
        deviations, spread, increments = stats
        b_owners = lax.dynamic_index_in_dim(owners, batch_id, keepdims=True)
        b_rank = lax.dynamic_index_in_dim(slot_rank, batch_id, keepdims=True)
        tables = [slot_table(b_owners, b_rank, n, capacity) for n in near]
        idx = jnp.concatenate([t[0][0] for t in tables])
        valid = jnp.concatenate([t[1][0] for t in tables])
        ensemble = update_state(
            ensemble,
            my_cols,
            deviations[idx],
            spread[idx],
            increments[idx],
            obs_home[batch_id][idx],
            valid,
            nblocks,
            decays,
        )
    return (ensemble, recorded)


def solution(mesh):
    placed = (P(None, None, None, ("slab", "sub")), P(), P(), P(), P(), P(), P())
    return jax.shard_map(
        per_device,
        mesh=mesh,
        in_specs=placed,
        out_specs=(P(None, None, None, ("slab", "sub")), P()),
        check_vma=False,
    )
```

```python
import functools

import jax
import jax.numpy as jnp
from jax import lax
from jax.experimental import pallas as pl
from jax.experimental.pallas import tpu as pltpu
from jax.sharding import PartitionSpec as P

MESH = pl.DeviceIdType.MESH

BANDS = 2
BLK = 16
BATCHES = 2
CAP = 8


HIGHEST = lax.Precision.HIGHEST


def gc_weight(first, second, nblocks, length):
    block_gap = jnp.abs(first - second)
    block_gap = jnp.minimum(block_gap, nblocks - block_gap)
    scaled_gap = block_gap.astype(jnp.float32) / length
    near_part = (
        ((-0.25 * scaled_gap + 0.5) * scaled_gap + 0.625) * scaled_gap**3
        - 5.0 / 3.0 * scaled_gap**2
        + 1.0
    )
    floored = jnp.maximum(scaled_gap, 1.0)
    far_part = (
        (
            (((scaled_gap / 12.0 - 0.5) * scaled_gap + 0.625) * scaled_gap + 5.0 / 3.0) * scaled_gap
            - 5.0
        )
        * scaled_gap
        + 4.0
        - 2.0 / (3.0 * floored)
    )
    return jnp.where(scaled_gap <= 1.0, near_part, jnp.where(scaled_gap < 2.0, far_part, 0.0))


def obs_statistics(current, values, variances, members):
    banded = current.reshape(current.shape[0], BANDS, members)
    whole_obs = jnp.sum(banded, axis=1)
    centre = jnp.mean(whole_obs, axis=1, keepdims=True)
    spread = jnp.sum((whole_obs - centre) ** 2, axis=1) / (members - 1) + 1e-06
    post_var = 1.0 / (1.0 / spread + 1.0 / variances)
    post_mean = post_var * (centre[:, 0] / spread + values / variances)
    increments = (post_mean - centre[:, 0])[:, None] + (jnp.sqrt(post_var / spread) - 1.0)[
        :, None
    ] * (whole_obs - centre)
    deviations = banded - jnp.mean(banded, axis=2, keepdims=True)
    return (deviations, spread, increments)


def update_pool(pool, pool_homes, deviations, spread, increments, obs_homes, nblocks, decays):
    members = deviations.shape[2]
    banded = pool.reshape(pool.shape[0], BANDS, members)
    new_bands = []
    for band_no in range(BANDS):
        pool_band = banded[:, band_no, :]
        pool_dev = pool_band - jnp.mean(pool_band, axis=1, keepdims=True)
        weights = (
            gc_weight(pool_homes[:, None], obs_homes[None, :], nblocks, decays[band_no])
            / ((members - 1) * spread)[None, :]
        )
        crossed = jnp.einsum("pm,km->pk", pool_dev, deviations[:, band_no, :], precision=HIGHEST)
        change = jnp.einsum("pk,km->pm", crossed * weights, increments, precision=HIGHEST)
        new_bands.append(pool_band + change)
    return jnp.stack(new_bands, axis=1).reshape(pool.shape)


def update_state(ensemble, my_cols, deviations, spread, increments, obs_homes, valid, nblocks, decays):
    members = ensemble.shape[2]
    new_bands = []
    for band_no in range(BANDS):
        band_layer = ensemble[band_no]
        layer_dev = band_layer - jnp.mean(band_layer, axis=1, keepdims=True)
        obs_dev = deviations[:, band_no, :]
        weights = (
            gc_weight((my_cols // BLK)[:, None], obs_homes[None, :], nblocks, decays[band_no])
            / ((members - 1) * spread)[None, :]
        )
        weights = jnp.where(valid[None, :], weights, 0.0)
        crossed = jnp.einsum("lmc,km->lck", layer_dev, obs_dev, precision=HIGHEST)
        change = jnp.einsum("lck,km->lmc", crossed * weights[None], increments, precision=HIGHEST)
        new_bands.append(band_layer + change)
    return jnp.stack(new_bands, axis=0)


def slot_table(owners, slot_rank, slab_number, capacity):
    obs_count = owners.shape[1]
    matches = (owners == slab_number)[:, None, :] & (
        slot_rank[:, None, :] == jnp.arange(capacity, dtype=jnp.int32)[None, :, None]
    )
    slot_obs = jnp.sum(
        jnp.where(matches, jnp.arange(obs_count, dtype=jnp.int32)[None, None, :], 0), axis=2
    )
    slot_valid = jnp.any(matches, axis=2)
    return (slot_obs, slot_valid)


def gather_kernel(n_row, picked_ref, out_ref, part_ref, sem0, send0, sem_a, send_a, sem_b, send_b, sem_c, send_c):
    n_slab = lax.axis_size("slab")
    n_sub = lax.axis_size("sub")
    s = lax.axis_index("slab")
    u = lax.axis_index("sub")
    n_rows = n_slab // n_row
    row, loc = s // n_row, s % n_row

    def copy(src, dst, send, recv, dev):
        return pltpu.make_async_remote_copy(
            src_ref=src, dst_ref=dst, send_sem=send, recv_sem=recv, device_id=dev, device_id_type=MESH
        )

    def to_sub(d):
        q = (u + d) % n_sub
        return copy(picked_ref.at[q], part_ref.at[u], send0.at[q], sem0.at[u], (s, q))

    def from_sub(d):
        q = (u + d) % n_sub
        return copy(picked_ref.at[q], part_ref.at[q], send0.at[q], sem0.at[q], (s, q))

    barrier = pltpu.get_barrier_semaphore()
    for d in range(1, n_sub):
        pl.semaphore_signal(barrier, 1, device_id=(s, (u + d) % n_sub), device_id_type=MESH)

    def greet(d, c):
        dev = (row * n_row + (loc + d) % n_row, u)
        pl.semaphore_signal(barrier, 1, device_id=dev, device_id_type=MESH)
        return c

    lax.fori_loop(1, n_row, greet, 0)
    for d in range(1, n_rows):
        dev = (((row + d) % n_rows) * n_row + loc, u)
        pl.semaphore_signal(barrier, 1, device_id=dev, device_id_type=MESH)
    pl.semaphore_wait(barrier, (n_sub - 1) + (n_row - 1) + (n_rows - 1))

    for d in range(1, n_sub):
        to_sub(d).start()
    total = picked_ref[pl.ds(u, 1), :]
    for d in range(1, n_sub):
        from_sub(d).wait_recv()
        total = total + part_ref[pl.ds((u + d) % n_sub, 1), :]
    out_ref[u, pl.ds(s, 1), :] = total

    def own(r):
        return out_ref.at[u, pl.ds(r, 1)]

    def to_a(d):
        j = (loc + d) % n_row
        return copy(own(s), own(s), send_a.at[j], sem_a.at[loc], (row * n_row + j, u))

    def from_a(d):
        j = (loc + d) % n_row
        src = row * n_row + j
        return copy(own(src), own(src), send_a.at[j], sem_a.at[j], (src, u))

    def start_a(d, c):
        to_a(d).start()
        return c

    def wait_a(d, c):
        from_a(d).wait_recv()
        return c

    lax.fori_loop(1, n_row, start_a, 0)
    lax.fori_loop(1, n_row, wait_a, 0)

    def block(r):
        return out_ref.at[u, pl.ds(r * n_row, n_row)]

    def to_b(d):
        r = (row + d) % n_rows
        return copy(block(row), block(row), send_b.at[r], sem_b.at[row], (r * n_row + loc, u))

    def from_b(d):
        r = (row + d) % n_rows
        return copy(block(r), block(r), send_b.at[r], sem_b.at[r], (r * n_row + loc, u))

    for d in range(1, n_rows):
        to_b(d).start()
    for d in range(1, n_rows):
        from_b(d).wait_recv()

    def to_c(d):
        q = (u + d) % n_sub
        return copy(out_ref.at[u], out_ref.at[u], send_c.at[q], sem_c.at[u], (s, q))

    def from_c(d):
        q = (u + d) % n_sub
        return copy(out_ref.at[q], out_ref.at[q], send_c.at[q], sem_c.at[q], (s, q))

    for d in range(1, n_sub):
        to_c(d).start()
    for d in range(1, n_sub):
        from_c(d).wait_recv()

    for d in range(1, n_sub):
        to_sub(d).wait_send()
    lax.fori_loop(1, n_row, lambda d, c: (to_a(d).wait_send(), c)[1], 0)
    for d in range(1, n_rows):
        to_b(d).wait_send()
    for d in range(1, n_sub):
        to_c(d).wait_send()


def gather_slots(picked, n_slab, n_sub, n_row):
    rows, width = picked.shape
    lanes = rows // n_sub * width
    n_rows = n_slab // n_row
    return pl.pallas_call(
        functools.partial(gather_kernel, n_row),
        out_shape=jax.ShapeDtypeStruct((n_sub, n_slab, lanes), jnp.float32),
        in_specs=[pl.BlockSpec(memory_space=pltpu.VMEM)],
        out_specs=pl.BlockSpec(memory_space=pltpu.VMEM),
        scratch_shapes=[
            pltpu.VMEM((n_sub, lanes), jnp.float32),
            pltpu.SemaphoreType.DMA((n_sub,)),
            pltpu.SemaphoreType.DMA((n_sub,)),
            pltpu.SemaphoreType.DMA((n_row,)),
            pltpu.SemaphoreType.DMA((n_row,)),
            pltpu.SemaphoreType.DMA((n_rows,)),
            pltpu.SemaphoreType.DMA((n_rows,)),
            pltpu.SemaphoreType.DMA((n_sub,)),
            pltpu.SemaphoreType.DMA((n_sub,)),
        ],
        compiler_params=pltpu.CompilerParams(has_side_effects=True, collective_id=0),
    )(picked.reshape(n_sub, lanes))


def per_device(ensemble, obs_value, obs_var, obs_owner, obs_column, home_block, batch_order):
    members = ensemble.shape[2]
    levels_count = ensemble.shape[1]
    cols_dev = ensemble.shape[3]
    slab_count = lax.axis_size("slab")
    sub_count = lax.axis_size("sub")
    slab_index = lax.axis_index("slab")
    sub_index = lax.axis_index("sub")
    capacity = CAP
    cols_slab = cols_dev * sub_count
    nblocks = cols_slab * slab_count // BLK
    span_broad = cols_slab // (4 * BLK)
    span_narrow = max(span_broad // 4, 1)
    decays = (float(span_broad), float(span_narrow))
    assert 2 * span_broad + 1 <= cols_slab // BLK and slab_count >= 3
    owners = obs_owner[:, :, 0]
    obs_home = jnp.mod((owners * cols_slab + obs_column) // BLK + home_block, nblocks)
    onehot = (owners[:, :, None] == jnp.arange(slab_count, dtype=jnp.int32)[None, None, :]).astype(
        jnp.int32
    )
    running = jnp.cumsum(onehot, axis=1) - 1
    slot_rank = jnp.sum(onehot * running, axis=2)
    slot_global = owners * capacity + slot_rank
    slot_obs, slot_valid = slot_table(owners, slot_rank, slab_index, capacity)
    slot_column = jnp.take_along_axis(obs_column, slot_obs, axis=1)
    slot_level = slot_obs % levels_count
    holder = slot_column // cols_dev
    local_col = slot_column % cols_dev
    picked = ensemble[:, slot_level, :, local_col]
    retain = slot_valid & (holder == sub_index)
    picked = jnp.where(retain[:, :, None, None], picked, 0.0).reshape(
        BATCHES * capacity, BANDS * members
    )
    n_row = 32 if slab_count % 32 == 0 else slab_count
    gathered = gather_slots(picked, slab_count, sub_count, n_row)
    q_rows = BATCHES * capacity // sub_count
    row_of = jnp.arange(BATCHES, dtype=jnp.int32)[:, None] * capacity + slot_rank
    flat = (row_of // q_rows) * (slab_count * q_rows) + owners * q_rows + row_of % q_rows
    priors = jnp.take(gathered.reshape(-1, BANDS * members), flat, axis=0)

    first, second = batch_order[0], batch_order[1]
    y0 = priors[first]
    stats0 = obs_statistics(y0, obs_value[first], obs_var[first], members)
    y1 = update_pool(priors[second], obs_home[second], *stats0, obs_home[first], nblocks, decays)
    stats1 = obs_statistics(y1, obs_value[second], obs_var[second], members)
    recorded = jnp.zeros_like(priors).at[first].set(y0).at[second].set(y1)

    my_cols = (slab_index * sub_count + sub_index) * cols_dev + jnp.arange(
        cols_dev, dtype=jnp.int32
    )
    near = [jnp.mod(slab_index + d, slab_count) for d in (-1, 0, 1)]
    for batch_id, stats in ((first, stats0), (second, stats1)):
        deviations, spread, increments = stats
        b_owners = lax.dynamic_index_in_dim(owners, batch_id, keepdims=True)
        b_rank = lax.dynamic_index_in_dim(slot_rank, batch_id, keepdims=True)
        tables = [slot_table(b_owners, b_rank, n, capacity) for n in near]
        idx = jnp.concatenate([t[0][0] for t in tables])
        valid = jnp.concatenate([t[1][0] for t in tables])
        ensemble = update_state(
            ensemble,
            my_cols,
            deviations[idx],
            spread[idx],
            increments[idx],
            obs_home[batch_id][idx],
            valid,
            nblocks,
            decays,
        )
    return (ensemble, recorded)


def solution(mesh):
    placed = (P(None, None, None, ("slab", "sub")), P(), P(), P(), P(), P(), P())
    return jax.shard_map(
        per_device,
        mesh=mesh,
        in_specs=placed,
        out_specs=(P(None, None, None, ("slab", "sub")), P()),
        check_vma=False,
    )
```

```python
import functools

import jax
import jax.numpy as jnp
from jax import lax
from jax.experimental import pallas as pl
from jax.experimental.pallas import tpu as pltpu
from jax.sharding import PartitionSpec as P

MESH = pl.DeviceIdType.MESH

BANDS = 2
BLK = 16
BATCHES = 2
CAP = 8


HIGHEST = lax.Precision.HIGHEST


def gc_weight(first, second, nblocks, length):
    block_gap = jnp.abs(first - second)
    block_gap = jnp.minimum(block_gap, nblocks - block_gap)
    scaled_gap = block_gap.astype(jnp.float32) / length
    near_part = (
        ((-0.25 * scaled_gap + 0.5) * scaled_gap + 0.625) * scaled_gap**3
        - 5.0 / 3.0 * scaled_gap**2
        + 1.0
    )
    floored = jnp.maximum(scaled_gap, 1.0)
    far_part = (
        (
            (((scaled_gap / 12.0 - 0.5) * scaled_gap + 0.625) * scaled_gap + 5.0 / 3.0) * scaled_gap
            - 5.0
        )
        * scaled_gap
        + 4.0
        - 2.0 / (3.0 * floored)
    )
    return jnp.where(scaled_gap <= 1.0, near_part, jnp.where(scaled_gap < 2.0, far_part, 0.0))


def obs_statistics(current, values, variances, members):
    banded = current.reshape(current.shape[0], BANDS, members)
    whole_obs = jnp.sum(banded, axis=1)
    centre = jnp.mean(whole_obs, axis=1, keepdims=True)
    spread = jnp.sum((whole_obs - centre) ** 2, axis=1) / (members - 1) + 1e-06
    post_var = 1.0 / (1.0 / spread + 1.0 / variances)
    post_mean = post_var * (centre[:, 0] / spread + values / variances)
    increments = (post_mean - centre[:, 0])[:, None] + (jnp.sqrt(post_var / spread) - 1.0)[
        :, None
    ] * (whole_obs - centre)
    deviations = banded - jnp.mean(banded, axis=2, keepdims=True)
    return (deviations, spread, increments)


def update_pool(pool, pool_homes, deviations, spread, increments, obs_homes, nblocks, decays):
    members = deviations.shape[2]
    banded = pool.reshape(pool.shape[0], BANDS, members)
    new_bands = []
    for band_no in range(BANDS):
        pool_band = banded[:, band_no, :]
        pool_dev = pool_band - jnp.mean(pool_band, axis=1, keepdims=True)
        weights = (
            gc_weight(pool_homes[:, None], obs_homes[None, :], nblocks, decays[band_no])
            / ((members - 1) * spread)[None, :]
        )
        crossed = jnp.einsum("pm,km->pk", pool_dev, deviations[:, band_no, :], precision=HIGHEST)
        change = jnp.einsum("pk,km->pm", crossed * weights, increments, precision=HIGHEST)
        new_bands.append(pool_band + change)
    return jnp.stack(new_bands, axis=1).reshape(pool.shape)


def update_state(ensemble, my_cols, deviations, spread, increments, obs_homes, valid, nblocks, decays):
    members = ensemble.shape[2]
    new_bands = []
    for band_no in range(BANDS):
        band_layer = ensemble[band_no]
        layer_dev = band_layer - jnp.mean(band_layer, axis=1, keepdims=True)
        obs_dev = deviations[:, band_no, :]
        weights = (
            gc_weight((my_cols // BLK)[:, None], obs_homes[None, :], nblocks, decays[band_no])
            / ((members - 1) * spread)[None, :]
        )
        weights = jnp.where(valid[None, :], weights, 0.0)
        crossed = jnp.einsum("lmc,km->lck", layer_dev, obs_dev, precision=HIGHEST)
        change = jnp.einsum("lck,km->lmc", crossed * weights[None], increments, precision=HIGHEST)
        new_bands.append(band_layer + change)
    return jnp.stack(new_bands, axis=0)


def slot_table(owners, slot_rank, slab_number, capacity):
    obs_count = owners.shape[1]
    matches = (owners == slab_number)[:, None, :] & (
        slot_rank[:, None, :] == jnp.arange(capacity, dtype=jnp.int32)[None, :, None]
    )
    slot_obs = jnp.sum(
        jnp.where(matches, jnp.arange(obs_count, dtype=jnp.int32)[None, None, :], 0), axis=2
    )
    slot_valid = jnp.any(matches, axis=2)
    return (slot_obs, slot_valid)


def gather_kernel(n_row, picked_ref, out_ref, part_ref, sem0, send0, sem_a, send_a, sem_b, send_b, sem_c, send_c):
    n_slab = lax.axis_size("slab")
    n_sub = lax.axis_size("sub")
    s = lax.axis_index("slab")
    u = lax.axis_index("sub")
    n_rows = n_slab // n_row
    row, loc = s // n_row, s % n_row

    def copy(src, dst, send, recv, dev):
        return pltpu.make_async_remote_copy(
            src_ref=src, dst_ref=dst, send_sem=send, recv_sem=recv, device_id=dev, device_id_type=MESH
        )

    def to_sub(d):
        q = (u + d) % n_sub
        return copy(picked_ref.at[q], part_ref.at[u], send0.at[q], sem0.at[u], (s, q))

    def from_sub(d):
        q = (u + d) % n_sub
        return copy(picked_ref.at[q], part_ref.at[q], send0.at[q], sem0.at[q], (s, q))

    barrier = pltpu.get_barrier_semaphore()
    for d in range(1, n_sub):
        pl.semaphore_signal(barrier, 1, device_id=(s, (u + d) % n_sub), device_id_type=MESH)

    def greet(d, c):
        dev = (row * n_row + (loc + d) % n_row, u)
        pl.semaphore_signal(barrier, 1, device_id=dev, device_id_type=MESH)
        return c

    lax.fori_loop(1, n_row, greet, 0)
    for d in range(1, n_rows):
        dev = (((row + d) % n_rows) * n_row + loc, u)
        pl.semaphore_signal(barrier, 1, device_id=dev, device_id_type=MESH)
    pl.semaphore_wait(barrier, (n_sub - 1) + (n_row - 1) + (n_rows - 1))

    for d in range(1, n_sub):
        to_sub(d).start()
    total = picked_ref[pl.ds(u, 1), :]
    for d in range(1, n_sub):
        from_sub(d).wait_recv()
        total = total + part_ref[pl.ds((u + d) % n_sub, 1), :]
    half = n_row // 2

    def own(t):
        j = t % n_row
        return out_ref.at[u, t // n_row, j // half, pl.ds(j % half, 1)]

    own(s)[...] = total

    def to_a(d):
        j = (loc + d) % n_row
        return copy(own(s), own(s), send_a.at[j], sem_a.at[loc], (row * n_row + j, u))

    def from_a(d):
        j = (loc + d) % n_row
        src = row * n_row + j
        return copy(own(src), own(src), send_a.at[j], sem_a.at[j], (src, u))

    def start_a(d, c):
        to_a(d).start()
        return c

    def wait_a(d, c):
        from_a(d).wait_recv()
        return c

    lax.fori_loop(1, n_row, start_a, 0)
    lax.fori_loop(1, n_row, wait_a, 0)

    def peer_x(d):
        r = (row + d) % n_rows
        return r, (r * n_row + loc, u)

    def peer_y(d):
        q = (u + d) % n_sub
        return q, (s, q)

    def to_b1(d):
        r, dev = peer_x(d)
        return copy(out_ref.at[u, row, 0], out_ref.at[u, row, 0], send_b.at[0, r], sem_b.at[0, row], dev)

    def from_b1(d):
        r, dev = peer_x(d)
        return copy(out_ref.at[u, r, 0], out_ref.at[u, r, 0], send_b.at[0, r], sem_b.at[0, r], dev)

    def to_c1(d):
        q, dev = peer_y(d)
        return copy(out_ref.at[u, row, 1], out_ref.at[u, row, 1], send_c.at[0, q], sem_c.at[0, u], dev)

    def from_c1(d):
        q, dev = peer_y(d)
        return copy(out_ref.at[q, row, 1], out_ref.at[q, row, 1], send_c.at[0, q], sem_c.at[0, q], dev)

    def to_b2(d):
        r, dev = peer_x(d)
        return copy(out_ref.at[:, row, 1], out_ref.at[:, row, 1], send_b.at[1, r], sem_b.at[1, row], dev)

    def from_b2(d):
        r, dev = peer_x(d)
        return copy(out_ref.at[:, r, 1], out_ref.at[:, r, 1], send_b.at[1, r], sem_b.at[1, r], dev)

    def to_c2(d):
        q, dev = peer_y(d)
        return copy(out_ref.at[u, :, 0], out_ref.at[u, :, 0], send_c.at[1, q], sem_c.at[1, u], dev)

    def from_c2(d):
        q, dev = peer_y(d)
        return copy(out_ref.at[q, :, 0], out_ref.at[q, :, 0], send_c.at[1, q], sem_c.at[1, q], dev)

    for d in range(1, n_rows):
        to_b1(d).start()
    for d in range(1, n_sub):
        to_c1(d).start()
    for d in range(1, n_sub):
        from_c1(d).wait_recv()
    for d in range(1, n_rows):
        to_b2(d).start()
    for d in range(1, n_rows):
        from_b1(d).wait_recv()
    for d in range(1, n_sub):
        to_c2(d).start()
    for d in range(1, n_rows):
        from_b2(d).wait_recv()
    for d in range(1, n_sub):
        from_c2(d).wait_recv()

    for d in range(1, n_sub):
        to_sub(d).wait_send()
    lax.fori_loop(1, n_row, lambda d, c: (to_a(d).wait_send(), c)[1], 0)
    for d in range(1, n_rows):
        to_b1(d).wait_send()
        to_b2(d).wait_send()
    for d in range(1, n_sub):
        to_c1(d).wait_send()
        to_c2(d).wait_send()


def gather_slots(picked, n_slab, n_sub, n_row):
    rows, width = picked.shape
    lanes = rows // n_sub * width
    n_rows = n_slab // n_row
    gathered = pl.pallas_call(
        functools.partial(gather_kernel, n_row),
        out_shape=jax.ShapeDtypeStruct((n_sub, n_rows, 2, n_row // 2, lanes), jnp.float32),
        in_specs=[pl.BlockSpec(memory_space=pltpu.VMEM)],
        out_specs=pl.BlockSpec(memory_space=pltpu.VMEM),
        scratch_shapes=[
            pltpu.VMEM((n_sub, lanes), jnp.float32),
            pltpu.SemaphoreType.DMA((n_sub,)),
            pltpu.SemaphoreType.DMA((n_sub,)),
            pltpu.SemaphoreType.DMA((n_row,)),
            pltpu.SemaphoreType.DMA((n_row,)),
            pltpu.SemaphoreType.DMA((2, n_rows)),
            pltpu.SemaphoreType.DMA((2, n_rows)),
            pltpu.SemaphoreType.DMA((2, n_sub)),
            pltpu.SemaphoreType.DMA((2, n_sub)),
        ],
        compiler_params=pltpu.CompilerParams(has_side_effects=True, collective_id=0),
    )(picked.reshape(n_sub, lanes))
    return gathered.reshape(n_sub, n_slab, lanes)


def per_device(ensemble, obs_value, obs_var, obs_owner, obs_column, home_block, batch_order):
    members = ensemble.shape[2]
    levels_count = ensemble.shape[1]
    cols_dev = ensemble.shape[3]
    slab_count = lax.axis_size("slab")
    sub_count = lax.axis_size("sub")
    slab_index = lax.axis_index("slab")
    sub_index = lax.axis_index("sub")
    capacity = CAP
    cols_slab = cols_dev * sub_count
    nblocks = cols_slab * slab_count // BLK
    span_broad = cols_slab // (4 * BLK)
    span_narrow = max(span_broad // 4, 1)
    decays = (float(span_broad), float(span_narrow))
    assert 2 * span_broad + 1 <= cols_slab // BLK and slab_count >= 3
    owners = obs_owner[:, :, 0]
    obs_home = jnp.mod((owners * cols_slab + obs_column) // BLK + home_block, nblocks)
    onehot = (owners[:, :, None] == jnp.arange(slab_count, dtype=jnp.int32)[None, None, :]).astype(
        jnp.int32
    )
    running = jnp.cumsum(onehot, axis=1) - 1
    slot_rank = jnp.sum(onehot * running, axis=2)
    slot_global = owners * capacity + slot_rank
    slot_obs, slot_valid = slot_table(owners, slot_rank, slab_index, capacity)
    slot_column = jnp.take_along_axis(obs_column, slot_obs, axis=1)
    slot_level = slot_obs % levels_count
    holder = slot_column // cols_dev
    local_col = slot_column % cols_dev
    picked = ensemble[:, slot_level, :, local_col]
    retain = slot_valid & (holder == sub_index)
    picked = jnp.where(retain[:, :, None, None], picked, 0.0).reshape(
        BATCHES * capacity, BANDS * members
    )
    n_row = 32 if slab_count % 32 == 0 else slab_count
    gathered = gather_slots(picked, slab_count, sub_count, n_row)
    q_rows = BATCHES * capacity // sub_count
    row_of = jnp.arange(BATCHES, dtype=jnp.int32)[:, None] * capacity + slot_rank
    flat = (row_of // q_rows) * (slab_count * q_rows) + owners * q_rows + row_of % q_rows
    priors = jnp.take(gathered.reshape(-1, BANDS * members), flat, axis=0)

    first, second = batch_order[0], batch_order[1]
    y0 = priors[first]
    stats0 = obs_statistics(y0, obs_value[first], obs_var[first], members)
    y1 = update_pool(priors[second], obs_home[second], *stats0, obs_home[first], nblocks, decays)
    stats1 = obs_statistics(y1, obs_value[second], obs_var[second], members)
    recorded = jnp.zeros_like(priors).at[first].set(y0).at[second].set(y1)

    my_cols = (slab_index * sub_count + sub_index) * cols_dev + jnp.arange(
        cols_dev, dtype=jnp.int32
    )
    near = [jnp.mod(slab_index + d, slab_count) for d in (-1, 0, 1)]
    for batch_id, stats in ((first, stats0), (second, stats1)):
        deviations, spread, increments = stats
        b_owners = lax.dynamic_index_in_dim(owners, batch_id, keepdims=True)
        b_rank = lax.dynamic_index_in_dim(slot_rank, batch_id, keepdims=True)
        tables = [slot_table(b_owners, b_rank, n, capacity) for n in near]
        idx = jnp.concatenate([t[0][0] for t in tables])
        valid = jnp.concatenate([t[1][0] for t in tables])
        ensemble = update_state(
            ensemble,
            my_cols,
            deviations[idx],
            spread[idx],
            increments[idx],
            obs_home[batch_id][idx],
            valid,
            nblocks,
            decays,
        )
    return (ensemble, recorded)


def solution(mesh):
    placed = (P(None, None, None, ("slab", "sub")), P(), P(), P(), P(), P(), P())
    return jax.shard_map(
        per_device,
        mesh=mesh,
        in_specs=placed,
        out_specs=(P(None, None, None, ("slab", "sub")), P()),
        check_vma=False,
    )
```

```python
import functools

import jax
import jax.numpy as jnp
from jax import lax
from jax.experimental import pallas as pl
from jax.experimental.pallas import tpu as pltpu
from jax.sharding import PartitionSpec as P

MESH = pl.DeviceIdType.MESH

BANDS = 2
BLK = 16
BATCHES = 2
CAP = 8


HIGHEST = lax.Precision.HIGHEST


def gc_weight(first, second, nblocks, length):
    block_gap = jnp.abs(first - second)
    block_gap = jnp.minimum(block_gap, nblocks - block_gap)
    scaled_gap = block_gap.astype(jnp.float32) / length
    near_part = (
        ((-0.25 * scaled_gap + 0.5) * scaled_gap + 0.625) * scaled_gap**3
        - 5.0 / 3.0 * scaled_gap**2
        + 1.0
    )
    floored = jnp.maximum(scaled_gap, 1.0)
    far_part = (
        (
            (((scaled_gap / 12.0 - 0.5) * scaled_gap + 0.625) * scaled_gap + 5.0 / 3.0) * scaled_gap
            - 5.0
        )
        * scaled_gap
        + 4.0
        - 2.0 / (3.0 * floored)
    )
    return jnp.where(scaled_gap <= 1.0, near_part, jnp.where(scaled_gap < 2.0, far_part, 0.0))


def obs_statistics(current, values, variances, members):
    banded = current.reshape(current.shape[0], BANDS, members)
    whole_obs = jnp.sum(banded, axis=1)
    centre = jnp.mean(whole_obs, axis=1, keepdims=True)
    spread = jnp.sum((whole_obs - centre) ** 2, axis=1) / (members - 1) + 1e-06
    post_var = 1.0 / (1.0 / spread + 1.0 / variances)
    post_mean = post_var * (centre[:, 0] / spread + values / variances)
    increments = (post_mean - centre[:, 0])[:, None] + (jnp.sqrt(post_var / spread) - 1.0)[
        :, None
    ] * (whole_obs - centre)
    deviations = banded - jnp.mean(banded, axis=2, keepdims=True)
    return (deviations, spread, increments)


def update_pool(pool, pool_homes, deviations, spread, increments, obs_homes, nblocks, decays):
    members = deviations.shape[2]
    banded = pool.reshape(pool.shape[0], BANDS, members)
    pool_dev = banded - jnp.mean(banded, axis=2, keepdims=True)
    weights = jnp.stack(
        [gc_weight(pool_homes[:, None], obs_homes[None, :], nblocks, decay) for decay in decays]
    ) / ((members - 1) * spread)[None, None, :]
    crossed = jnp.einsum("pbm,kbm->bpk", pool_dev, deviations, precision=HIGHEST)
    change = jnp.einsum("bpk,km->pbm", crossed * weights, increments, precision=HIGHEST)
    return (banded + change).reshape(pool.shape)


def update_state(ensemble, col_blocks, deviations, spread, increments, obs_homes, valid, nblocks, decays):
    members = ensemble.shape[2]
    layer_dev = ensemble - jnp.mean(ensemble, axis=2, keepdims=True)
    weights = jnp.stack(
        [gc_weight(col_blocks[:, None], obs_homes[None, :], nblocks, decay) for decay in decays]
    ) / ((members - 1) * spread)[None, None, :]
    weights = jnp.where(valid[None, None, :], weights, 0.0)
    crossed = jnp.einsum("blmc,kbm->blck", layer_dev, deviations, precision=HIGHEST)
    change = jnp.einsum("blck,km->blmc", crossed * weights[:, None], increments, precision=HIGHEST)
    return ensemble + change


def pick(stacked, which):
    out = stacked[0]
    for i in range(1, stacked.shape[0]):
        out = jnp.where(which == i, stacked[i], out)
    return out


def slot_table(owners, slot_rank, slab_number, capacity):
    obs_count = owners.shape[1]
    matches = (owners == slab_number)[:, None, :] & (
        slot_rank[:, None, :] == jnp.arange(capacity, dtype=jnp.int32)[None, :, None]
    )
    slot_obs = jnp.sum(
        jnp.where(matches, jnp.arange(obs_count, dtype=jnp.int32)[None, None, :], 0), axis=2
    )
    slot_valid = jnp.any(matches, axis=2)
    return (slot_obs, slot_valid)


def gather_kernel(n_row, picked_ref, out_ref, part_ref, sem0, send0, sem_a, send_a, sem_b, send_b, sem_c, send_c):
    n_slab = lax.axis_size("slab")
    n_sub = lax.axis_size("sub")
    s = lax.axis_index("slab")
    u = lax.axis_index("sub")
    n_rows = n_slab // n_row
    row, loc = s // n_row, s % n_row

    def copy(src, dst, send, recv, dev):
        return pltpu.make_async_remote_copy(
            src_ref=src, dst_ref=dst, send_sem=send, recv_sem=recv, device_id=dev, device_id_type=MESH
        )

    def to_sub(d):
        q = (u + d) % n_sub
        return copy(picked_ref.at[q], part_ref.at[u], send0.at[q], sem0.at[u], (s, q))

    def from_sub(d):
        q = (u + d) % n_sub
        return copy(picked_ref.at[q], part_ref.at[q], send0.at[q], sem0.at[q], (s, q))

    barrier = pltpu.get_barrier_semaphore()
    for d in range(1, n_sub):
        pl.semaphore_signal(barrier, 1, device_id=(s, (u + d) % n_sub), device_id_type=MESH)

    def greet(d, c):
        dev = (row * n_row + (loc + d) % n_row, u)
        pl.semaphore_signal(barrier, 1, device_id=dev, device_id_type=MESH)
        return c

    lax.fori_loop(1, n_row, greet, 0)
    for d in range(1, n_rows):
        dev = (((row + d) % n_rows) * n_row + loc, u)
        pl.semaphore_signal(barrier, 1, device_id=dev, device_id_type=MESH)
    pl.semaphore_wait(barrier, (n_sub - 1) + (n_row - 1) + (n_rows - 1))

    for d in range(1, n_sub):
        to_sub(d).start()
    total = picked_ref[pl.ds(u, 1), :]
    for d in range(1, n_sub):
        from_sub(d).wait_recv()
        total = total + part_ref[pl.ds((u + d) % n_sub, 1), :]
    half = n_row // 2

    def own(t):
        j = t % n_row
        return out_ref.at[u, t // n_row, j // half, pl.ds(j % half, 1)]

    own(s)[...] = total

    def to_a(d):
        j = (loc + d) % n_row
        return copy(own(s), own(s), send_a.at[j], sem_a.at[loc], (row * n_row + j, u))

    def from_a(d):
        j = (loc + d) % n_row
        src = row * n_row + j
        return copy(own(src), own(src), send_a.at[j], sem_a.at[j], (src, u))

    def start_a(d, c):
        to_a(d).start()
        return c

    def wait_a(d, c):
        from_a(d).wait_recv()
        return c

    lax.fori_loop(1, n_row, start_a, 0)
    lax.fori_loop(1, n_row, wait_a, 0)

    def peer_x(d):
        r = (row + d) % n_rows
        return r, (r * n_row + loc, u)

    def peer_y(d):
        q = (u + d) % n_sub
        return q, (s, q)

    def to_b1(d):
        r, dev = peer_x(d)
        return copy(out_ref.at[u, row, 0], out_ref.at[u, row, 0], send_b.at[0, r], sem_b.at[0, row], dev)

    def from_b1(d):
        r, dev = peer_x(d)
        return copy(out_ref.at[u, r, 0], out_ref.at[u, r, 0], send_b.at[0, r], sem_b.at[0, r], dev)

    def to_c1(d):
        q, dev = peer_y(d)
        return copy(out_ref.at[u, row, 1], out_ref.at[u, row, 1], send_c.at[0, q], sem_c.at[0, u], dev)

    def from_c1(d):
        q, dev = peer_y(d)
        return copy(out_ref.at[q, row, 1], out_ref.at[q, row, 1], send_c.at[0, q], sem_c.at[0, q], dev)

    def to_b2(d):
        r, dev = peer_x(d)
        return copy(out_ref.at[:, row, 1], out_ref.at[:, row, 1], send_b.at[1, r], sem_b.at[1, row], dev)

    def from_b2(d):
        r, dev = peer_x(d)
        return copy(out_ref.at[:, r, 1], out_ref.at[:, r, 1], send_b.at[1, r], sem_b.at[1, r], dev)

    def to_c2(d):
        q, dev = peer_y(d)
        return copy(out_ref.at[u, :, 0], out_ref.at[u, :, 0], send_c.at[1, q], sem_c.at[1, u], dev)

    def from_c2(d):
        q, dev = peer_y(d)
        return copy(out_ref.at[q, :, 0], out_ref.at[q, :, 0], send_c.at[1, q], sem_c.at[1, q], dev)

    for d in range(1, n_rows):
        to_b1(d).start()
    for d in range(1, n_sub):
        to_c1(d).start()
    for d in range(1, n_sub):
        from_c1(d).wait_recv()
    for d in range(1, n_rows):
        to_b2(d).start()
    for d in range(1, n_rows):
        from_b1(d).wait_recv()
    for d in range(1, n_sub):
        to_c2(d).start()
    for d in range(1, n_rows):
        from_b2(d).wait_recv()
    for d in range(1, n_sub):
        from_c2(d).wait_recv()

    for d in range(1, n_sub):
        to_sub(d).wait_send()
    lax.fori_loop(1, n_row, lambda d, c: (to_a(d).wait_send(), c)[1], 0)
    for d in range(1, n_rows):
        to_b1(d).wait_send()
        to_b2(d).wait_send()
    for d in range(1, n_sub):
        to_c1(d).wait_send()
        to_c2(d).wait_send()


def gather_slots(picked, n_slab, n_sub, n_row):
    rows, width = picked.shape
    lanes = rows // n_sub * width
    n_rows = n_slab // n_row
    gathered = pl.pallas_call(
        functools.partial(gather_kernel, n_row),
        out_shape=jax.ShapeDtypeStruct((n_sub, n_rows, 2, n_row // 2, lanes), jnp.float32),
        in_specs=[pl.BlockSpec(memory_space=pltpu.VMEM)],
        out_specs=pl.BlockSpec(memory_space=pltpu.VMEM),
        scratch_shapes=[
            pltpu.VMEM((n_sub, lanes), jnp.float32),
            pltpu.SemaphoreType.DMA((n_sub,)),
            pltpu.SemaphoreType.DMA((n_sub,)),
            pltpu.SemaphoreType.DMA((n_row,)),
            pltpu.SemaphoreType.DMA((n_row,)),
            pltpu.SemaphoreType.DMA((2, n_rows)),
            pltpu.SemaphoreType.DMA((2, n_rows)),
            pltpu.SemaphoreType.DMA((2, n_sub)),
            pltpu.SemaphoreType.DMA((2, n_sub)),
        ],
        compiler_params=pltpu.CompilerParams(has_side_effects=True, collective_id=0),
    )(picked.reshape(n_sub, lanes))
    return gathered.reshape(n_sub, n_slab, lanes)


def per_device(ensemble, obs_value, obs_var, obs_owner, obs_column, home_block, batch_order):
    members = ensemble.shape[2]
    levels_count = ensemble.shape[1]
    cols_dev = ensemble.shape[3]
    slab_count = lax.axis_size("slab")
    sub_count = lax.axis_size("sub")
    slab_index = lax.axis_index("slab")
    sub_index = lax.axis_index("sub")
    capacity = CAP
    cols_slab = cols_dev * sub_count
    nblocks = cols_slab * slab_count // BLK
    span_broad = cols_slab // (4 * BLK)
    span_narrow = max(span_broad // 4, 1)
    decays = (float(span_broad), float(span_narrow))
    assert 2 * span_broad + 1 <= cols_slab // BLK and slab_count >= 3
    owners = obs_owner[:, :, 0]
    obs_home = jnp.mod((owners * cols_slab + obs_column) // BLK + home_block, nblocks)
    onehot = (owners[:, :, None] == jnp.arange(slab_count, dtype=jnp.int32)[None, None, :]).astype(
        jnp.int32
    )
    running = jnp.cumsum(onehot, axis=1) - 1
    slot_rank = jnp.sum(onehot * running, axis=2)
    slot_obs, slot_valid = slot_table(owners, slot_rank, slab_index, capacity)
    slot_column = jnp.take_along_axis(obs_column, slot_obs, axis=1)
    slot_level = slot_obs % levels_count
    holder = slot_column // cols_dev
    local_col = slot_column % cols_dev
    picked = ensemble[:, slot_level, :, local_col]
    retain = slot_valid & (holder == sub_index)
    picked = jnp.where(retain[:, :, None, None], picked, 0.0).reshape(
        BATCHES * capacity, BANDS * members
    )
    n_row = 32 if slab_count % 32 == 0 else slab_count
    gathered = gather_slots(picked, slab_count, sub_count, n_row)
    q_rows = BATCHES * capacity // sub_count
    width = BANDS * members
    row_of = jnp.arange(BATCHES, dtype=jnp.int32)[:, None] * capacity + slot_rank
    lines = jnp.take(
        gathered.reshape(sub_count * slab_count, q_rows * width),
        ((row_of // q_rows) * slab_count + owners).reshape(-1),
        axis=0,
    )
    part = (row_of % q_rows).reshape(-1, 1)
    flat_priors = lines[:, :width]
    for r in range(1, q_rows):
        flat_priors = jnp.where(part == r, lines[:, r * width : (r + 1) * width], flat_priors)
    priors = flat_priors.reshape(BATCHES, -1, width)

    first, second = batch_order[0], batch_order[1]
    y0 = pick(priors, first)
    home0 = pick(obs_home, first)
    home1 = pick(obs_home, second)
    stats0 = obs_statistics(y0, pick(obs_value, first), pick(obs_var, first), members)
    y1 = update_pool(pick(priors, second), home1, *stats0, home0, nblocks, decays)
    stats1 = obs_statistics(y1, pick(obs_value, second), pick(obs_var, second), members)
    which = jnp.arange(BATCHES, dtype=jnp.int32)[:, None, None]
    recorded = jnp.where(which == first, y0[None], y1[None])

    col_blocks = ((slab_index * sub_count + sub_index) * cols_dev + jnp.arange(
        cols_dev, dtype=jnp.int32
    )) // BLK
    near = jnp.mod(slab_index + jnp.arange(-1, 2, dtype=jnp.int32), slab_count)
    matches = (owners[:, None, None, :] == near[None, :, None, None]) & (
        slot_rank[:, None, None, :] == jnp.arange(capacity, dtype=jnp.int32)[None, None, :, None]
    )
    near_obs = jnp.sum(
        jnp.where(matches, jnp.arange(owners.shape[1], dtype=jnp.int32), 0), axis=3
    ).reshape(BATCHES, -1)
    near_valid = jnp.any(matches, axis=3).reshape(BATCHES, -1)
    for batch_id, homes, stats in ((first, home0, stats0), (second, home1, stats1)):
        deviations, spread, increments = stats
        table = jnp.concatenate(
            [
                deviations.reshape(-1, width),
                increments,
                spread[:, None],
                homes[:, None].astype(jnp.float32),
            ],
            axis=1,
        )
        rows = jnp.take(table, pick(near_obs, batch_id), axis=0)
        ensemble = update_state(
            ensemble,
            col_blocks,
            rows[:, :width].reshape(-1, BANDS, members),
            rows[:, width + members],
            rows[:, width : width + members],
            rows[:, width + members + 1].astype(jnp.int32),
            pick(near_valid, batch_id),
            nblocks,
            decays,
        )
    return (ensemble, recorded)


def solution(mesh):
    placed = (P(None, None, None, ("slab", "sub")), P(), P(), P(), P(), P(), P())
    return jax.shard_map(
        per_device,
        mesh=mesh,
        in_specs=placed,
        out_specs=(P(None, None, None, ("slab", "sub")), P()),
        check_vma=False,
    )
```

```python
import functools

import jax
import jax.numpy as jnp
from jax import lax
from jax.experimental import pallas as pl
from jax.experimental.pallas import tpu as pltpu
from jax.sharding import PartitionSpec as P

MESH = pl.DeviceIdType.MESH

BANDS = 2
BLK = 16
BATCHES = 2
CAP = 8


HIGHEST = lax.Precision.HIGHEST


def gc_weight(first, second, nblocks, length):
    block_gap = jnp.abs(first - second)
    block_gap = jnp.minimum(block_gap, nblocks - block_gap)
    scaled_gap = block_gap.astype(jnp.float32) / length
    near_part = (
        ((-0.25 * scaled_gap + 0.5) * scaled_gap + 0.625) * scaled_gap**3
        - 5.0 / 3.0 * scaled_gap**2
        + 1.0
    )
    floored = jnp.maximum(scaled_gap, 1.0)
    far_part = (
        (
            (((scaled_gap / 12.0 - 0.5) * scaled_gap + 0.625) * scaled_gap + 5.0 / 3.0) * scaled_gap
            - 5.0
        )
        * scaled_gap
        + 4.0
        - 2.0 / (3.0 * floored)
    )
    return jnp.where(scaled_gap <= 1.0, near_part, jnp.where(scaled_gap < 2.0, far_part, 0.0))


def obs_statistics(current, values, variances, members):
    banded = current.reshape(current.shape[0], BANDS, members)
    whole_obs = jnp.sum(banded, axis=1)
    centre = jnp.mean(whole_obs, axis=1, keepdims=True)
    spread = jnp.sum((whole_obs - centre) ** 2, axis=1) / (members - 1) + 1e-06
    post_var = 1.0 / (1.0 / spread + 1.0 / variances)
    post_mean = post_var * (centre[:, 0] / spread + values / variances)
    increments = (post_mean - centre[:, 0])[:, None] + (jnp.sqrt(post_var / spread) - 1.0)[
        :, None
    ] * (whole_obs - centre)
    deviations = banded - jnp.mean(banded, axis=2, keepdims=True)
    return (deviations, spread, increments)


def update_pool(pool, pool_homes, deviations, spread, increments, obs_homes, nblocks, decays):
    members = deviations.shape[2]
    banded = pool.reshape(pool.shape[0], BANDS, members)
    pool_dev = banded - jnp.mean(banded, axis=2, keepdims=True)
    weights = jnp.stack(
        [gc_weight(pool_homes[:, None], obs_homes[None, :], nblocks, decay) for decay in decays]
    ) / ((members - 1) * spread)[None, None, :]
    crossed = jnp.einsum("pbm,kbm->bpk", pool_dev, deviations, precision=HIGHEST)
    change = jnp.einsum("bpk,km->pbm", crossed * weights, increments, precision=HIGHEST)
    return (banded + change).reshape(pool.shape)


def update_state(ensemble, col_blocks, deviations, spread, increments, obs_homes, valid, nblocks, decays):
    members = ensemble.shape[2]
    layer_dev = ensemble - jnp.mean(ensemble, axis=2, keepdims=True)
    weights = jnp.stack(
        [gc_weight(col_blocks[:, None], obs_homes[None, :], nblocks, decay) for decay in decays]
    ) / ((members - 1) * spread)[None, None, :]
    weights = jnp.where(valid[None, None, :], weights, 0.0)
    crossed = jnp.einsum("blmc,kbm->blck", layer_dev, deviations, precision=HIGHEST)
    change = jnp.einsum("blck,km->blmc", crossed * weights[:, None], increments, precision=HIGHEST)
    return ensemble + change


def pick(stacked, which):
    out = stacked[0]
    for i in range(1, stacked.shape[0]):
        out = jnp.where(which == i, stacked[i], out)
    return out


def slot_table(owners, slot_rank, slab_number, capacity):
    obs_count = owners.shape[1]
    matches = (owners == slab_number)[:, None, :] & (
        slot_rank[:, None, :] == jnp.arange(capacity, dtype=jnp.int32)[None, :, None]
    )
    slot_obs = jnp.sum(
        jnp.where(matches, jnp.arange(obs_count, dtype=jnp.int32)[None, None, :], 0), axis=2
    )
    slot_valid = jnp.any(matches, axis=2)
    return (slot_obs, slot_valid)


def gather_kernel(n_row, picked_ref, out_ref, part_ref, sem0, send0, sem_a, send_a, sem_b, send_b, sem_c, send_c):
    n_slab = lax.axis_size("slab")
    n_sub = lax.axis_size("sub")
    s = lax.axis_index("slab")
    u = lax.axis_index("sub")
    n_rows = n_slab // n_row
    row, loc = s // n_row, s % n_row

    def copy(src, dst, send, recv, dev):
        return pltpu.make_async_remote_copy(
            src_ref=src, dst_ref=dst, send_sem=send, recv_sem=recv, device_id=dev, device_id_type=MESH
        )

    def to_sub(d):
        q = (u + d) % n_sub
        return copy(picked_ref.at[q], part_ref.at[u], send0.at[q], sem0.at[u], (s, q))

    def from_sub(d):
        q = (u + d) % n_sub
        return copy(picked_ref.at[q], part_ref.at[q], send0.at[q], sem0.at[q], (s, q))

    barrier = pltpu.get_barrier_semaphore()
    for d in range(1, n_sub):
        pl.semaphore_signal(barrier, 1, device_id=(s, (u + d) % n_sub), device_id_type=MESH)

    def greet(d, c):
        dev = (row * n_row + (loc + d) % n_row, u)
        pl.semaphore_signal(barrier, 1, device_id=dev, device_id_type=MESH)
        return c

    lax.fori_loop(1, n_row, greet, 0)
    for d in range(1, n_rows):
        dev = (((row + d) % n_rows) * n_row + loc, u)
        pl.semaphore_signal(barrier, 1, device_id=dev, device_id_type=MESH)
    pl.semaphore_wait(barrier, (n_sub - 1) + (n_row - 1) + (n_rows - 1))

    for d in range(1, n_sub):
        to_sub(d).start()
    total = picked_ref[pl.ds(u, 1), :]
    for d in range(1, n_sub):
        from_sub(d).wait_recv()
        total = total + part_ref[pl.ds((u + d) % n_sub, 1), :]
    half = n_row // 2

    def own(t):
        j = t % n_row
        return out_ref.at[u, t // n_row, j // half, pl.ds(j % half, 1)]

    own(s)[...] = total

    def to_a(d):
        j = (loc + d) % n_row
        return copy(own(s), own(s), send_a.at[j], sem_a.at[loc], (row * n_row + j, u))

    def from_a(d):
        j = (loc + d) % n_row
        src = row * n_row + j
        return copy(own(src), own(src), send_a.at[j], sem_a.at[j], (src, u))

    def start_a(d, c):
        to_a(d).start()
        return c

    def wait_a(d, c):
        from_a(d).wait_recv()
        return c

    lax.fori_loop(1, n_row, start_a, 0)
    lax.fori_loop(1, n_row, wait_a, 0)

    def peer_x(d):
        r = (row + d) % n_rows
        return r, (r * n_row + loc, u)

    def peer_y(d):
        q = (u + d) % n_sub
        return q, (s, q)

    def to_b1(d):
        r, dev = peer_x(d)
        return copy(out_ref.at[u, row, 0], out_ref.at[u, row, 0], send_b.at[0, r], sem_b.at[0, row], dev)

    def from_b1(d):
        r, dev = peer_x(d)
        return copy(out_ref.at[u, r, 0], out_ref.at[u, r, 0], send_b.at[0, r], sem_b.at[0, r], dev)

    def to_c1(d):
        q, dev = peer_y(d)
        return copy(out_ref.at[u, row, 1], out_ref.at[u, row, 1], send_c.at[0, q], sem_c.at[0, u], dev)

    def from_c1(d):
        q, dev = peer_y(d)
        return copy(out_ref.at[q, row, 1], out_ref.at[q, row, 1], send_c.at[0, q], sem_c.at[0, q], dev)

    def to_b2(d):
        r, dev = peer_x(d)
        return copy(out_ref.at[:, row, 1], out_ref.at[:, row, 1], send_b.at[1, r], sem_b.at[1, row], dev)

    def from_b2(d):
        r, dev = peer_x(d)
        return copy(out_ref.at[:, r, 1], out_ref.at[:, r, 1], send_b.at[1, r], sem_b.at[1, r], dev)

    def to_c2(d):
        q, dev = peer_y(d)
        return copy(out_ref.at[u, :, 0], out_ref.at[u, :, 0], send_c.at[1, q], sem_c.at[1, u], dev)

    def from_c2(d):
        q, dev = peer_y(d)
        return copy(out_ref.at[q, :, 0], out_ref.at[q, :, 0], send_c.at[1, q], sem_c.at[1, q], dev)

    for d in range(1, n_rows):
        to_b1(d).start()
    for d in range(1, n_sub):
        to_c1(d).start()
    for d in range(1, n_sub):
        from_c1(d).wait_recv()
    for d in range(1, n_rows):
        to_b2(d).start()
    for d in range(1, n_rows):
        from_b1(d).wait_recv()
    for d in range(1, n_sub):
        to_c2(d).start()
    for d in range(1, n_rows):
        from_b2(d).wait_recv()
    for d in range(1, n_sub):
        from_c2(d).wait_recv()

    for d in range(1, n_sub):
        to_sub(d).wait_send()
    lax.fori_loop(1, n_row, lambda d, c: (to_a(d).wait_send(), c)[1], 0)
    for d in range(1, n_rows):
        to_b1(d).wait_send()
        to_b2(d).wait_send()
    for d in range(1, n_sub):
        to_c1(d).wait_send()
        to_c2(d).wait_send()


def gather_slots(picked, n_slab, n_sub, n_row):
    rows, width = picked.shape
    lanes = rows // n_sub * width
    n_rows = n_slab // n_row
    gathered = pl.pallas_call(
        functools.partial(gather_kernel, n_row),
        out_shape=jax.ShapeDtypeStruct((n_sub, n_rows, 2, n_row // 2, lanes), jnp.float32),
        in_specs=[pl.BlockSpec(memory_space=pltpu.VMEM)],
        out_specs=pl.BlockSpec(memory_space=pltpu.VMEM),
        scratch_shapes=[
            pltpu.VMEM((n_sub, lanes), jnp.float32),
            pltpu.SemaphoreType.DMA((n_sub,)),
            pltpu.SemaphoreType.DMA((n_sub,)),
            pltpu.SemaphoreType.DMA((n_row,)),
            pltpu.SemaphoreType.DMA((n_row,)),
            pltpu.SemaphoreType.DMA((2, n_rows)),
            pltpu.SemaphoreType.DMA((2, n_rows)),
            pltpu.SemaphoreType.DMA((2, n_sub)),
            pltpu.SemaphoreType.DMA((2, n_sub)),
        ],
        compiler_params=pltpu.CompilerParams(has_side_effects=True, collective_id=0),
    )(picked.reshape(n_sub, lanes))
    return gathered.reshape(n_sub, n_slab, lanes)


def per_device(ensemble, obs_value, obs_var, obs_owner, obs_column, home_block, batch_order):
    members = ensemble.shape[2]
    levels_count = ensemble.shape[1]
    cols_dev = ensemble.shape[3]
    slab_count = lax.axis_size("slab")
    sub_count = lax.axis_size("sub")
    slab_index = lax.axis_index("slab")
    sub_index = lax.axis_index("sub")
    capacity = CAP
    cols_slab = cols_dev * sub_count
    nblocks = cols_slab * slab_count // BLK
    span_broad = cols_slab // (4 * BLK)
    span_narrow = max(span_broad // 4, 1)
    decays = (float(span_broad), float(span_narrow))
    assert 2 * span_broad + 1 <= cols_slab // BLK and slab_count >= 3
    owners = obs_owner[:, :, 0]
    obs_home = jnp.mod((owners * cols_slab + obs_column) // BLK + home_block, nblocks)
    onehot = (owners[:, :, None] == jnp.arange(slab_count, dtype=jnp.int32)[None, None, :]).astype(
        jnp.int32
    )
    running = jnp.cumsum(onehot, axis=1) - 1
    slot_rank = jnp.sum(onehot * running, axis=2)
    slot_obs, slot_valid = slot_table(owners, slot_rank, slab_index, capacity)
    slot_column = jnp.take_along_axis(obs_column, slot_obs, axis=1)
    slot_level = slot_obs % levels_count
    holder = slot_column // cols_dev
    local_col = slot_column % cols_dev
    levels = jnp.take(ensemble, slot_level.reshape(-1), axis=1)
    retain = (slot_valid & (holder == sub_index)).reshape(-1)
    chosen = (jnp.arange(cols_dev, dtype=jnp.int32)[None, :] == local_col.reshape(-1, 1)) & retain[:, None]
    picked = jnp.sum(jnp.where(chosen[None, :, None, :], levels, 0.0), axis=3)
    picked = jnp.transpose(picked, (1, 0, 2)).reshape(BATCHES * capacity, BANDS * members)
    n_row = 32 if slab_count % 32 == 0 else slab_count
    gathered = gather_slots(picked, slab_count, sub_count, n_row)
    q_rows = BATCHES * capacity // sub_count
    width = BANDS * members
    row_of = jnp.arange(BATCHES, dtype=jnp.int32)[:, None] * capacity + slot_rank
    lines = jnp.take(
        gathered.reshape(sub_count * slab_count, q_rows * width),
        ((row_of // q_rows) * slab_count + owners).reshape(-1),
        axis=0,
    )
    part = (row_of % q_rows).reshape(-1, 1)
    flat_priors = lines[:, :width]
    for r in range(1, q_rows):
        flat_priors = jnp.where(part == r, lines[:, r * width : (r + 1) * width], flat_priors)
    priors = flat_priors.reshape(BATCHES, -1, width)

    first, second = batch_order[0], batch_order[1]
    y0 = pick(priors, first)
    home0 = pick(obs_home, first)
    home1 = pick(obs_home, second)
    stats0 = obs_statistics(y0, pick(obs_value, first), pick(obs_var, first), members)
    y1 = update_pool(pick(priors, second), home1, *stats0, home0, nblocks, decays)
    stats1 = obs_statistics(y1, pick(obs_value, second), pick(obs_var, second), members)
    which = jnp.arange(BATCHES, dtype=jnp.int32)[:, None, None]
    recorded = jnp.where(which == first, y0[None], y1[None])

    col_blocks = ((slab_index * sub_count + sub_index) * cols_dev + jnp.arange(
        cols_dev, dtype=jnp.int32
    )) // BLK
    near = jnp.mod(slab_index + jnp.arange(-1, 2, dtype=jnp.int32), slab_count)
    matches = (owners[:, None, None, :] == near[None, :, None, None]) & (
        slot_rank[:, None, None, :] == jnp.arange(capacity, dtype=jnp.int32)[None, None, :, None]
    )
    near_obs = jnp.sum(
        jnp.where(matches, jnp.arange(owners.shape[1], dtype=jnp.int32), 0), axis=3
    ).reshape(BATCHES, -1)
    near_valid = jnp.any(matches, axis=3).reshape(BATCHES, -1)
    for batch_id, homes, stats in ((first, home0, stats0), (second, home1, stats1)):
        deviations, spread, increments = stats
        table = jnp.concatenate(
            [
                deviations.reshape(-1, width),
                increments,
                spread[:, None],
                homes[:, None].astype(jnp.float32),
            ],
            axis=1,
        )
        rows = jnp.take(table, pick(near_obs, batch_id), axis=0)
        ensemble = update_state(
            ensemble,
            col_blocks,
            rows[:, :width].reshape(-1, BANDS, members),
            rows[:, width + members],
            rows[:, width : width + members],
            rows[:, width + members + 1].astype(jnp.int32),
            pick(near_valid, batch_id),
            nblocks,
            decays,
        )
    return (ensemble, recorded)


def solution(mesh):
    placed = (P(None, None, None, ("slab", "sub")), P(), P(), P(), P(), P(), P())
    return jax.shard_map(
        per_device,
        mesh=mesh,
        in_specs=placed,
        out_specs=(P(None, None, None, ("slab", "sub")), P()),
        check_vma=False,
    )
```

```python
import functools

import jax
import jax.numpy as jnp
from jax import lax
from jax.experimental import pallas as pl
from jax.experimental.pallas import tpu as pltpu
from jax.sharding import PartitionSpec as P

MESH = pl.DeviceIdType.MESH

BANDS = 2
BLK = 16
BATCHES = 2
CAP = 8


PRODUCT = lax.Precision.HIGH


def gc_weight(first, second, nblocks, length):
    block_gap = jnp.abs(first - second)
    block_gap = jnp.minimum(block_gap, nblocks - block_gap)
    scaled_gap = block_gap.astype(jnp.float32) / length
    near_part = (
        ((-0.25 * scaled_gap + 0.5) * scaled_gap + 0.625) * scaled_gap**3
        - 5.0 / 3.0 * scaled_gap**2
        + 1.0
    )
    floored = jnp.maximum(scaled_gap, 1.0)
    far_part = (
        (
            (((scaled_gap / 12.0 - 0.5) * scaled_gap + 0.625) * scaled_gap + 5.0 / 3.0) * scaled_gap
            - 5.0
        )
        * scaled_gap
        + 4.0
        - 2.0 / (3.0 * floored)
    )
    return jnp.where(scaled_gap <= 1.0, near_part, jnp.where(scaled_gap < 2.0, far_part, 0.0))


def obs_statistics(current, values, variances, members):
    banded = current.reshape(current.shape[0], BANDS, members)
    whole_obs = jnp.sum(banded, axis=1)
    centre = jnp.mean(whole_obs, axis=1, keepdims=True)
    spread = jnp.sum((whole_obs - centre) ** 2, axis=1) / (members - 1) + 1e-06
    post_var = 1.0 / (1.0 / spread + 1.0 / variances)
    post_mean = post_var * (centre[:, 0] / spread + values / variances)
    increments = (post_mean - centre[:, 0])[:, None] + (jnp.sqrt(post_var / spread) - 1.0)[
        :, None
    ] * (whole_obs - centre)
    deviations = banded - jnp.mean(banded, axis=2, keepdims=True)
    return (deviations, spread, increments)


def update_pool(pool, pool_homes, deviations, spread, increments, obs_homes, nblocks, decays):
    members = deviations.shape[2]
    banded = pool.reshape(pool.shape[0], BANDS, members)
    pool_dev = banded - jnp.mean(banded, axis=2, keepdims=True)
    weights = jnp.stack(
        [gc_weight(pool_homes[:, None], obs_homes[None, :], nblocks, decay) for decay in decays]
    ) / ((members - 1) * spread)[None, None, :]
    crossed = jnp.einsum("pbm,kbm->bpk", pool_dev, deviations, precision=PRODUCT)
    change = jnp.einsum("bpk,km->pbm", crossed * weights, increments, precision=PRODUCT)
    return (banded + change).reshape(pool.shape)


def update_state(ensemble, col_blocks, deviations, spread, increments, obs_homes, valid, nblocks, decays):
    members = ensemble.shape[2]
    layer_dev = ensemble - jnp.mean(ensemble, axis=2, keepdims=True)
    weights = jnp.stack(
        [gc_weight(col_blocks[:, None], obs_homes[None, :], nblocks, decay) for decay in decays]
    ) / ((members - 1) * spread)[None, None, :]
    weights = jnp.where(valid[None, None, :], weights, 0.0)
    crossed = jnp.einsum("blmc,kbm->blck", layer_dev, deviations, precision=PRODUCT)
    change = jnp.einsum("blck,km->blmc", crossed * weights[:, None], increments, precision=PRODUCT)
    return ensemble + change


def pick(stacked, which):
    out = stacked[0]
    for i in range(1, stacked.shape[0]):
        out = jnp.where(which == i, stacked[i], out)
    return out


def slot_table(owners, slot_rank, slab_number, capacity):
    obs_count = owners.shape[1]
    matches = (owners == slab_number)[:, None, :] & (
        slot_rank[:, None, :] == jnp.arange(capacity, dtype=jnp.int32)[None, :, None]
    )
    slot_obs = jnp.sum(
        jnp.where(matches, jnp.arange(obs_count, dtype=jnp.int32)[None, None, :], 0), axis=2
    )
    slot_valid = jnp.any(matches, axis=2)
    return (slot_obs, slot_valid)


def gather_kernel(n_row, picked_ref, out_ref, part_ref, sem0, send0, sem_a, send_a, sem_b, send_b, sem_c, send_c):
    n_slab = lax.axis_size("slab")
    n_sub = lax.axis_size("sub")
    s = lax.axis_index("slab")
    u = lax.axis_index("sub")
    n_rows = n_slab // n_row
    row, loc = s // n_row, s % n_row

    def copy(src, dst, send, recv, dev):
        return pltpu.make_async_remote_copy(
            src_ref=src, dst_ref=dst, send_sem=send, recv_sem=recv, device_id=dev, device_id_type=MESH
        )

    def to_sub(d):
        q = (u + d) % n_sub
        return copy(picked_ref.at[q], part_ref.at[u], send0.at[q], sem0.at[u], (s, q))

    def from_sub(d):
        q = (u + d) % n_sub
        return copy(picked_ref.at[q], part_ref.at[q], send0.at[q], sem0.at[q], (s, q))

    barrier = pltpu.get_barrier_semaphore()
    for d in range(1, n_sub):
        pl.semaphore_signal(barrier, 1, device_id=(s, (u + d) % n_sub), device_id_type=MESH)

    def greet(d, c):
        dev = (row * n_row + (loc + d) % n_row, u)
        pl.semaphore_signal(barrier, 1, device_id=dev, device_id_type=MESH)
        return c

    lax.fori_loop(1, n_row, greet, 0)
    for d in range(1, n_rows):
        dev = (((row + d) % n_rows) * n_row + loc, u)
        pl.semaphore_signal(barrier, 1, device_id=dev, device_id_type=MESH)
    pl.semaphore_wait(barrier, (n_sub - 1) + (n_row - 1) + (n_rows - 1))

    for d in range(1, n_sub):
        to_sub(d).start()
    total = picked_ref[pl.ds(u, 1), :]
    for d in range(1, n_sub):
        from_sub(d).wait_recv()
        total = total + part_ref[pl.ds((u + d) % n_sub, 1), :]
    half = n_row // 2

    def own(t):
        j = t % n_row
        return out_ref.at[u, t // n_row, j // half, pl.ds(j % half, 1)]

    own(s)[...] = total

    def to_a(d):
        j = (loc + d) % n_row
        return copy(own(s), own(s), send_a.at[j], sem_a.at[loc], (row * n_row + j, u))

    def from_a(d):
        j = (loc + d) % n_row
        src = row * n_row + j
        return copy(own(src), own(src), send_a.at[j], sem_a.at[j], (src, u))

    def start_a(d, c):
        to_a(d).start()
        return c

    def wait_a(d, c):
        from_a(d).wait_recv()
        return c

    lax.fori_loop(1, n_row, start_a, 0)
    lax.fori_loop(1, n_row, wait_a, 0)

    def peer_x(d):
        r = (row + d) % n_rows
        return r, (r * n_row + loc, u)

    def peer_y(d):
        q = (u + d) % n_sub
        return q, (s, q)

    def to_b1(d):
        r, dev = peer_x(d)
        return copy(out_ref.at[u, row, 0], out_ref.at[u, row, 0], send_b.at[0, r], sem_b.at[0, row], dev)

    def from_b1(d):
        r, dev = peer_x(d)
        return copy(out_ref.at[u, r, 0], out_ref.at[u, r, 0], send_b.at[0, r], sem_b.at[0, r], dev)

    def to_c1(d):
        q, dev = peer_y(d)
        return copy(out_ref.at[u, row, 1], out_ref.at[u, row, 1], send_c.at[0, q], sem_c.at[0, u], dev)

    def from_c1(d):
        q, dev = peer_y(d)
        return copy(out_ref.at[q, row, 1], out_ref.at[q, row, 1], send_c.at[0, q], sem_c.at[0, q], dev)

    def to_b2(d):
        r, dev = peer_x(d)
        return copy(out_ref.at[:, row, 1], out_ref.at[:, row, 1], send_b.at[1, r], sem_b.at[1, row], dev)

    def from_b2(d):
        r, dev = peer_x(d)
        return copy(out_ref.at[:, r, 1], out_ref.at[:, r, 1], send_b.at[1, r], sem_b.at[1, r], dev)

    def to_c2(d):
        q, dev = peer_y(d)
        return copy(out_ref.at[u, :, 0], out_ref.at[u, :, 0], send_c.at[1, q], sem_c.at[1, u], dev)

    def from_c2(d):
        q, dev = peer_y(d)
        return copy(out_ref.at[q, :, 0], out_ref.at[q, :, 0], send_c.at[1, q], sem_c.at[1, q], dev)

    for d in range(1, n_rows):
        to_b1(d).start()
    for d in range(1, n_sub):
        to_c1(d).start()
    for d in range(1, n_sub):
        from_c1(d).wait_recv()
    for d in range(1, n_rows):
        to_b2(d).start()
    for d in range(1, n_rows):
        from_b1(d).wait_recv()
    for d in range(1, n_sub):
        to_c2(d).start()
    for d in range(1, n_rows):
        from_b2(d).wait_recv()
    for d in range(1, n_sub):
        from_c2(d).wait_recv()

    for d in range(1, n_sub):
        to_sub(d).wait_send()
    lax.fori_loop(1, n_row, lambda d, c: (to_a(d).wait_send(), c)[1], 0)
    for d in range(1, n_rows):
        to_b1(d).wait_send()
        to_b2(d).wait_send()
    for d in range(1, n_sub):
        to_c1(d).wait_send()
        to_c2(d).wait_send()


def gather_slots(picked, n_slab, n_sub, n_row):
    rows, width = picked.shape
    lanes = rows // n_sub * width
    n_rows = n_slab // n_row
    gathered = pl.pallas_call(
        functools.partial(gather_kernel, n_row),
        out_shape=jax.ShapeDtypeStruct((n_sub, n_rows, 2, n_row // 2, lanes), jnp.float32),
        in_specs=[pl.BlockSpec(memory_space=pltpu.VMEM)],
        out_specs=pl.BlockSpec(memory_space=pltpu.VMEM),
        scratch_shapes=[
            pltpu.VMEM((n_sub, lanes), jnp.float32),
            pltpu.SemaphoreType.DMA((n_sub,)),
            pltpu.SemaphoreType.DMA((n_sub,)),
            pltpu.SemaphoreType.DMA((n_row,)),
            pltpu.SemaphoreType.DMA((n_row,)),
            pltpu.SemaphoreType.DMA((2, n_rows)),
            pltpu.SemaphoreType.DMA((2, n_rows)),
            pltpu.SemaphoreType.DMA((2, n_sub)),
            pltpu.SemaphoreType.DMA((2, n_sub)),
        ],
        compiler_params=pltpu.CompilerParams(has_side_effects=True, collective_id=0),
    )(picked.reshape(n_sub, lanes))
    return gathered.reshape(n_sub, n_slab, lanes)


def per_device(ensemble, obs_value, obs_var, obs_owner, obs_column, home_block, batch_order):
    members = ensemble.shape[2]
    levels_count = ensemble.shape[1]
    cols_dev = ensemble.shape[3]
    slab_count = lax.axis_size("slab")
    sub_count = lax.axis_size("sub")
    slab_index = lax.axis_index("slab")
    sub_index = lax.axis_index("sub")
    capacity = CAP
    cols_slab = cols_dev * sub_count
    nblocks = cols_slab * slab_count // BLK
    span_broad = cols_slab // (4 * BLK)
    span_narrow = max(span_broad // 4, 1)
    decays = (float(span_broad), float(span_narrow))
    assert 2 * span_broad + 1 <= cols_slab // BLK and slab_count >= 3
    owners = obs_owner[:, :, 0]
    obs_home = jnp.mod((owners * cols_slab + obs_column) // BLK + home_block, nblocks)
    onehot = (owners[:, :, None] == jnp.arange(slab_count, dtype=jnp.int32)[None, None, :]).astype(
        jnp.int32
    )
    running = jnp.cumsum(onehot, axis=1) - 1
    slot_rank = jnp.sum(onehot * running, axis=2)
    slot_obs, slot_valid = slot_table(owners, slot_rank, slab_index, capacity)
    slot_column = jnp.take_along_axis(obs_column, slot_obs, axis=1)
    slot_level = slot_obs % levels_count
    holder = slot_column // cols_dev
    local_col = slot_column % cols_dev
    levels = jnp.take(ensemble, slot_level.reshape(-1), axis=1)
    retain = (slot_valid & (holder == sub_index)).reshape(-1)
    chosen = (jnp.arange(cols_dev, dtype=jnp.int32)[None, :] == local_col.reshape(-1, 1)) & retain[:, None]
    picked = jnp.sum(jnp.where(chosen[None, :, None, :], levels, 0.0), axis=3)
    picked = jnp.transpose(picked, (1, 0, 2)).reshape(BATCHES * capacity, BANDS * members)
    n_row = 32 if slab_count % 32 == 0 else slab_count
    gathered = gather_slots(picked, slab_count, sub_count, n_row)
    q_rows = BATCHES * capacity // sub_count
    width = BANDS * members
    row_of = jnp.arange(BATCHES, dtype=jnp.int32)[:, None] * capacity + slot_rank
    lines = jnp.take(
        gathered.reshape(sub_count * slab_count, q_rows * width),
        ((row_of // q_rows) * slab_count + owners).reshape(-1),
        axis=0,
    )
    part = (row_of % q_rows).reshape(-1, 1)
    flat_priors = lines[:, :width]
    for r in range(1, q_rows):
        flat_priors = jnp.where(part == r, lines[:, r * width : (r + 1) * width], flat_priors)
    priors = flat_priors.reshape(BATCHES, -1, width)

    first, second = batch_order[0], batch_order[1]
    y0 = pick(priors, first)
    home0 = pick(obs_home, first)
    home1 = pick(obs_home, second)
    stats0 = obs_statistics(y0, pick(obs_value, first), pick(obs_var, first), members)
    y1 = update_pool(pick(priors, second), home1, *stats0, home0, nblocks, decays)
    stats1 = obs_statistics(y1, pick(obs_value, second), pick(obs_var, second), members)
    which = jnp.arange(BATCHES, dtype=jnp.int32)[:, None, None]
    recorded = jnp.where(which == first, y0[None], y1[None])

    col_blocks = ((slab_index * sub_count + sub_index) * cols_dev + jnp.arange(
        cols_dev, dtype=jnp.int32
    )) // BLK
    near = jnp.mod(slab_index + jnp.arange(-1, 2, dtype=jnp.int32), slab_count)
    matches = (owners[:, None, None, :] == near[None, :, None, None]) & (
        slot_rank[:, None, None, :] == jnp.arange(capacity, dtype=jnp.int32)[None, None, :, None]
    )
    near_obs = jnp.sum(
        jnp.where(matches, jnp.arange(owners.shape[1], dtype=jnp.int32), 0), axis=3
    ).reshape(BATCHES, -1)
    near_valid = jnp.any(matches, axis=3).reshape(BATCHES, -1)
    for batch_id, homes, stats in ((first, home0, stats0), (second, home1, stats1)):
        deviations, spread, increments = stats
        table = jnp.concatenate(
            [
                deviations.reshape(-1, width),
                increments,
                spread[:, None],
                homes[:, None].astype(jnp.float32),
            ],
            axis=1,
        )
        rows = jnp.take(table, pick(near_obs, batch_id), axis=0)
        ensemble = update_state(
            ensemble,
            col_blocks,
            rows[:, :width].reshape(-1, BANDS, members),
            rows[:, width + members],
            rows[:, width : width + members],
            rows[:, width + members + 1].astype(jnp.int32),
            pick(near_valid, batch_id),
            nblocks,
            decays,
        )
    return (ensemble, recorded)


def solution(mesh):
    placed = (P(None, None, None, ("slab", "sub")), P(), P(), P(), P(), P(), P())
    return jax.shard_map(
        per_device,
        mesh=mesh,
        in_specs=placed,
        out_specs=(P(None, None, None, ("slab", "sub")), P()),
        check_vma=False,
    )
```

```python
import functools

import jax
import jax.numpy as jnp
from jax import lax
from jax.experimental import pallas as pl
from jax.experimental.pallas import tpu as pltpu
from jax.sharding import PartitionSpec as P

MESH = pl.DeviceIdType.MESH

BANDS = 2
BLK = 16
BATCHES = 2
CAP = 8


PRODUCT = lax.Precision.HIGH


def gc_weight(first, second, nblocks, length):
    block_gap = jnp.abs(first - second)
    block_gap = jnp.minimum(block_gap, nblocks - block_gap)
    scaled_gap = block_gap.astype(jnp.float32) / length
    near_part = (
        ((-0.25 * scaled_gap + 0.5) * scaled_gap + 0.625) * scaled_gap**3
        - 5.0 / 3.0 * scaled_gap**2
        + 1.0
    )
    floored = jnp.maximum(scaled_gap, 1.0)
    far_part = (
        (
            (((scaled_gap / 12.0 - 0.5) * scaled_gap + 0.625) * scaled_gap + 5.0 / 3.0) * scaled_gap
            - 5.0
        )
        * scaled_gap
        + 4.0
        - 2.0 / (3.0 * floored)
    )
    return jnp.where(scaled_gap <= 1.0, near_part, jnp.where(scaled_gap < 2.0, far_part, 0.0))


def obs_statistics(current, values, variances, members):
    banded = current.reshape(current.shape[0], BANDS, members)
    whole_obs = jnp.sum(banded, axis=1)
    centre = jnp.mean(whole_obs, axis=1, keepdims=True)
    spread = jnp.sum((whole_obs - centre) ** 2, axis=1) / (members - 1) + 1e-06
    post_var = 1.0 / (1.0 / spread + 1.0 / variances)
    post_mean = post_var * (centre[:, 0] / spread + values / variances)
    increments = (post_mean - centre[:, 0])[:, None] + (jnp.sqrt(post_var / spread) - 1.0)[
        :, None
    ] * (whole_obs - centre)
    deviations = banded - jnp.mean(banded, axis=2, keepdims=True)
    return (deviations, spread, increments)


def update_pool(pool, pool_homes, deviations, spread, increments, obs_homes, nblocks, decays):
    members = deviations.shape[2]
    banded = pool.reshape(pool.shape[0], BANDS, members)
    pool_dev = banded - jnp.mean(banded, axis=2, keepdims=True)
    weights = jnp.stack(
        [gc_weight(pool_homes[:, None], obs_homes[None, :], nblocks, decay) for decay in decays]
    ) / ((members - 1) * spread)[None, None, :]
    crossed = jnp.einsum("pbm,kbm->bpk", pool_dev, deviations, precision=PRODUCT)
    change = jnp.einsum("bpk,km->pbm", crossed * weights, increments, precision=PRODUCT)
    return (banded + change).reshape(pool.shape)


def update_state(ensemble, col_blocks, deviations, spread, increments, obs_homes, valid, nblocks, decays):
    members = ensemble.shape[2]
    layer_dev = ensemble - jnp.mean(ensemble, axis=2, keepdims=True)
    weights = jnp.stack(
        [gc_weight(col_blocks[:, None], obs_homes[None, :], nblocks, decay) for decay in decays]
    ) / ((members - 1) * spread)[None, None, :]
    weights = jnp.where(valid[None, None, :], weights, 0.0)
    crossed = jnp.einsum("blmc,kbm->blck", layer_dev, deviations, precision=PRODUCT)
    change = jnp.einsum("blck,km->blmc", crossed * weights[:, None], increments, precision=PRODUCT)
    return ensemble + change


def pick(stacked, which):
    out = stacked[0]
    for i in range(1, stacked.shape[0]):
        out = jnp.where(which == i, stacked[i], out)
    return out


def slot_table(owners, slot_rank, slab_number, capacity):
    obs_count = owners.shape[1]
    matches = (owners == slab_number)[:, None, :] & (
        slot_rank[:, None, :] == jnp.arange(capacity, dtype=jnp.int32)[None, :, None]
    )
    slot_obs = jnp.sum(
        jnp.where(matches, jnp.arange(obs_count, dtype=jnp.int32)[None, None, :], 0), axis=2
    )
    slot_valid = jnp.any(matches, axis=2)
    return (slot_obs, slot_valid)


def gather_kernel(n_row, picked_ref, out_ref, part_ref, sem0, send0, sem_a, send_a, sem_b, send_b, sem_c, send_c):
    n_slab = lax.axis_size("slab")
    n_sub = lax.axis_size("sub")
    s = lax.axis_index("slab")
    u = lax.axis_index("sub")
    n_rows = n_slab // n_row
    row, loc = s // n_row, s % n_row

    def copy(src, dst, send, recv, dev):
        return pltpu.make_async_remote_copy(
            src_ref=src, dst_ref=dst, send_sem=send, recv_sem=recv, device_id=dev, device_id_type=MESH
        )

    def to_sub(d):
        q = (u + d) % n_sub
        return copy(picked_ref.at[q], part_ref.at[u], send0.at[q], sem0.at[u], (s, q))

    def from_sub(d):
        q = (u + d) % n_sub
        return copy(picked_ref.at[q], part_ref.at[q], send0.at[q], sem0.at[q], (s, q))

    barrier = pltpu.get_barrier_semaphore()
    for d in range(1, n_sub):
        pl.semaphore_signal(barrier, 1, device_id=(s, (u + d) % n_sub), device_id_type=MESH)

    def far(i):
        return n_row // 2 + (2 * (i % 2) - 1) * ((i + 1) // 2)

    def greet(i, c):
        dev = (row * n_row + (loc + far(i)) % n_row, u)
        pl.semaphore_signal(barrier, 1, device_id=dev, device_id_type=MESH)
        return c

    lax.fori_loop(0, n_row - 1, greet, 0)
    for d in range(1, n_rows):
        dev = (((row + d) % n_rows) * n_row + loc, u)
        pl.semaphore_signal(barrier, 1, device_id=dev, device_id_type=MESH)
    pl.semaphore_wait(barrier, (n_sub - 1) + (n_row - 1) + (n_rows - 1))

    for d in range(1, n_sub):
        to_sub(d).start()
    total = picked_ref[pl.ds(u, 1), :]
    for d in range(1, n_sub):
        from_sub(d).wait_recv()
        total = total + part_ref[pl.ds((u + d) % n_sub, 1), :]
    half = n_row // 2

    def own(t):
        j = t % n_row
        return out_ref.at[u, t // n_row, j // half, pl.ds(j % half, 1)]

    own(s)[...] = total

    def to_a(d):
        j = (loc + d) % n_row
        return copy(own(s), own(s), send_a.at[j], sem_a.at[loc], (row * n_row + j, u))

    def from_a(d):
        j = (loc + d) % n_row
        src = row * n_row + j
        return copy(own(src), own(src), send_a.at[j], sem_a.at[j], (src, u))

    def start_a(i, c):
        to_a(far(i)).start()
        return c

    def wait_half(h):
        def body(j, c):
            @pl.when(h * half + j != loc)
            def _():
                from_a((h * half + j - loc + n_row) % n_row).wait_recv()

            return c

        lax.fori_loop(0, half, body, 0)

    lax.fori_loop(0, n_row - 1, start_a, 0)
    mine = loc // half

    def peer_x(d):
        r = (row + d) % n_rows
        return r, (r * n_row + loc, u)

    def peer_y(d):
        q = (u + d) % n_sub
        return q, (s, q)

    def to_b1(d):
        r, dev = peer_x(d)
        return copy(out_ref.at[u, row, 0], out_ref.at[u, row, 0], send_b.at[0, r], sem_b.at[0, row], dev)

    def from_b1(d):
        r, dev = peer_x(d)
        return copy(out_ref.at[u, r, 0], out_ref.at[u, r, 0], send_b.at[0, r], sem_b.at[0, r], dev)

    def to_c1(d):
        q, dev = peer_y(d)
        return copy(out_ref.at[u, row, 1], out_ref.at[u, row, 1], send_c.at[0, q], sem_c.at[0, u], dev)

    def from_c1(d):
        q, dev = peer_y(d)
        return copy(out_ref.at[q, row, 1], out_ref.at[q, row, 1], send_c.at[0, q], sem_c.at[0, q], dev)

    def to_b2(d):
        r, dev = peer_x(d)
        return copy(out_ref.at[:, row, 1], out_ref.at[:, row, 1], send_b.at[1, r], sem_b.at[1, row], dev)

    def from_b2(d):
        r, dev = peer_x(d)
        return copy(out_ref.at[:, r, 1], out_ref.at[:, r, 1], send_b.at[1, r], sem_b.at[1, r], dev)

    def to_c2(d):
        q, dev = peer_y(d)
        return copy(out_ref.at[u, :, 0], out_ref.at[u, :, 0], send_c.at[1, q], sem_c.at[1, u], dev)

    def from_c2(d):
        q, dev = peer_y(d)
        return copy(out_ref.at[q, :, 0], out_ref.at[q, :, 0], send_c.at[1, q], sem_c.at[1, q], dev)

    def start_b1():
        for d in range(1, n_rows):
            to_b1(d).start()

    def start_c1():
        for d in range(1, n_sub):
            to_c1(d).start()

    wait_half(mine)
    pl.when(mine == 0)(start_b1)
    pl.when(mine == 1)(start_c1)
    wait_half(1 - mine)
    pl.when(mine == 0)(start_c1)
    pl.when(mine == 1)(start_b1)
    for d in range(1, n_sub):
        from_c1(d).wait_recv()
    for d in range(1, n_rows):
        to_b2(d).start()
    for d in range(1, n_rows):
        from_b1(d).wait_recv()
    for d in range(1, n_sub):
        to_c2(d).start()
    for d in range(1, n_rows):
        from_b2(d).wait_recv()
    for d in range(1, n_sub):
        from_c2(d).wait_recv()

    for d in range(1, n_sub):
        to_sub(d).wait_send()
    lax.fori_loop(1, n_row, lambda d, c: (to_a(d).wait_send(), c)[1], 0)
    for d in range(1, n_rows):
        to_b1(d).wait_send()
        to_b2(d).wait_send()
    for d in range(1, n_sub):
        to_c1(d).wait_send()
        to_c2(d).wait_send()


def gather_slots(picked, n_slab, n_sub, n_row):
    rows, width = picked.shape
    lanes = rows // n_sub * width
    n_rows = n_slab // n_row
    gathered = pl.pallas_call(
        functools.partial(gather_kernel, n_row),
        out_shape=jax.ShapeDtypeStruct((n_sub, n_rows, 2, n_row // 2, lanes), jnp.float32),
        in_specs=[pl.BlockSpec(memory_space=pltpu.VMEM)],
        out_specs=pl.BlockSpec(memory_space=pltpu.VMEM),
        scratch_shapes=[
            pltpu.VMEM((n_sub, lanes), jnp.float32),
            pltpu.SemaphoreType.DMA((n_sub,)),
            pltpu.SemaphoreType.DMA((n_sub,)),
            pltpu.SemaphoreType.DMA((n_row,)),
            pltpu.SemaphoreType.DMA((n_row,)),
            pltpu.SemaphoreType.DMA((2, n_rows)),
            pltpu.SemaphoreType.DMA((2, n_rows)),
            pltpu.SemaphoreType.DMA((2, n_sub)),
            pltpu.SemaphoreType.DMA((2, n_sub)),
        ],
        compiler_params=pltpu.CompilerParams(has_side_effects=True, collective_id=0),
    )(picked.reshape(n_sub, lanes))
    return gathered.reshape(n_sub, n_slab, lanes)


def per_device(ensemble, obs_value, obs_var, obs_owner, obs_column, home_block, batch_order):
    members = ensemble.shape[2]
    levels_count = ensemble.shape[1]
    cols_dev = ensemble.shape[3]
    slab_count = lax.axis_size("slab")
    sub_count = lax.axis_size("sub")
    slab_index = lax.axis_index("slab")
    sub_index = lax.axis_index("sub")
    capacity = CAP
    cols_slab = cols_dev * sub_count
    nblocks = cols_slab * slab_count // BLK
    span_broad = cols_slab // (4 * BLK)
    span_narrow = max(span_broad // 4, 1)
    decays = (float(span_broad), float(span_narrow))
    assert 2 * span_broad + 1 <= cols_slab // BLK and slab_count >= 3
    owners = obs_owner[:, :, 0]
    obs_home = jnp.mod((owners * cols_slab + obs_column) // BLK + home_block, nblocks)
    onehot = (owners[:, :, None] == jnp.arange(slab_count, dtype=jnp.int32)[None, None, :]).astype(
        jnp.int32
    )
    running = jnp.cumsum(onehot, axis=1) - 1
    slot_rank = jnp.sum(onehot * running, axis=2)
    slot_obs, slot_valid = slot_table(owners, slot_rank, slab_index, capacity)
    slot_column = jnp.take_along_axis(obs_column, slot_obs, axis=1)
    slot_level = slot_obs % levels_count
    holder = slot_column // cols_dev
    local_col = slot_column % cols_dev
    levels = jnp.take(ensemble, slot_level.reshape(-1), axis=1)
    retain = (slot_valid & (holder == sub_index)).reshape(-1)
    chosen = (jnp.arange(cols_dev, dtype=jnp.int32)[None, :] == local_col.reshape(-1, 1)) & retain[:, None]
    picked = jnp.sum(jnp.where(chosen[None, :, None, :], levels, 0.0), axis=3)
    picked = jnp.transpose(picked, (1, 0, 2)).reshape(BATCHES * capacity, BANDS * members)
    n_row = 32 if slab_count % 32 == 0 else slab_count
    gathered = gather_slots(picked, slab_count, sub_count, n_row)
    q_rows = BATCHES * capacity // sub_count
    width = BANDS * members
    row_of = jnp.arange(BATCHES, dtype=jnp.int32)[:, None] * capacity + slot_rank
    lines = jnp.take(
        gathered.reshape(sub_count * slab_count, q_rows * width),
        ((row_of // q_rows) * slab_count + owners).reshape(-1),
        axis=0,
    )
    part = (row_of % q_rows).reshape(-1, 1)
    flat_priors = lines[:, :width]
    for r in range(1, q_rows):
        flat_priors = jnp.where(part == r, lines[:, r * width : (r + 1) * width], flat_priors)
    priors = flat_priors.reshape(BATCHES, -1, width)

    first, second = batch_order[0], batch_order[1]
    y0 = pick(priors, first)
    home0 = pick(obs_home, first)
    home1 = pick(obs_home, second)
    stats0 = obs_statistics(y0, pick(obs_value, first), pick(obs_var, first), members)
    y1 = update_pool(pick(priors, second), home1, *stats0, home0, nblocks, decays)
    stats1 = obs_statistics(y1, pick(obs_value, second), pick(obs_var, second), members)
    which = jnp.arange(BATCHES, dtype=jnp.int32)[:, None, None]
    recorded = jnp.where(which == first, y0[None], y1[None])

    col_blocks = ((slab_index * sub_count + sub_index) * cols_dev + jnp.arange(
        cols_dev, dtype=jnp.int32
    )) // BLK
    near = jnp.mod(slab_index + jnp.arange(-1, 2, dtype=jnp.int32), slab_count)
    matches = (owners[:, None, None, :] == near[None, :, None, None]) & (
        slot_rank[:, None, None, :] == jnp.arange(capacity, dtype=jnp.int32)[None, None, :, None]
    )
    near_obs = jnp.sum(
        jnp.where(matches, jnp.arange(owners.shape[1], dtype=jnp.int32), 0), axis=3
    ).reshape(BATCHES, -1)
    near_valid = jnp.any(matches, axis=3).reshape(BATCHES, -1)
    for batch_id, homes, stats in ((first, home0, stats0), (second, home1, stats1)):
        deviations, spread, increments = stats
        table = jnp.concatenate(
            [
                deviations.reshape(-1, width),
                increments,
                spread[:, None],
                homes[:, None].astype(jnp.float32),
            ],
            axis=1,
        )
        rows = jnp.take(table, pick(near_obs, batch_id), axis=0)
        ensemble = update_state(
            ensemble,
            col_blocks,
            rows[:, :width].reshape(-1, BANDS, members),
            rows[:, width + members],
            rows[:, width : width + members],
            rows[:, width + members + 1].astype(jnp.int32),
            pick(near_valid, batch_id),
            nblocks,
            decays,
        )
    return (ensemble, recorded)


def solution(mesh):
    placed = (P(None, None, None, ("slab", "sub")), P(), P(), P(), P(), P(), P())
    return jax.shard_map(
        per_device,
        mesh=mesh,
        in_specs=placed,
        out_specs=(P(None, None, None, ("slab", "sub")), P()),
        check_vma=False,
    )
```

```python
import functools

import jax
import jax.numpy as jnp
from jax import lax
from jax.experimental import pallas as pl
from jax.experimental.pallas import tpu as pltpu
from jax.sharding import PartitionSpec as P

MESH = pl.DeviceIdType.MESH

BANDS = 2
BLK = 16
BATCHES = 2
CAP = 8


PRODUCT = lax.Precision.HIGH


def gc_weight(first, second, nblocks, length):
    block_gap = jnp.abs(first - second)
    block_gap = jnp.minimum(block_gap, nblocks - block_gap)
    scaled_gap = block_gap.astype(jnp.float32) / length
    near_part = (
        ((-0.25 * scaled_gap + 0.5) * scaled_gap + 0.625) * scaled_gap**3
        - 5.0 / 3.0 * scaled_gap**2
        + 1.0
    )
    floored = jnp.maximum(scaled_gap, 1.0)
    far_part = (
        (
            (((scaled_gap / 12.0 - 0.5) * scaled_gap + 0.625) * scaled_gap + 5.0 / 3.0) * scaled_gap
            - 5.0
        )
        * scaled_gap
        + 4.0
        - 2.0 / (3.0 * floored)
    )
    return jnp.where(scaled_gap <= 1.0, near_part, jnp.where(scaled_gap < 2.0, far_part, 0.0))


def obs_statistics(current, values, variances, members):
    banded = current.reshape(current.shape[0], BANDS, members)
    whole_obs = jnp.sum(banded, axis=1)
    centre = jnp.mean(whole_obs, axis=1, keepdims=True)
    spread = jnp.sum((whole_obs - centre) ** 2, axis=1) / (members - 1) + 1e-06
    post_var = 1.0 / (1.0 / spread + 1.0 / variances)
    post_mean = post_var * (centre[:, 0] / spread + values / variances)
    increments = (post_mean - centre[:, 0])[:, None] + (jnp.sqrt(post_var / spread) - 1.0)[
        :, None
    ] * (whole_obs - centre)
    deviations = banded - jnp.mean(banded, axis=2, keepdims=True)
    return (deviations, spread, increments)


def update_pool(pool, pool_homes, deviations, spread, increments, obs_homes, nblocks, decays):
    members = deviations.shape[2]
    banded = pool.reshape(pool.shape[0], BANDS, members)
    pool_dev = banded - jnp.mean(banded, axis=2, keepdims=True)
    weights = jnp.stack(
        [gc_weight(pool_homes[:, None], obs_homes[None, :], nblocks, decay) for decay in decays]
    ) / ((members - 1) * spread)[None, None, :]
    crossed = jnp.einsum("pbm,kbm->bpk", pool_dev, deviations, precision=PRODUCT)
    change = jnp.einsum("bpk,km->pbm", crossed * weights, increments, precision=PRODUCT)
    return (banded + change).reshape(pool.shape)


def update_state(ensemble, col_blocks, deviations, spread, increments, obs_homes, valid, nblocks, decays):
    members = ensemble.shape[2]
    layer_dev = ensemble - jnp.mean(ensemble, axis=2, keepdims=True)
    weights = jnp.stack(
        [gc_weight(col_blocks[:, None], obs_homes[None, :], nblocks, decay) for decay in decays]
    ) / ((members - 1) * spread)[None, None, :]
    weights = jnp.where(valid[None, None, :], weights, 0.0)
    crossed = jnp.einsum("blmc,kbm->blck", layer_dev, deviations, precision=PRODUCT)
    change = jnp.einsum("blck,km->blmc", crossed * weights[:, None], increments, precision=PRODUCT)
    return ensemble + change


def pick(stacked, which):
    out = stacked[0]
    for i in range(1, stacked.shape[0]):
        out = jnp.where(which == i, stacked[i], out)
    return out


def slot_table(owners, slot_rank, slab_number, capacity):
    obs_count = owners.shape[1]
    matches = (owners == slab_number)[:, None, :] & (
        slot_rank[:, None, :] == jnp.arange(capacity, dtype=jnp.int32)[None, :, None]
    )
    slot_obs = jnp.sum(
        jnp.where(matches, jnp.arange(obs_count, dtype=jnp.int32)[None, None, :], 0), axis=2
    )
    slot_valid = jnp.any(matches, axis=2)
    return (slot_obs, slot_valid)


def gather_kernel(n_row, picked_ref, out_ref, part_ref, sem0, send0, sem_a, send_a, sem_b, send_b, sem_c, send_c):
    n_slab = lax.axis_size("slab")
    n_sub = lax.axis_size("sub")
    s = lax.axis_index("slab")
    u = lax.axis_index("sub")
    n_rows = n_slab // n_row
    row, loc = s // n_row, s % n_row

    def copy(src, dst, send, recv, dev):
        return pltpu.make_async_remote_copy(
            src_ref=src, dst_ref=dst, send_sem=send, recv_sem=recv, device_id=dev, device_id_type=MESH
        )

    def to_sub(d):
        q = (u + d) % n_sub
        return copy(picked_ref.at[q], part_ref.at[u], send0.at[q], sem0.at[u], (s, q))

    def from_sub(d):
        q = (u + d) % n_sub
        return copy(picked_ref.at[q], part_ref.at[q], send0.at[q], sem0.at[q], (s, q))

    barrier = pltpu.get_barrier_semaphore()
    for d in range(1, n_sub):
        pl.semaphore_signal(barrier, 1, device_id=(s, (u + d) % n_sub), device_id_type=MESH)

    def greet(d, c):
        dev = (row * n_row + (loc + d) % n_row, u)
        pl.semaphore_signal(barrier, 1, device_id=dev, device_id_type=MESH)
        return c

    lax.fori_loop(1, n_row, greet, 0)
    for d in range(1, n_rows):
        dev = (((row + d) % n_rows) * n_row + loc, u)
        pl.semaphore_signal(barrier, 1, device_id=dev, device_id_type=MESH)
    pl.semaphore_wait(barrier, (n_sub - 1) + (n_row - 1) + (n_rows - 1))

    for d in range(1, n_sub):
        to_sub(d).start()
    total = picked_ref[pl.ds(u, 1), :]
    for d in range(1, n_sub):
        from_sub(d).wait_recv()
        total = total + part_ref[pl.ds((u + d) % n_sub, 1), :]
    half = n_row // 2

    def own(t):
        j = t % n_row
        return out_ref.at[u, t // n_row, j // half, pl.ds(j % half, 1)]

    own(s)[...] = total

    def to_a(d):
        j = (loc + d) % n_row
        return copy(own(s), own(s), send_a.at[j], sem_a.at[loc], (row * n_row + j, u))

    def from_a(d):
        j = (loc + d) % n_row
        src = row * n_row + j
        return copy(own(src), own(src), send_a.at[j], sem_a.at[j], (src, u))

    def start_a(d, c):
        to_a(d).start()
        return c

    def wait_a(d, c):
        from_a(d).wait_recv()
        return c

    lax.fori_loop(1, n_row, start_a, 0)
    lax.fori_loop(1, n_row, wait_a, 0)

    def peer_x(d):
        r = (row + d) % n_rows
        return r, (r * n_row + loc, u)

    def peer_y(d):
        q = (u + d) % n_sub
        return q, (s, q)

    def to_b1(d):
        r, dev = peer_x(d)
        return copy(out_ref.at[u, row, 0], out_ref.at[u, row, 0], send_b.at[0, r], sem_b.at[0, row], dev)

    def from_b1(d):
        r, dev = peer_x(d)
        return copy(out_ref.at[u, r, 0], out_ref.at[u, r, 0], send_b.at[0, r], sem_b.at[0, r], dev)

    def to_c1(d):
        q, dev = peer_y(d)
        return copy(out_ref.at[u, row, 1], out_ref.at[u, row, 1], send_c.at[0, q], sem_c.at[0, u], dev)

    def from_c1(d):
        q, dev = peer_y(d)
        return copy(out_ref.at[q, row, 1], out_ref.at[q, row, 1], send_c.at[0, q], sem_c.at[0, q], dev)

    def to_b2(d):
        r, dev = peer_x(d)
        return copy(out_ref.at[:, row, 1], out_ref.at[:, row, 1], send_b.at[1, r], sem_b.at[1, row], dev)

    def from_b2(d):
        r, dev = peer_x(d)
        return copy(out_ref.at[:, r, 1], out_ref.at[:, r, 1], send_b.at[1, r], sem_b.at[1, r], dev)

    def to_c2(d):
        q, dev = peer_y(d)
        return copy(out_ref.at[u, :, 0], out_ref.at[u, :, 0], send_c.at[1, q], sem_c.at[1, u], dev)

    def from_c2(d):
        q, dev = peer_y(d)
        return copy(out_ref.at[q, :, 0], out_ref.at[q, :, 0], send_c.at[1, q], sem_c.at[1, q], dev)

    for d in range(1, n_rows):
        to_b1(d).start()
    for d in range(1, n_sub):
        to_c1(d).start()
    for d in range(1, n_sub):
        from_c1(d).wait_recv()
    for d in range(1, n_rows):
        to_b2(d).start()
    for d in range(1, n_rows):
        from_b1(d).wait_recv()
    for d in range(1, n_sub):
        to_c2(d).start()
    for d in range(1, n_rows):
        from_b2(d).wait_recv()
    for d in range(1, n_sub):
        from_c2(d).wait_recv()

    for d in range(1, n_sub):
        to_sub(d).wait_send()
    lax.fori_loop(1, n_row, lambda d, c: (to_a(d).wait_send(), c)[1], 0)
    for d in range(1, n_rows):
        to_b1(d).wait_send()
        to_b2(d).wait_send()
    for d in range(1, n_sub):
        to_c1(d).wait_send()
        to_c2(d).wait_send()


def gather_slots(picked, n_slab, n_sub, n_row):
    rows, width = picked.shape
    lanes = rows // n_sub * width
    n_rows = n_slab // n_row
    gathered = pl.pallas_call(
        functools.partial(gather_kernel, n_row),
        out_shape=jax.ShapeDtypeStruct((n_sub, n_rows, 2, n_row // 2, lanes), jnp.float32),
        in_specs=[pl.BlockSpec(memory_space=pltpu.VMEM)],
        out_specs=pl.BlockSpec(memory_space=pltpu.VMEM),
        scratch_shapes=[
            pltpu.VMEM((n_sub, lanes), jnp.float32),
            pltpu.SemaphoreType.DMA((n_sub,)),
            pltpu.SemaphoreType.DMA((n_sub,)),
            pltpu.SemaphoreType.DMA((n_row,)),
            pltpu.SemaphoreType.DMA((n_row,)),
            pltpu.SemaphoreType.DMA((2, n_rows)),
            pltpu.SemaphoreType.DMA((2, n_rows)),
            pltpu.SemaphoreType.DMA((2, n_sub)),
            pltpu.SemaphoreType.DMA((2, n_sub)),
        ],
        compiler_params=pltpu.CompilerParams(has_side_effects=True, collective_id=0),
    )(picked.reshape(n_sub, lanes))
    return gathered.reshape(n_sub, n_slab, lanes)


def per_device(ensemble, obs_value, obs_var, obs_owner, obs_column, home_block, batch_order):
    members = ensemble.shape[2]
    levels_count = ensemble.shape[1]
    cols_dev = ensemble.shape[3]
    slab_count = lax.axis_size("slab")
    sub_count = lax.axis_size("sub")
    slab_index = lax.axis_index("slab")
    sub_index = lax.axis_index("sub")
    capacity = CAP
    cols_slab = cols_dev * sub_count
    nblocks = cols_slab * slab_count // BLK
    span_broad = cols_slab // (4 * BLK)
    span_narrow = max(span_broad // 4, 1)
    decays = (float(span_broad), float(span_narrow))
    assert 2 * span_broad + 1 <= cols_slab // BLK and slab_count >= 3
    owners = obs_owner[:, :, 0]
    obs_home = jnp.mod((owners * cols_slab + obs_column) // BLK + home_block, nblocks)
    order = jnp.arange(owners.shape[1], dtype=jnp.int32)
    earlier = (owners[:, None, :] == owners[:, :, None]) & (order[None, :] < order[:, None])[None]
    slot_rank = jnp.sum(earlier.astype(jnp.int32), axis=2)
    slot_obs, slot_valid = slot_table(owners, slot_rank, slab_index, capacity)
    slot_column = jnp.take_along_axis(obs_column, slot_obs, axis=1)
    slot_level = slot_obs % levels_count
    holder = slot_column // cols_dev
    local_col = slot_column % cols_dev
    levels = jnp.take(ensemble, slot_level.reshape(-1), axis=1)
    retain = (slot_valid & (holder == sub_index)).reshape(-1)
    chosen = (jnp.arange(cols_dev, dtype=jnp.int32)[None, :] == local_col.reshape(-1, 1)) & retain[:, None]
    picked = jnp.sum(jnp.where(chosen[None, :, None, :], levels, 0.0), axis=3)
    picked = jnp.transpose(picked, (1, 0, 2)).reshape(BATCHES * capacity, BANDS * members)
    n_row = 32 if slab_count % 32 == 0 else slab_count
    gathered = gather_slots(picked, slab_count, sub_count, n_row)
    q_rows = BATCHES * capacity // sub_count
    width = BANDS * members
    row_of = jnp.arange(BATCHES, dtype=jnp.int32)[:, None] * capacity + slot_rank
    lines = jnp.take(
        gathered.reshape(sub_count * slab_count, q_rows * width),
        ((row_of // q_rows) * slab_count + owners).reshape(-1),
        axis=0,
    )
    part = (row_of % q_rows).reshape(-1, 1)
    flat_priors = lines[:, :width]
    for r in range(1, q_rows):
        flat_priors = jnp.where(part == r, lines[:, r * width : (r + 1) * width], flat_priors)
    priors = flat_priors.reshape(BATCHES, -1, width)

    first, second = batch_order[0], batch_order[1]
    y0 = pick(priors, first)
    home0 = pick(obs_home, first)
    home1 = pick(obs_home, second)
    stats0 = obs_statistics(y0, pick(obs_value, first), pick(obs_var, first), members)
    y1 = update_pool(pick(priors, second), home1, *stats0, home0, nblocks, decays)
    stats1 = obs_statistics(y1, pick(obs_value, second), pick(obs_var, second), members)
    which = jnp.arange(BATCHES, dtype=jnp.int32)[:, None, None]
    recorded = jnp.where(which == first, y0[None], y1[None])

    col_blocks = ((slab_index * sub_count + sub_index) * cols_dev + jnp.arange(
        cols_dev, dtype=jnp.int32
    )) // BLK
    near = jnp.mod(slab_index + jnp.arange(-1, 2, dtype=jnp.int32), slab_count)
    matches = (owners[:, None, None, :] == near[None, :, None, None]) & (
        slot_rank[:, None, None, :] == jnp.arange(capacity, dtype=jnp.int32)[None, None, :, None]
    )
    near_obs = jnp.sum(
        jnp.where(matches, jnp.arange(owners.shape[1], dtype=jnp.int32), 0), axis=3
    ).reshape(BATCHES, -1)
    near_valid = jnp.any(matches, axis=3).reshape(BATCHES, -1)
    for batch_id, homes, stats in ((first, home0, stats0), (second, home1, stats1)):
        deviations, spread, increments = stats
        table = jnp.concatenate(
            [
                deviations.reshape(-1, width),
                increments,
                spread[:, None],
                homes[:, None].astype(jnp.float32),
            ],
            axis=1,
        )
        rows = jnp.take(table, pick(near_obs, batch_id), axis=0)
        ensemble = update_state(
            ensemble,
            col_blocks,
            rows[:, :width].reshape(-1, BANDS, members),
            rows[:, width + members],
            rows[:, width : width + members],
            rows[:, width + members + 1].astype(jnp.int32),
            pick(near_valid, batch_id),
            nblocks,
            decays,
        )
    return (ensemble, recorded)


def solution(mesh):
    placed = (P(None, None, None, ("slab", "sub")), P(), P(), P(), P(), P(), P())
    return jax.shard_map(
        per_device,
        mesh=mesh,
        in_specs=placed,
        out_specs=(P(None, None, None, ("slab", "sub")), P()),
        check_vma=False,
    )
```

```python
import functools

import jax
import jax.numpy as jnp
from jax import lax
from jax.experimental import pallas as pl
from jax.experimental.pallas import tpu as pltpu
from jax.sharding import PartitionSpec as P

MESH = pl.DeviceIdType.MESH

BANDS = 2
BLK = 16
BATCHES = 2
CAP = 8


PRODUCT = lax.Precision.HIGH


def gc_weight(first, second, nblocks, length):
    block_gap = jnp.abs(first - second)
    block_gap = jnp.minimum(block_gap, nblocks - block_gap)
    scaled_gap = block_gap.astype(jnp.float32) / length
    near_part = (
        ((-0.25 * scaled_gap + 0.5) * scaled_gap + 0.625) * scaled_gap**3
        - 5.0 / 3.0 * scaled_gap**2
        + 1.0
    )
    floored = jnp.maximum(scaled_gap, 1.0)
    far_part = (
        (
            (((scaled_gap / 12.0 - 0.5) * scaled_gap + 0.625) * scaled_gap + 5.0 / 3.0) * scaled_gap
            - 5.0
        )
        * scaled_gap
        + 4.0
        - 2.0 / (3.0 * floored)
    )
    return jnp.where(scaled_gap <= 1.0, near_part, jnp.where(scaled_gap < 2.0, far_part, 0.0))


def obs_statistics(current, values, variances, members):
    banded = current.reshape(current.shape[0], BANDS, members)
    whole_obs = jnp.sum(banded, axis=1)
    centre = jnp.mean(whole_obs, axis=1, keepdims=True)
    spread = jnp.sum((whole_obs - centre) ** 2, axis=1) / (members - 1) + 1e-06
    post_var = 1.0 / (1.0 / spread + 1.0 / variances)
    post_mean = post_var * (centre[:, 0] / spread + values / variances)
    increments = (post_mean - centre[:, 0])[:, None] + (jnp.sqrt(post_var / spread) - 1.0)[
        :, None
    ] * (whole_obs - centre)
    deviations = banded - jnp.mean(banded, axis=2, keepdims=True)
    return (deviations, spread, increments)


def update_pool(pool, pool_homes, deviations, spread, increments, obs_homes, nblocks, decays):
    members = deviations.shape[2]
    banded = pool.reshape(pool.shape[0], BANDS, members)
    pool_dev = banded - jnp.mean(banded, axis=2, keepdims=True)
    weights = jnp.stack(
        [gc_weight(pool_homes[:, None], obs_homes[None, :], nblocks, decay) for decay in decays]
    ) / ((members - 1) * spread)[None, None, :]
    crossed = jnp.einsum("pbm,kbm->bpk", pool_dev, deviations, precision=PRODUCT)
    change = jnp.einsum("bpk,km->pbm", crossed * weights, increments, precision=PRODUCT)
    return (banded + change).reshape(pool.shape)


def update_state(ensemble, col_blocks, deviations, spread, increments, obs_homes, valid, nblocks, decays):
    members = ensemble.shape[2]
    layer_dev = ensemble - jnp.mean(ensemble, axis=2, keepdims=True)
    weights = jnp.stack(
        [gc_weight(col_blocks[:, None], obs_homes[None, :], nblocks, decay) for decay in decays]
    ) / ((members - 1) * spread)[None, None, :]
    weights = jnp.where(valid[None, None, :], weights, 0.0)
    crossed = jnp.einsum("blmc,kbm->blck", layer_dev, deviations, precision=PRODUCT)
    change = jnp.einsum("blck,km->blmc", crossed * weights[:, None], increments, precision=PRODUCT)
    return ensemble + change


def pick(stacked, chosen):
    weights = chosen.astype(stacked.dtype).reshape((-1,) + (1,) * (stacked.ndim - 1))
    return jnp.sum(stacked * weights, axis=0)


def slot_table(owners, slot_rank, slab_number, capacity):
    obs_count = owners.shape[1]
    matches = (owners == slab_number)[:, None, :] & (
        slot_rank[:, None, :] == jnp.arange(capacity, dtype=jnp.int32)[None, :, None]
    )
    slot_obs = jnp.sum(
        jnp.where(matches, jnp.arange(obs_count, dtype=jnp.int32)[None, None, :], 0), axis=2
    )
    slot_valid = jnp.any(matches, axis=2)
    return (slot_obs, slot_valid)


def gather_kernel(n_row, picked_ref, out_ref, part_ref, sem0, send0, sem_a, send_a, sem_b, send_b, sem_c, send_c):
    n_slab = lax.axis_size("slab")
    n_sub = lax.axis_size("sub")
    s = lax.axis_index("slab")
    u = lax.axis_index("sub")
    n_rows = n_slab // n_row
    row, loc = s // n_row, s % n_row

    def copy(src, dst, send, recv, dev):
        return pltpu.make_async_remote_copy(
            src_ref=src, dst_ref=dst, send_sem=send, recv_sem=recv, device_id=dev, device_id_type=MESH
        )

    def to_sub(d):
        q = (u + d) % n_sub
        return copy(picked_ref.at[q], part_ref.at[u], send0.at[q], sem0.at[u], (s, q))

    def from_sub(d):
        q = (u + d) % n_sub
        return copy(picked_ref.at[q], part_ref.at[q], send0.at[q], sem0.at[q], (s, q))

    barrier = pltpu.get_barrier_semaphore()
    for d in range(1, n_sub):
        pl.semaphore_signal(barrier, 1, device_id=(s, (u + d) % n_sub), device_id_type=MESH)

    def greet(d, c):
        dev = (row * n_row + (loc + d) % n_row, u)
        pl.semaphore_signal(barrier, 1, device_id=dev, device_id_type=MESH)
        return c

    lax.fori_loop(1, n_row, greet, 0)
    for d in range(1, n_rows):
        dev = (((row + d) % n_rows) * n_row + loc, u)
        pl.semaphore_signal(barrier, 1, device_id=dev, device_id_type=MESH)
    pl.semaphore_wait(barrier, (n_sub - 1) + (n_row - 1) + (n_rows - 1))

    for d in range(1, n_sub):
        to_sub(d).start()
    total = picked_ref[pl.ds(u, 1), :]
    for d in range(1, n_sub):
        from_sub(d).wait_recv()
        total = total + part_ref[pl.ds((u + d) % n_sub, 1), :]
    half = n_row // 2

    def own(t):
        j = t % n_row
        return out_ref.at[u, t // n_row, j // half, pl.ds(j % half, 1)]

    own(s)[...] = total

    def to_a(d):
        j = (loc + d) % n_row
        return copy(own(s), own(s), send_a.at[j], sem_a.at[loc], (row * n_row + j, u))

    def from_a(d):
        j = (loc + d) % n_row
        src = row * n_row + j
        return copy(own(src), own(src), send_a.at[j], sem_a.at[j], (src, u))

    def start_a(d, c):
        to_a(d).start()
        return c

    def wait_a(d, c):
        from_a(d).wait_recv()
        return c

    lax.fori_loop(1, n_row, start_a, 0)
    lax.fori_loop(1, n_row, wait_a, 0)

    def peer_x(d):
        r = (row + d) % n_rows
        return r, (r * n_row + loc, u)

    def peer_y(d):
        q = (u + d) % n_sub
        return q, (s, q)

    def to_b1(d):
        r, dev = peer_x(d)
        return copy(out_ref.at[u, row, 0], out_ref.at[u, row, 0], send_b.at[0, r], sem_b.at[0, row], dev)

    def from_b1(d):
        r, dev = peer_x(d)
        return copy(out_ref.at[u, r, 0], out_ref.at[u, r, 0], send_b.at[0, r], sem_b.at[0, r], dev)

    def to_c1(d):
        q, dev = peer_y(d)
        return copy(out_ref.at[u, row, 1], out_ref.at[u, row, 1], send_c.at[0, q], sem_c.at[0, u], dev)

    def from_c1(d):
        q, dev = peer_y(d)
        return copy(out_ref.at[q, row, 1], out_ref.at[q, row, 1], send_c.at[0, q], sem_c.at[0, q], dev)

    def to_b2(d):
        r, dev = peer_x(d)
        return copy(out_ref.at[:, row, 1], out_ref.at[:, row, 1], send_b.at[1, r], sem_b.at[1, row], dev)

    def from_b2(d):
        r, dev = peer_x(d)
        return copy(out_ref.at[:, r, 1], out_ref.at[:, r, 1], send_b.at[1, r], sem_b.at[1, r], dev)

    def to_c2(d):
        q, dev = peer_y(d)
        return copy(out_ref.at[u, :, 0], out_ref.at[u, :, 0], send_c.at[1, q], sem_c.at[1, u], dev)

    def from_c2(d):
        q, dev = peer_y(d)
        return copy(out_ref.at[q, :, 0], out_ref.at[q, :, 0], send_c.at[1, q], sem_c.at[1, q], dev)

    for d in range(1, n_rows):
        to_b1(d).start()
    for d in range(1, n_sub):
        to_c1(d).start()
    for d in range(1, n_sub):
        from_c1(d).wait_recv()
    for d in range(1, n_rows):
        to_b2(d).start()
    for d in range(1, n_rows):
        from_b1(d).wait_recv()
    for d in range(1, n_sub):
        to_c2(d).start()
    for d in range(1, n_rows):
        from_b2(d).wait_recv()
    for d in range(1, n_sub):
        from_c2(d).wait_recv()

    for d in range(1, n_sub):
        to_sub(d).wait_send()
    lax.fori_loop(1, n_row, lambda d, c: (to_a(d).wait_send(), c)[1], 0)
    for d in range(1, n_rows):
        to_b1(d).wait_send()
        to_b2(d).wait_send()
    for d in range(1, n_sub):
        to_c1(d).wait_send()
        to_c2(d).wait_send()


def gather_slots(picked, n_slab, n_sub, n_row):
    rows, width = picked.shape
    lanes = rows // n_sub * width
    n_rows = n_slab // n_row
    gathered = pl.pallas_call(
        functools.partial(gather_kernel, n_row),
        out_shape=jax.ShapeDtypeStruct((n_sub, n_rows, 2, n_row // 2, lanes), jnp.float32),
        in_specs=[pl.BlockSpec(memory_space=pltpu.VMEM)],
        out_specs=pl.BlockSpec(memory_space=pltpu.VMEM),
        scratch_shapes=[
            pltpu.VMEM((n_sub, lanes), jnp.float32),
            pltpu.SemaphoreType.DMA((n_sub,)),
            pltpu.SemaphoreType.DMA((n_sub,)),
            pltpu.SemaphoreType.DMA((n_row,)),
            pltpu.SemaphoreType.DMA((n_row,)),
            pltpu.SemaphoreType.DMA((2, n_rows)),
            pltpu.SemaphoreType.DMA((2, n_rows)),
            pltpu.SemaphoreType.DMA((2, n_sub)),
            pltpu.SemaphoreType.DMA((2, n_sub)),
        ],
        compiler_params=pltpu.CompilerParams(has_side_effects=True, collective_id=0),
    )(picked.reshape(n_sub, lanes))
    return gathered.reshape(n_sub, n_slab, lanes)


def per_device(ensemble, obs_value, obs_var, obs_owner, obs_column, home_block, batch_order):
    members = ensemble.shape[2]
    levels_count = ensemble.shape[1]
    cols_dev = ensemble.shape[3]
    slab_count = lax.axis_size("slab")
    sub_count = lax.axis_size("sub")
    slab_index = lax.axis_index("slab")
    sub_index = lax.axis_index("sub")
    capacity = CAP
    cols_slab = cols_dev * sub_count
    nblocks = cols_slab * slab_count // BLK
    span_broad = cols_slab // (4 * BLK)
    span_narrow = max(span_broad // 4, 1)
    decays = (float(span_broad), float(span_narrow))
    assert 2 * span_broad + 1 <= cols_slab // BLK and slab_count >= 3
    owners = obs_owner[:, :, 0]
    obs_home = jnp.mod((owners * cols_slab + obs_column) // BLK + home_block, nblocks)
    onehot = (owners[:, :, None] == jnp.arange(slab_count, dtype=jnp.int32)[None, None, :]).astype(
        jnp.int32
    )
    running = jnp.cumsum(onehot, axis=1) - 1
    slot_rank = jnp.sum(onehot * running, axis=2)
    slot_obs, slot_valid = slot_table(owners, slot_rank, slab_index, capacity)
    slot_column = jnp.take_along_axis(obs_column, slot_obs, axis=1)
    slot_level = slot_obs % levels_count
    holder = slot_column // cols_dev
    local_col = slot_column % cols_dev
    levels = jnp.take(ensemble, slot_level.reshape(-1), axis=1)
    retain = (slot_valid & (holder == sub_index)).reshape(-1)
    chosen = (jnp.arange(cols_dev, dtype=jnp.int32)[None, :] == local_col.reshape(-1, 1)) & retain[:, None]
    picked = jnp.sum(jnp.where(chosen[None, :, None, :], levels, 0.0), axis=3)
    picked = jnp.transpose(picked, (1, 0, 2)).reshape(BATCHES * capacity, BANDS * members)
    n_row = 32 if slab_count % 32 == 0 else slab_count
    gathered = gather_slots(picked, slab_count, sub_count, n_row)
    q_rows = BATCHES * capacity // sub_count
    width = BANDS * members
    row_of = jnp.arange(BATCHES, dtype=jnp.int32)[:, None] * capacity + slot_rank
    lines = jnp.take(
        gathered.reshape(sub_count * slab_count, q_rows * width),
        ((row_of // q_rows) * slab_count + owners).reshape(-1),
        axis=0,
    )
    part = (row_of % q_rows).reshape(-1, 1)
    flat_priors = lines[:, :width]
    for r in range(1, q_rows):
        flat_priors = jnp.where(part == r, lines[:, r * width : (r + 1) * width], flat_priors)
    priors = flat_priors.reshape(BATCHES, -1, width)

    turns = batch_order[:, None] == jnp.arange(BATCHES, dtype=jnp.int32)[None, :]
    first, second = turns[0], turns[1]
    y0 = pick(priors, first)
    home0 = pick(obs_home, first)
    home1 = pick(obs_home, second)
    stats0 = obs_statistics(y0, pick(obs_value, first), pick(obs_var, first), members)
    y1 = update_pool(pick(priors, second), home1, *stats0, home0, nblocks, decays)
    stats1 = obs_statistics(y1, pick(obs_value, second), pick(obs_var, second), members)
    recorded = jnp.sum(
        jnp.stack([y0, y1])[:, None] * turns.astype(jnp.float32)[:, :, None, None], axis=0
    )

    col_blocks = ((slab_index * sub_count + sub_index) * cols_dev + jnp.arange(
        cols_dev, dtype=jnp.int32
    )) // BLK
    near = jnp.mod(slab_index + jnp.arange(-1, 2, dtype=jnp.int32), slab_count)
    matches = (owners[:, None, None, :] == near[None, :, None, None]) & (
        slot_rank[:, None, None, :] == jnp.arange(capacity, dtype=jnp.int32)[None, None, :, None]
    )
    near_obs = jnp.sum(
        jnp.where(matches, jnp.arange(owners.shape[1], dtype=jnp.int32), 0), axis=3
    ).reshape(BATCHES, -1)
    near_valid = jnp.any(matches, axis=3).reshape(BATCHES, -1)
    for batch_id, homes, stats in ((first, home0, stats0), (second, home1, stats1)):
        deviations, spread, increments = stats
        table = jnp.concatenate(
            [
                deviations.reshape(-1, width),
                increments,
                spread[:, None],
                homes[:, None].astype(jnp.float32),
            ],
            axis=1,
        )
        rows = jnp.take(table, pick(near_obs, batch_id), axis=0)
        ensemble = update_state(
            ensemble,
            col_blocks,
            rows[:, :width].reshape(-1, BANDS, members),
            rows[:, width + members],
            rows[:, width : width + members],
            rows[:, width + members + 1].astype(jnp.int32),
            pick(near_valid.astype(jnp.int32), batch_id) > 0,
            nblocks,
            decays,
        )
    return (ensemble, recorded)


def solution(mesh):
    placed = (P(None, None, None, ("slab", "sub")), P(), P(), P(), P(), P(), P())
    return jax.shard_map(
        per_device,
        mesh=mesh,
        in_specs=placed,
        out_specs=(P(None, None, None, ("slab", "sub")), P()),
        check_vma=False,
    )
```

```python
import functools

import jax
import jax.numpy as jnp
from jax import lax
from jax.experimental import pallas as pl
from jax.experimental.pallas import tpu as pltpu
from jax.sharding import PartitionSpec as P

MESH = pl.DeviceIdType.MESH

BANDS = 2
BLK = 16
BATCHES = 2
CAP = 8


PRODUCT = lax.Precision.HIGH


def gc_weight(first, second, nblocks, length):
    block_gap = jnp.abs(first - second)
    block_gap = jnp.minimum(block_gap, nblocks - block_gap)
    scaled_gap = block_gap.astype(jnp.float32) / length
    near_part = (
        ((-0.25 * scaled_gap + 0.5) * scaled_gap + 0.625) * scaled_gap**3
        - 5.0 / 3.0 * scaled_gap**2
        + 1.0
    )
    floored = jnp.maximum(scaled_gap, 1.0)
    far_part = (
        (
            (((scaled_gap / 12.0 - 0.5) * scaled_gap + 0.625) * scaled_gap + 5.0 / 3.0) * scaled_gap
            - 5.0
        )
        * scaled_gap
        + 4.0
        - 2.0 / (3.0 * floored)
    )
    return jnp.where(scaled_gap <= 1.0, near_part, jnp.where(scaled_gap < 2.0, far_part, 0.0))


def obs_statistics(current, values, variances, members):
    banded = current.reshape(current.shape[0], BANDS, members)
    whole_obs = jnp.sum(banded, axis=1)
    centre = jnp.mean(whole_obs, axis=1, keepdims=True)
    spread = jnp.sum((whole_obs - centre) ** 2, axis=1) / (members - 1) + 1e-06
    post_var = 1.0 / (1.0 / spread + 1.0 / variances)
    post_mean = post_var * (centre[:, 0] / spread + values / variances)
    increments = (post_mean - centre[:, 0])[:, None] + (jnp.sqrt(post_var / spread) - 1.0)[
        :, None
    ] * (whole_obs - centre)
    deviations = banded - jnp.mean(banded, axis=2, keepdims=True)
    return (deviations, spread, increments)


def update_pool(pool, pool_homes, deviations, spread, increments, obs_homes, nblocks, decays):
    members = deviations.shape[2]
    banded = pool.reshape(pool.shape[0], BANDS, members)
    pool_dev = banded - jnp.mean(banded, axis=2, keepdims=True)
    weights = jnp.stack(
        [gc_weight(pool_homes[:, None], obs_homes[None, :], nblocks, decay) for decay in decays]
    ) / ((members - 1) * spread)[None, None, :]
    crossed = jnp.einsum("pbm,kbm->bpk", pool_dev, deviations, precision=PRODUCT)
    change = jnp.einsum("bpk,km->pbm", crossed * weights, increments, precision=PRODUCT)
    return (banded + change).reshape(pool.shape)


def update_state(ensemble, col_blocks, deviations, spread, increments, obs_homes, valid, nblocks, decays):
    members = ensemble.shape[2]
    layer_dev = ensemble - jnp.mean(ensemble, axis=2, keepdims=True)
    weights = jnp.stack(
        [gc_weight(col_blocks[:, None], obs_homes[None, :], nblocks, decay) for decay in decays]
    ) / ((members - 1) * spread)[None, None, :]
    weights = jnp.where(valid[None, None, :], weights, 0.0)
    crossed = jnp.einsum("blmc,kbm->blck", layer_dev, deviations, precision=PRODUCT)
    change = jnp.einsum("blck,km->blmc", crossed * weights[:, None], increments, precision=PRODUCT)
    return ensemble + change


def pick(stacked, chosen):
    weights = chosen.astype(stacked.dtype).reshape((-1,) + (1,) * (stacked.ndim - 1))
    return jnp.sum(stacked * weights, axis=0)


def slot_table(owners, slot_rank, slab_number, capacity, columns):
    obs_count = owners.shape[1]
    matches = (owners == slab_number)[:, None, :] & (
        slot_rank[:, None, :] == jnp.arange(capacity, dtype=jnp.int32)[None, :, None]
    )
    slot_obs = jnp.sum(
        jnp.where(matches, jnp.arange(obs_count, dtype=jnp.int32)[None, None, :], 0), axis=2
    )
    slot_valid = jnp.any(matches, axis=2)
    slot_column = jnp.sum(jnp.where(matches, columns[:, None, :], 0), axis=2)
    return (slot_obs, slot_valid, slot_column)


def gather_kernel(n_row, picked_ref, out_ref, part_ref, sem0, send0, sem_a, send_a, sem_b, send_b, sem_c, send_c):
    n_slab = lax.axis_size("slab")
    n_sub = lax.axis_size("sub")
    s = lax.axis_index("slab")
    u = lax.axis_index("sub")
    n_rows = n_slab // n_row
    row, loc = s // n_row, s % n_row

    def copy(src, dst, send, recv, dev):
        return pltpu.make_async_remote_copy(
            src_ref=src, dst_ref=dst, send_sem=send, recv_sem=recv, device_id=dev, device_id_type=MESH
        )

    def to_sub(d):
        q = (u + d) % n_sub
        return copy(picked_ref.at[q], part_ref.at[u], send0.at[q], sem0.at[u], (s, q))

    def from_sub(d):
        q = (u + d) % n_sub
        return copy(picked_ref.at[q], part_ref.at[q], send0.at[q], sem0.at[q], (s, q))

    barrier = pltpu.get_barrier_semaphore()
    for d in range(1, n_sub):
        pl.semaphore_signal(barrier, 1, device_id=(s, (u + d) % n_sub), device_id_type=MESH)

    def greet(d, c):
        dev = (row * n_row + (loc + d) % n_row, u)
        pl.semaphore_signal(barrier, 1, device_id=dev, device_id_type=MESH)
        return c

    lax.fori_loop(1, n_row, greet, 0)
    for d in range(1, n_rows):
        dev = (((row + d) % n_rows) * n_row + loc, u)
        pl.semaphore_signal(barrier, 1, device_id=dev, device_id_type=MESH)
    pl.semaphore_wait(barrier, (n_sub - 1) + (n_row - 1) + (n_rows - 1))

    for d in range(1, n_sub):
        to_sub(d).start()
    total = picked_ref[pl.ds(u, 1), :]
    for d in range(1, n_sub):
        from_sub(d).wait_recv()
        total = total + part_ref[pl.ds((u + d) % n_sub, 1), :]
    half = n_row // 2

    def own(t):
        j = t % n_row
        return out_ref.at[u, t // n_row, j // half, pl.ds(j % half, 1)]

    own(s)[...] = total

    def to_a(d):
        j = (loc + d) % n_row
        return copy(own(s), own(s), send_a.at[j], sem_a.at[loc], (row * n_row + j, u))

    def from_a(d):
        j = (loc + d) % n_row
        src = row * n_row + j
        return copy(own(src), own(src), send_a.at[j], sem_a.at[j], (src, u))

    def start_a(d, c):
        to_a(d).start()
        return c

    def wait_a(d, c):
        from_a(d).wait_recv()
        return c

    lax.fori_loop(1, n_row, start_a, 0)
    lax.fori_loop(1, n_row, wait_a, 0)

    def peer_x(d):
        r = (row + d) % n_rows
        return r, (r * n_row + loc, u)

    def peer_y(d):
        q = (u + d) % n_sub
        return q, (s, q)

    def to_b1(d):
        r, dev = peer_x(d)
        return copy(out_ref.at[u, row, 0], out_ref.at[u, row, 0], send_b.at[0, r], sem_b.at[0, row], dev)

    def from_b1(d):
        r, dev = peer_x(d)
        return copy(out_ref.at[u, r, 0], out_ref.at[u, r, 0], send_b.at[0, r], sem_b.at[0, r], dev)

    def to_c1(d):
        q, dev = peer_y(d)
        return copy(out_ref.at[u, row, 1], out_ref.at[u, row, 1], send_c.at[0, q], sem_c.at[0, u], dev)

    def from_c1(d):
        q, dev = peer_y(d)
        return copy(out_ref.at[q, row, 1], out_ref.at[q, row, 1], send_c.at[0, q], sem_c.at[0, q], dev)

    def to_b2(d):
        r, dev = peer_x(d)
        return copy(out_ref.at[:, row, 1], out_ref.at[:, row, 1], send_b.at[1, r], sem_b.at[1, row], dev)

    def from_b2(d):
        r, dev = peer_x(d)
        return copy(out_ref.at[:, r, 1], out_ref.at[:, r, 1], send_b.at[1, r], sem_b.at[1, r], dev)

    def to_c2(d):
        q, dev = peer_y(d)
        return copy(out_ref.at[u, :, 0], out_ref.at[u, :, 0], send_c.at[1, q], sem_c.at[1, u], dev)

    def from_c2(d):
        q, dev = peer_y(d)
        return copy(out_ref.at[q, :, 0], out_ref.at[q, :, 0], send_c.at[1, q], sem_c.at[1, q], dev)

    for d in range(1, n_rows):
        to_b1(d).start()
    for d in range(1, n_sub):
        to_c1(d).start()
    for d in range(1, n_sub):
        from_c1(d).wait_recv()
    for d in range(1, n_rows):
        to_b2(d).start()
    for d in range(1, n_rows):
        from_b1(d).wait_recv()
    for d in range(1, n_sub):
        to_c2(d).start()
    for d in range(1, n_rows):
        from_b2(d).wait_recv()
    for d in range(1, n_sub):
        from_c2(d).wait_recv()

    for d in range(1, n_sub):
        to_sub(d).wait_send()
    lax.fori_loop(1, n_row, lambda d, c: (to_a(d).wait_send(), c)[1], 0)
    for d in range(1, n_rows):
        to_b1(d).wait_send()
        to_b2(d).wait_send()
    for d in range(1, n_sub):
        to_c1(d).wait_send()
        to_c2(d).wait_send()


def gather_slots(picked, n_slab, n_sub, n_row):
    rows, width = picked.shape
    lanes = rows // n_sub * width
    n_rows = n_slab // n_row
    gathered = pl.pallas_call(
        functools.partial(gather_kernel, n_row),
        out_shape=jax.ShapeDtypeStruct((n_sub, n_rows, 2, n_row // 2, lanes), jnp.float32),
        in_specs=[pl.BlockSpec(memory_space=pltpu.VMEM)],
        out_specs=pl.BlockSpec(memory_space=pltpu.VMEM),
        scratch_shapes=[
            pltpu.VMEM((n_sub, lanes), jnp.float32),
            pltpu.SemaphoreType.DMA((n_sub,)),
            pltpu.SemaphoreType.DMA((n_sub,)),
            pltpu.SemaphoreType.DMA((n_row,)),
            pltpu.SemaphoreType.DMA((n_row,)),
            pltpu.SemaphoreType.DMA((2, n_rows)),
            pltpu.SemaphoreType.DMA((2, n_rows)),
            pltpu.SemaphoreType.DMA((2, n_sub)),
            pltpu.SemaphoreType.DMA((2, n_sub)),
        ],
        compiler_params=pltpu.CompilerParams(has_side_effects=True, collective_id=0),
    )(picked.reshape(n_sub, lanes))
    return gathered.reshape(n_sub, n_slab, lanes)


def per_device(ensemble, obs_value, obs_var, obs_owner, obs_column, home_block, batch_order):
    members = ensemble.shape[2]
    levels_count = ensemble.shape[1]
    cols_dev = ensemble.shape[3]
    slab_count = lax.axis_size("slab")
    sub_count = lax.axis_size("sub")
    slab_index = lax.axis_index("slab")
    sub_index = lax.axis_index("sub")
    capacity = CAP
    cols_slab = cols_dev * sub_count
    nblocks = cols_slab * slab_count // BLK
    span_broad = cols_slab // (4 * BLK)
    span_narrow = max(span_broad // 4, 1)
    decays = (float(span_broad), float(span_narrow))
    assert 2 * span_broad + 1 <= cols_slab // BLK and slab_count >= 3
    owners = obs_owner[:, :, 0]
    obs_home = jnp.mod((owners * cols_slab + obs_column) // BLK + home_block, nblocks)
    order = jnp.arange(owners.shape[1], dtype=jnp.int32)
    earlier = (owners[:, None, :] == owners[:, :, None]) & (order[None, :] < order[:, None])[None]
    slot_rank = jnp.sum(earlier.astype(jnp.int32), axis=2)
    slot_obs, slot_valid, slot_column = slot_table(owners, slot_rank, slab_index, capacity, obs_column)
    slot_level = slot_obs % levels_count
    holder = slot_column // cols_dev
    local_col = slot_column % cols_dev
    levels = jnp.take(ensemble, slot_level.reshape(-1), axis=1)
    retain = (slot_valid & (holder == sub_index)).reshape(-1)
    chosen = (jnp.arange(cols_dev, dtype=jnp.int32)[None, :] == local_col.reshape(-1, 1)) & retain[:, None]
    picked = jnp.sum(jnp.where(chosen[None, :, None, :], levels, 0.0), axis=3)
    picked = jnp.transpose(picked, (1, 0, 2)).reshape(BATCHES * capacity, BANDS * members)
    n_row = 32 if slab_count % 32 == 0 else slab_count
    gathered = gather_slots(picked, slab_count, sub_count, n_row)
    q_rows = BATCHES * capacity // sub_count
    width = BANDS * members
    row_of = jnp.arange(BATCHES, dtype=jnp.int32)[:, None] * capacity + slot_rank
    lines = jnp.take(
        gathered.reshape(sub_count * slab_count, q_rows * width),
        ((row_of // q_rows) * slab_count + owners).reshape(-1),
        axis=0,
    )
    part = (row_of % q_rows).reshape(-1, 1)
    flat_priors = lines[:, :width]
    for r in range(1, q_rows):
        flat_priors = jnp.where(part == r, lines[:, r * width : (r + 1) * width], flat_priors)
    priors = flat_priors.reshape(BATCHES, -1, width)

    turns = batch_order[:, None] == jnp.arange(BATCHES, dtype=jnp.int32)[None, :]
    first, second = turns[0], turns[1]
    y0 = pick(priors, first)
    home0 = pick(obs_home, first)
    home1 = pick(obs_home, second)
    stats0 = obs_statistics(y0, pick(obs_value, first), pick(obs_var, first), members)
    y1 = update_pool(pick(priors, second), home1, *stats0, home0, nblocks, decays)
    stats1 = obs_statistics(y1, pick(obs_value, second), pick(obs_var, second), members)
    recorded = jnp.sum(
        jnp.stack([y0, y1])[:, None] * turns.astype(jnp.float32)[:, :, None, None], axis=0
    )

    col_blocks = ((slab_index * sub_count + sub_index) * cols_dev + jnp.arange(
        cols_dev, dtype=jnp.int32
    )) // BLK
    near = jnp.mod(slab_index + jnp.arange(-1, 2, dtype=jnp.int32), slab_count)
    matches = (owners[:, None, None, :] == near[None, :, None, None]) & (
        slot_rank[:, None, None, :] == jnp.arange(capacity, dtype=jnp.int32)[None, None, :, None]
    )
    near_obs = jnp.sum(
        jnp.where(matches, jnp.arange(owners.shape[1], dtype=jnp.int32), 0), axis=3
    ).reshape(BATCHES, -1)
    near_valid = jnp.any(matches, axis=3).reshape(BATCHES, -1)
    for batch_id, homes, stats in ((first, home0, stats0), (second, home1, stats1)):
        deviations, spread, increments = stats
        table = jnp.concatenate(
            [
                deviations.reshape(-1, width),
                increments,
                spread[:, None],
                homes[:, None].astype(jnp.float32),
            ],
            axis=1,
        )
        rows = jnp.take(table, pick(near_obs, batch_id), axis=0)
        ensemble = update_state(
            ensemble,
            col_blocks,
            rows[:, :width].reshape(-1, BANDS, members),
            rows[:, width + members],
            rows[:, width : width + members],
            rows[:, width + members + 1].astype(jnp.int32),
            pick(near_valid.astype(jnp.int32), batch_id) > 0,
            nblocks,
            decays,
        )
    return (ensemble, recorded)


def solution(mesh):
    placed = (P(None, None, None, ("slab", "sub")), P(), P(), P(), P(), P(), P())
    return jax.shard_map(
        per_device,
        mesh=mesh,
        in_specs=placed,
        out_specs=(P(None, None, None, ("slab", "sub")), P()),
        check_vma=False,
    )
```

```python
import functools

import jax
import jax.numpy as jnp
from jax import lax
from jax.experimental import pallas as pl
from jax.experimental.pallas import tpu as pltpu
from jax.sharding import PartitionSpec as P

MESH = pl.DeviceIdType.MESH

BANDS = 2
BLK = 16
BATCHES = 2
CAP = 8


PRODUCT = lax.Precision.HIGH


def gc_weight(first, second, nblocks, length):
    block_gap = jnp.abs(first - second)
    block_gap = jnp.minimum(block_gap, nblocks - block_gap)
    scaled_gap = block_gap.astype(jnp.float32) / length
    near_part = (
        ((-0.25 * scaled_gap + 0.5) * scaled_gap + 0.625) * scaled_gap**3
        - 5.0 / 3.0 * scaled_gap**2
        + 1.0
    )
    floored = jnp.maximum(scaled_gap, 1.0)
    far_part = (
        (
            (((scaled_gap / 12.0 - 0.5) * scaled_gap + 0.625) * scaled_gap + 5.0 / 3.0) * scaled_gap
            - 5.0
        )
        * scaled_gap
        + 4.0
        - 2.0 / (3.0 * floored)
    )
    return jnp.where(scaled_gap <= 1.0, near_part, jnp.where(scaled_gap < 2.0, far_part, 0.0))


def obs_statistics(current, values, variances, members):
    banded = current.reshape(current.shape[0], BANDS, members)
    whole_obs = jnp.sum(banded, axis=1)
    centre = jnp.mean(whole_obs, axis=1, keepdims=True)
    spread = jnp.sum((whole_obs - centre) ** 2, axis=1) / (members - 1) + 1e-06
    post_var = 1.0 / (1.0 / spread + 1.0 / variances)
    post_mean = post_var * (centre[:, 0] / spread + values / variances)
    increments = (post_mean - centre[:, 0])[:, None] + (jnp.sqrt(post_var / spread) - 1.0)[
        :, None
    ] * (whole_obs - centre)
    deviations = banded - jnp.mean(banded, axis=2, keepdims=True)
    return (deviations, spread, increments)


def update_pool(pool, pool_homes, deviations, spread, increments, obs_homes, nblocks, decays):
    members = deviations.shape[2]
    banded = pool.reshape(pool.shape[0], BANDS, members)
    pool_dev = banded - jnp.mean(banded, axis=2, keepdims=True)
    weights = jnp.stack(
        [gc_weight(pool_homes[:, None], obs_homes[None, :], nblocks, decay) for decay in decays]
    ) / ((members - 1) * spread)[None, None, :]
    crossed = jnp.einsum("pbm,kbm->bpk", pool_dev, deviations, precision=PRODUCT)
    change = jnp.einsum("bpk,km->pbm", crossed * weights, increments, precision=PRODUCT)
    return (banded + change).reshape(pool.shape)


def update_state(ensemble, col_blocks, deviations, spread, increments, obs_homes, valid, nblocks, decays):
    members = ensemble.shape[2]
    layer_dev = ensemble - jnp.mean(ensemble, axis=2, keepdims=True)
    weights = jnp.stack(
        [gc_weight(col_blocks[:, None], obs_homes[None, :], nblocks, decay) for decay in decays]
    ) / ((members - 1) * spread)[None, None, :]
    weights = jnp.where(valid[None, None, :], weights, 0.0)
    crossed = jnp.einsum("blmc,kbm->blck", layer_dev, deviations, precision=PRODUCT)
    change = jnp.einsum("blck,km->blmc", crossed * weights[:, None], increments, precision=PRODUCT)
    return ensemble + change


def pick(stacked, chosen):
    weights = chosen.astype(stacked.dtype).reshape((-1,) + (1,) * (stacked.ndim - 1))
    return jnp.sum(stacked * weights, axis=0)


def slot_table(owners, slot_rank, slab_number, capacity, columns):
    obs_count = owners.shape[1]
    matches = (owners == slab_number)[:, None, :] & (
        slot_rank[:, None, :] == jnp.arange(capacity, dtype=jnp.int32)[None, :, None]
    )
    slot_obs = jnp.sum(
        jnp.where(matches, jnp.arange(obs_count, dtype=jnp.int32)[None, None, :], 0), axis=2
    )
    slot_valid = jnp.any(matches, axis=2)
    slot_column = jnp.sum(jnp.where(matches, columns[:, None, :], 0), axis=2)
    return (slot_obs, slot_valid, slot_column)


def gather_kernel(n_row, picked_ref, out_ref, part_ref, sem0, send0, sem_a, send_a, sem_b, send_b, sem_c, send_c):
    n_slab = lax.axis_size("slab")
    n_sub = lax.axis_size("sub")
    s = lax.axis_index("slab")
    u = lax.axis_index("sub")
    n_rows = n_slab // n_row
    row, loc = s // n_row, s % n_row

    def copy(src, dst, send, recv, dev):
        return pltpu.make_async_remote_copy(
            src_ref=src, dst_ref=dst, send_sem=send, recv_sem=recv, device_id=dev, device_id_type=MESH
        )

    def to_sub(d):
        q = (u + d) % n_sub
        return copy(picked_ref.at[q], part_ref.at[u], send0.at[q], sem0.at[u], (s, q))

    def from_sub(d):
        q = (u + d) % n_sub
        return copy(picked_ref.at[q], part_ref.at[q], send0.at[q], sem0.at[q], (s, q))

    barrier = pltpu.get_barrier_semaphore()
    for d in range(1, n_sub):
        pl.semaphore_signal(barrier, 1, device_id=(s, (u + d) % n_sub), device_id_type=MESH)

    def greet(d, c):
        dev = (row * n_row + (loc + d) % n_row, u)
        pl.semaphore_signal(barrier, 1, device_id=dev, device_id_type=MESH)
        return c

    lax.fori_loop(1, n_row, greet, 0)
    for d in range(1, n_rows):
        dev = (((row + d) % n_rows) * n_row + loc, u)
        pl.semaphore_signal(barrier, 1, device_id=dev, device_id_type=MESH)
    pl.semaphore_wait(barrier, (n_sub - 1) + (n_row - 1) + (n_rows - 1))

    for d in range(1, n_sub):
        to_sub(d).start()
    total = picked_ref[pl.ds(u, 1), :]
    for d in range(1, n_sub):
        from_sub(d).wait_recv()
        total = total + part_ref[pl.ds((u + d) % n_sub, 1), :]
    half = n_row // 2

    def own(t):
        j = t % n_row
        return out_ref.at[u, t // n_row, j // half, pl.ds(j % half, 1)]

    own(s)[...] = total

    def to_a(d):
        j = (loc + d) % n_row
        return copy(own(s), own(s), send_a.at[j], sem_a.at[loc], (row * n_row + j, u))

    def from_a(d):
        j = (loc + d) % n_row
        src = row * n_row + j
        return copy(own(src), own(src), send_a.at[j], sem_a.at[j], (src, u))

    def start_a(d, c):
        to_a(d).start()
        return c

    def wait_a(d, c):
        from_a(d).wait_recv()
        return c

    lax.fori_loop(1, n_row, start_a, 0)
    lax.fori_loop(1, n_row, wait_a, 0)

    def peer_x(d):
        r = (row + d) % n_rows
        return r, (r * n_row + loc, u)

    def peer_y(d):
        q = (u + d) % n_sub
        return q, (s, q)

    def to_b1(d):
        r, dev = peer_x(d)
        return copy(out_ref.at[u, row, 0], out_ref.at[u, row, 0], send_b.at[0, r], sem_b.at[0, row], dev)

    def from_b1(d):
        r, dev = peer_x(d)
        return copy(out_ref.at[u, r, 0], out_ref.at[u, r, 0], send_b.at[0, r], sem_b.at[0, r], dev)

    def to_c1(d):
        q, dev = peer_y(d)
        return copy(out_ref.at[u, row, 1], out_ref.at[u, row, 1], send_c.at[0, q], sem_c.at[0, u], dev)

    def from_c1(d):
        q, dev = peer_y(d)
        return copy(out_ref.at[q, row, 1], out_ref.at[q, row, 1], send_c.at[0, q], sem_c.at[0, q], dev)

    def to_b2(d):
        r, dev = peer_x(d)
        return copy(out_ref.at[:, row, 1], out_ref.at[:, row, 1], send_b.at[1, r], sem_b.at[1, row], dev)

    def from_b2(d):
        r, dev = peer_x(d)
        return copy(out_ref.at[:, r, 1], out_ref.at[:, r, 1], send_b.at[1, r], sem_b.at[1, r], dev)

    def to_c2(d):
        q, dev = peer_y(d)
        return copy(out_ref.at[u, :, 0], out_ref.at[u, :, 0], send_c.at[1, q], sem_c.at[1, u], dev)

    def from_c2(d):
        q, dev = peer_y(d)
        return copy(out_ref.at[q, :, 0], out_ref.at[q, :, 0], send_c.at[1, q], sem_c.at[1, q], dev)

    for d in range(1, n_rows):
        to_b1(d).start()
    for d in range(1, n_sub):
        to_c1(d).start()
    for d in range(1, n_sub):
        from_c1(d).wait_recv()
    for d in range(1, n_rows):
        to_b2(d).start()
    for d in range(1, n_rows):
        from_b1(d).wait_recv()
    for d in range(1, n_sub):
        to_c2(d).start()
    for d in range(1, n_rows):
        from_b2(d).wait_recv()
    for d in range(1, n_sub):
        from_c2(d).wait_recv()

    for d in range(1, n_sub):
        to_sub(d).wait_send()
    lax.fori_loop(1, n_row, lambda d, c: (to_a(d).wait_send(), c)[1], 0)
    for d in range(1, n_rows):
        to_b1(d).wait_send()
        to_b2(d).wait_send()
    for d in range(1, n_sub):
        to_c1(d).wait_send()
        to_c2(d).wait_send()


def gather_slots(picked, n_slab, n_sub, n_row):
    rows, width = picked.shape
    lanes = rows // n_sub * width
    n_rows = n_slab // n_row
    gathered = pl.pallas_call(
        functools.partial(gather_kernel, n_row),
        out_shape=jax.ShapeDtypeStruct((n_sub, n_rows, 2, n_row // 2, lanes), jnp.float32),
        in_specs=[pl.BlockSpec(memory_space=pltpu.VMEM)],
        out_specs=pl.BlockSpec(memory_space=pltpu.VMEM),
        scratch_shapes=[
            pltpu.VMEM((n_sub, lanes), jnp.float32),
            pltpu.SemaphoreType.DMA((n_sub,)),
            pltpu.SemaphoreType.DMA((n_sub,)),
            pltpu.SemaphoreType.DMA((n_row,)),
            pltpu.SemaphoreType.DMA((n_row,)),
            pltpu.SemaphoreType.DMA((2, n_rows)),
            pltpu.SemaphoreType.DMA((2, n_rows)),
            pltpu.SemaphoreType.DMA((2, n_sub)),
            pltpu.SemaphoreType.DMA((2, n_sub)),
        ],
        compiler_params=pltpu.CompilerParams(has_side_effects=True, collective_id=0),
    )(picked.reshape(n_sub, lanes))
    return gathered.reshape(n_sub, n_slab, lanes)


def per_device(ensemble, obs_value, obs_var, obs_owner, obs_column, home_block, batch_order):
    members = ensemble.shape[2]
    levels_count = ensemble.shape[1]
    cols_dev = ensemble.shape[3]
    slab_count = lax.axis_size("slab")
    sub_count = lax.axis_size("sub")
    slab_index = lax.axis_index("slab")
    sub_index = lax.axis_index("sub")
    capacity = CAP
    cols_slab = cols_dev * sub_count
    nblocks = cols_slab * slab_count // BLK
    span_broad = cols_slab // (4 * BLK)
    span_narrow = max(span_broad // 4, 1)
    decays = (float(span_broad), float(span_narrow))
    assert 2 * span_broad + 1 <= cols_slab // BLK and slab_count >= 3
    owners = obs_owner[:, :, 0]
    obs_home = jnp.mod((owners * cols_slab + obs_column) // BLK + home_block, nblocks)
    onehot = (owners[:, :, None] == jnp.arange(slab_count, dtype=jnp.int32)[None, None, :]).astype(
        jnp.int32
    )
    running = jnp.cumsum(onehot, axis=1) - 1
    slot_rank = jnp.sum(onehot * running, axis=2)
    slot_obs, slot_valid, slot_column = slot_table(owners, slot_rank, slab_index, capacity, obs_column)
    slot_level = slot_obs % levels_count
    holder = slot_column // cols_dev
    local_col = slot_column % cols_dev
    levels = jnp.take(ensemble, slot_level.reshape(-1), axis=1)
    retain = (slot_valid & (holder == sub_index)).reshape(-1)
    chosen = (jnp.arange(cols_dev, dtype=jnp.int32)[None, :] == local_col.reshape(-1, 1)) & retain[:, None]
    picked = jnp.sum(jnp.where(chosen[None, :, None, :], levels, 0.0), axis=3)
    picked = jnp.transpose(picked, (1, 0, 2)).reshape(BATCHES * capacity, BANDS * members)
    n_row = 32 if slab_count % 32 == 0 else slab_count
    gathered = gather_slots(picked, slab_count, sub_count, n_row)
    q_rows = BATCHES * capacity // sub_count
    width = BANDS * members
    row_of = jnp.arange(BATCHES, dtype=jnp.int32)[:, None] * capacity + slot_rank
    lines = jnp.take(
        gathered.reshape(sub_count * slab_count, q_rows * width),
        ((row_of // q_rows) * slab_count + owners).reshape(-1),
        axis=0,
    )
    part = (row_of % q_rows).reshape(-1, 1)
    flat_priors = lines[:, :width]
    for r in range(1, q_rows):
        flat_priors = jnp.where(part == r, lines[:, r * width : (r + 1) * width], flat_priors)
    priors = flat_priors.reshape(BATCHES, -1, width)

    turns = batch_order[:, None] == jnp.arange(BATCHES, dtype=jnp.int32)[None, :]
    first, second = turns[0], turns[1]
    y0 = pick(priors, first)
    home0 = pick(obs_home, first)
    home1 = pick(obs_home, second)
    stats0 = obs_statistics(y0, pick(obs_value, first), pick(obs_var, first), members)
    y1 = update_pool(pick(priors, second), home1, *stats0, home0, nblocks, decays)
    stats1 = obs_statistics(y1, pick(obs_value, second), pick(obs_var, second), members)
    recorded = jnp.sum(
        jnp.stack([y0, y1])[:, None] * turns.astype(jnp.float32)[:, :, None, None], axis=0
    )

    col_blocks = ((slab_index * sub_count + sub_index) * cols_dev + jnp.arange(
        cols_dev, dtype=jnp.int32
    )) // BLK
    near = jnp.mod(slab_index + jnp.arange(-1, 2, dtype=jnp.int32), slab_count)
    matches = (owners[:, None, None, :] == near[None, :, None, None]) & (
        slot_rank[:, None, None, :] == jnp.arange(capacity, dtype=jnp.int32)[None, None, :, None]
    )
    near_obs = jnp.sum(
        jnp.where(matches, jnp.arange(owners.shape[1], dtype=jnp.int32), 0), axis=3
    ).reshape(BATCHES, -1)
    near_valid = jnp.any(matches, axis=3).reshape(BATCHES, -1)
    for batch_id, homes, stats in ((first, home0, stats0), (second, home1, stats1)):
        deviations, spread, increments = stats
        table = jnp.concatenate(
            [
                deviations.reshape(-1, width),
                increments,
                spread[:, None],
                homes[:, None].astype(jnp.float32),
            ],
            axis=1,
        )
        rows = jnp.take(table, pick(near_obs, batch_id), axis=0)
        ensemble = update_state(
            ensemble,
            col_blocks,
            rows[:, :width].reshape(-1, BANDS, members),
            rows[:, width + members],
            rows[:, width : width + members],
            rows[:, width + members + 1].astype(jnp.int32),
            pick(near_valid.astype(jnp.int32), batch_id) > 0,
            nblocks,
            decays,
        )
    return (ensemble, recorded)


def solution(mesh):
    placed = (P(None, None, None, ("slab", "sub")), P(), P(), P(), P(), P(), P())
    return jax.shard_map(
        per_device,
        mesh=mesh,
        in_specs=placed,
        out_specs=(P(None, None, None, ("slab", "sub")), P()),
        check_vma=False,
    )
```

```python
import functools

import jax
import jax.numpy as jnp
from jax import lax
from jax.experimental import pallas as pl
from jax.experimental.pallas import tpu as pltpu
from jax.sharding import PartitionSpec as P

MESH = pl.DeviceIdType.MESH

BANDS = 2
BLK = 16
BATCHES = 2
CAP = 8


PRODUCT = lax.Precision.HIGH


def gc_weight(first, second, nblocks, length):
    block_gap = jnp.abs(first - second)
    block_gap = jnp.minimum(block_gap, nblocks - block_gap)
    scaled_gap = block_gap.astype(jnp.float32) / length
    near_part = (
        ((-0.25 * scaled_gap + 0.5) * scaled_gap + 0.625) * scaled_gap**3
        - 5.0 / 3.0 * scaled_gap**2
        + 1.0
    )
    floored = jnp.maximum(scaled_gap, 1.0)
    far_part = (
        (
            (((scaled_gap / 12.0 - 0.5) * scaled_gap + 0.625) * scaled_gap + 5.0 / 3.0) * scaled_gap
            - 5.0
        )
        * scaled_gap
        + 4.0
        - 2.0 / (3.0 * floored)
    )
    return jnp.where(scaled_gap <= 1.0, near_part, jnp.where(scaled_gap < 2.0, far_part, 0.0))


def obs_statistics(current, values, variances, members):
    banded = current.reshape(current.shape[0], BANDS, members)
    whole_obs = jnp.sum(banded, axis=1)
    centre = jnp.mean(whole_obs, axis=1, keepdims=True)
    spread = jnp.sum((whole_obs - centre) ** 2, axis=1) / (members - 1) + 1e-06
    post_var = 1.0 / (1.0 / spread + 1.0 / variances)
    post_mean = post_var * (centre[:, 0] / spread + values / variances)
    increments = (post_mean - centre[:, 0])[:, None] + (jnp.sqrt(post_var / spread) - 1.0)[
        :, None
    ] * (whole_obs - centre)
    deviations = banded - jnp.mean(banded, axis=2, keepdims=True)
    return (deviations, spread, increments)


def update_pool(pool, pool_homes, deviations, spread, increments, obs_homes, nblocks, decays):
    members = deviations.shape[2]
    banded = pool.reshape(pool.shape[0], BANDS, members)
    pool_dev = banded - jnp.mean(banded, axis=2, keepdims=True)
    weights = jnp.stack(
        [gc_weight(pool_homes[:, None], obs_homes[None, :], nblocks, decay) for decay in decays]
    ) / ((members - 1) * spread)[None, None, :]
    crossed = jnp.einsum("pbm,kbm->bpk", pool_dev, deviations, precision=PRODUCT)
    change = jnp.einsum("bpk,km->pbm", crossed * weights, increments, precision=PRODUCT)
    return (banded + change).reshape(pool.shape)


def update_state(ensemble, col_blocks, deviations, spread, increments, obs_homes, valid, nblocks, decays):
    members = ensemble.shape[2]
    layer_dev = ensemble - jnp.mean(ensemble, axis=2, keepdims=True)
    weights = jnp.stack(
        [gc_weight(col_blocks[:, None], obs_homes[None, :], nblocks, decay) for decay in decays]
    ) / ((members - 1) * spread)[None, None, :]
    weights = jnp.where(valid[None, None, :], weights, 0.0)
    crossed = jnp.einsum("blmc,kbm->blck", layer_dev, deviations, precision=PRODUCT)
    change = jnp.einsum("blck,km->blmc", crossed * weights[:, None], increments, precision=PRODUCT)
    return ensemble + change


def pick(stacked, chosen):
    weights = chosen.astype(stacked.dtype).reshape((-1,) + (1,) * (stacked.ndim - 1))
    return jnp.sum(stacked * weights, axis=0)


def slot_table(owners, slot_rank, slab_number, capacity, columns):
    obs_count = owners.shape[1]
    matches = (owners == slab_number)[:, None, :] & (
        slot_rank[:, None, :] == jnp.arange(capacity, dtype=jnp.int32)[None, :, None]
    )
    slot_obs = jnp.sum(
        jnp.where(matches, jnp.arange(obs_count, dtype=jnp.int32)[None, None, :], 0), axis=2
    )
    slot_valid = jnp.any(matches, axis=2)
    slot_column = jnp.sum(jnp.where(matches, columns[:, None, :], 0), axis=2)
    return (slot_obs, slot_valid, slot_column)


def gather_kernel(n_row, picked_ref, out_ref, part_ref, sem0, send0, sem_a, send_a, sem_b, send_b, sem_c, send_c):
    n_slab = lax.axis_size("slab")
    n_sub = lax.axis_size("sub")
    s = lax.axis_index("slab")
    u = lax.axis_index("sub")
    n_rows = n_slab // n_row
    row, loc = s // n_row, s % n_row

    def copy(src, dst, send, recv, dev):
        return pltpu.make_async_remote_copy(
            src_ref=src, dst_ref=dst, send_sem=send, recv_sem=recv, device_id=dev, device_id_type=MESH
        )

    def to_sub(d):
        q = (u + d) % n_sub
        return copy(picked_ref.at[q], part_ref.at[u], send0.at[q], sem0.at[u], (s, q))

    def from_sub(d):
        q = (u + d) % n_sub
        return copy(picked_ref.at[q], part_ref.at[q], send0.at[q], sem0.at[q], (s, q))

    barrier = pltpu.get_barrier_semaphore()
    for d in range(1, n_sub):
        pl.semaphore_signal(barrier, 1, device_id=(s, (u + d) % n_sub), device_id_type=MESH)

    def greet(d, c):
        dev = (row * n_row + (loc + d) % n_row, u)
        pl.semaphore_signal(barrier, 1, device_id=dev, device_id_type=MESH)
        return c

    lax.fori_loop(1, n_row, greet, 0)
    for d in range(1, n_rows):
        dev = (((row + d) % n_rows) * n_row + loc, u)
        pl.semaphore_signal(barrier, 1, device_id=dev, device_id_type=MESH)
    pl.semaphore_wait(barrier, (n_sub - 1) + (n_row - 1) + (n_rows - 1))

    for d in range(1, n_sub):
        to_sub(d).start()
    total = picked_ref[pl.ds(u, 1), :]
    for d in range(1, n_sub):
        from_sub(d).wait_recv()
        total = total + part_ref[pl.ds((u + d) % n_sub, 1), :]
    half = n_row // 2

    def own(t):
        j = t % n_row
        return out_ref.at[u, t // n_row, j // half, pl.ds(j % half, 1)]

    own(s)[...] = total

    def to_a(d):
        j = (loc + d) % n_row
        return copy(own(s), own(s), send_a.at[j], sem_a.at[loc], (row * n_row + j, u))

    def from_a(d):
        j = (loc + d) % n_row
        src = row * n_row + j
        return copy(own(src), own(src), send_a.at[j], sem_a.at[j], (src, u))

    def start_a(d, c):
        to_a(d).start()
        return c

    def wait_a(d, c):
        from_a(d).wait_recv()
        return c

    lax.fori_loop(1, n_row, start_a, 0)
    lax.fori_loop(1, n_row, wait_a, 0)

    def peer_x(d):
        r = (row + d) % n_rows
        return r, (r * n_row + loc, u)

    def peer_y(d):
        q = (u + d) % n_sub
        return q, (s, q)

    def to_b1(d):
        r, dev = peer_x(d)
        return copy(out_ref.at[u, row, 0], out_ref.at[u, row, 0], send_b.at[0, r], sem_b.at[0, row], dev)

    def from_b1(d):
        r, dev = peer_x(d)
        return copy(out_ref.at[u, r, 0], out_ref.at[u, r, 0], send_b.at[0, r], sem_b.at[0, r], dev)

    def to_c1(d):
        q, dev = peer_y(d)
        return copy(out_ref.at[u, row, 1], out_ref.at[u, row, 1], send_c.at[0, q], sem_c.at[0, u], dev)

    def from_c1(d):
        q, dev = peer_y(d)
        return copy(out_ref.at[q, row, 1], out_ref.at[q, row, 1], send_c.at[0, q], sem_c.at[0, q], dev)

    def to_b2(d):
        r, dev = peer_x(d)
        return copy(out_ref.at[:, row, 1], out_ref.at[:, row, 1], send_b.at[1, r], sem_b.at[1, row], dev)

    def from_b2(d):
        r, dev = peer_x(d)
        return copy(out_ref.at[:, r, 1], out_ref.at[:, r, 1], send_b.at[1, r], sem_b.at[1, r], dev)

    def to_c2(d):
        q, dev = peer_y(d)
        return copy(out_ref.at[u, :, 0], out_ref.at[u, :, 0], send_c.at[1, q], sem_c.at[1, u], dev)

    def from_c2(d):
        q, dev = peer_y(d)
        return copy(out_ref.at[q, :, 0], out_ref.at[q, :, 0], send_c.at[1, q], sem_c.at[1, q], dev)

    for d in range(1, n_rows):
        to_b1(d).start()
    for d in range(1, n_sub):
        to_c1(d).start()
    for d in range(1, n_sub):
        from_c1(d).wait_recv()
    for d in range(1, n_rows):
        to_b2(d).start()
    for d in range(1, n_rows):
        from_b1(d).wait_recv()
    for d in range(1, n_sub):
        to_c2(d).start()
    for d in range(1, n_rows):
        from_b2(d).wait_recv()
    for d in range(1, n_sub):
        from_c2(d).wait_recv()

    for d in range(1, n_sub):
        to_sub(d).wait_send()
    lax.fori_loop(1, n_row, lambda d, c: (to_a(d).wait_send(), c)[1], 0)
    for d in range(1, n_rows):
        to_b1(d).wait_send()
        to_b2(d).wait_send()
    for d in range(1, n_sub):
        to_c1(d).wait_send()
        to_c2(d).wait_send()


def gather_slots(picked, n_slab, n_sub, n_row):
    rows, width = picked.shape
    lanes = rows // n_sub * width
    n_rows = n_slab // n_row
    gathered = pl.pallas_call(
        functools.partial(gather_kernel, n_row),
        out_shape=jax.ShapeDtypeStruct((n_sub, n_rows, 2, n_row // 2, lanes), jnp.float32),
        in_specs=[pl.BlockSpec(memory_space=pltpu.VMEM)],
        out_specs=pl.BlockSpec(memory_space=pltpu.VMEM),
        scratch_shapes=[
            pltpu.VMEM((n_sub, lanes), jnp.float32),
            pltpu.SemaphoreType.DMA((n_sub,)),
            pltpu.SemaphoreType.DMA((n_sub,)),
            pltpu.SemaphoreType.DMA((n_row,)),
            pltpu.SemaphoreType.DMA((n_row,)),
            pltpu.SemaphoreType.DMA((2, n_rows)),
            pltpu.SemaphoreType.DMA((2, n_rows)),
            pltpu.SemaphoreType.DMA((2, n_sub)),
            pltpu.SemaphoreType.DMA((2, n_sub)),
        ],
        compiler_params=pltpu.CompilerParams(has_side_effects=True, collective_id=0),
    )(picked.reshape(n_sub, lanes))
    return gathered.reshape(n_sub, n_slab, lanes)


def per_device(ensemble, obs_value, obs_var, obs_owner, obs_column, home_block, batch_order):
    members = ensemble.shape[2]
    levels_count = ensemble.shape[1]
    cols_dev = ensemble.shape[3]
    slab_count = lax.axis_size("slab")
    sub_count = lax.axis_size("sub")
    slab_index = lax.axis_index("slab")
    sub_index = lax.axis_index("sub")
    capacity = CAP
    cols_slab = cols_dev * sub_count
    nblocks = cols_slab * slab_count // BLK
    span_broad = cols_slab // (4 * BLK)
    span_narrow = max(span_broad // 4, 1)
    decays = (float(span_broad), float(span_narrow))
    assert 2 * span_broad + 1 <= cols_slab // BLK and slab_count >= 3
    owners = obs_owner[:, :, 0]
    obs_home = jnp.mod((owners * cols_slab + obs_column) // BLK + home_block, nblocks)
    onehot = (owners[:, :, None] == jnp.arange(slab_count, dtype=jnp.int32)[None, None, :]).astype(
        jnp.int32
    )
    running = jnp.cumsum(onehot, axis=1) - 1
    slot_rank = jnp.sum(onehot * running, axis=2)
    slot_obs, slot_valid, slot_column = slot_table(owners, slot_rank, slab_index, capacity, obs_column)
    slot_level = slot_obs % levels_count
    holder = slot_column // cols_dev
    local_col = slot_column % cols_dev
    levels = ensemble.at[:, slot_level.reshape(-1)].get(mode="promise_in_bounds")
    retain = (slot_valid & (holder == sub_index)).reshape(-1)
    chosen = (jnp.arange(cols_dev, dtype=jnp.int32)[None, :] == local_col.reshape(-1, 1)) & retain[:, None]
    picked = jnp.sum(jnp.where(chosen[None, :, None, :], levels, 0.0), axis=3)
    picked = jnp.transpose(picked, (1, 0, 2)).reshape(BATCHES * capacity, BANDS * members)
    n_row = 32 if slab_count % 32 == 0 else slab_count
    gathered = gather_slots(picked, slab_count, sub_count, n_row)
    q_rows = BATCHES * capacity // sub_count
    width = BANDS * members
    row_of = jnp.arange(BATCHES, dtype=jnp.int32)[:, None] * capacity + slot_rank
    lines = gathered.reshape(sub_count * slab_count, q_rows * width).at[
        ((row_of // q_rows) * slab_count + owners).reshape(-1)
    ].get(mode="promise_in_bounds")
    part = (row_of % q_rows).reshape(-1, 1)
    flat_priors = lines[:, :width]
    for r in range(1, q_rows):
        flat_priors = jnp.where(part == r, lines[:, r * width : (r + 1) * width], flat_priors)
    priors = flat_priors.reshape(BATCHES, -1, width)

    turns = batch_order[:, None] == jnp.arange(BATCHES, dtype=jnp.int32)[None, :]
    first, second = turns[0], turns[1]
    y0 = pick(priors, first)
    home0 = pick(obs_home, first)
    home1 = pick(obs_home, second)
    stats0 = obs_statistics(y0, pick(obs_value, first), pick(obs_var, first), members)
    y1 = update_pool(pick(priors, second), home1, *stats0, home0, nblocks, decays)
    stats1 = obs_statistics(y1, pick(obs_value, second), pick(obs_var, second), members)
    recorded = jnp.sum(
        jnp.stack([y0, y1])[:, None] * turns.astype(jnp.float32)[:, :, None, None], axis=0
    )

    col_blocks = ((slab_index * sub_count + sub_index) * cols_dev + jnp.arange(
        cols_dev, dtype=jnp.int32
    )) // BLK
    near = jnp.mod(slab_index + jnp.arange(-1, 2, dtype=jnp.int32), slab_count)
    matches = (owners[:, None, None, :] == near[None, :, None, None]) & (
        slot_rank[:, None, None, :] == jnp.arange(capacity, dtype=jnp.int32)[None, None, :, None]
    )
    near_obs = jnp.sum(
        jnp.where(matches, jnp.arange(owners.shape[1], dtype=jnp.int32), 0), axis=3
    ).reshape(BATCHES, -1)
    near_valid = jnp.any(matches, axis=3).reshape(BATCHES, -1)
    for batch_id, homes, stats in ((first, home0, stats0), (second, home1, stats1)):
        deviations, spread, increments = stats
        table = jnp.concatenate(
            [
                deviations.reshape(-1, width),
                increments,
                spread[:, None],
                homes[:, None].astype(jnp.float32),
            ],
            axis=1,
        )
        rows = table.at[pick(near_obs, batch_id)].get(mode="promise_in_bounds")
        ensemble = update_state(
            ensemble,
            col_blocks,
            rows[:, :width].reshape(-1, BANDS, members),
            rows[:, width + members],
            rows[:, width : width + members],
            rows[:, width + members + 1].astype(jnp.int32),
            pick(near_valid.astype(jnp.int32), batch_id) > 0,
            nblocks,
            decays,
        )
    return (ensemble, recorded)


def solution(mesh):
    placed = (P(None, None, None, ("slab", "sub")), P(), P(), P(), P(), P(), P())
    return jax.shard_map(
        per_device,
        mesh=mesh,
        in_specs=placed,
        out_specs=(P(None, None, None, ("slab", "sub")), P()),
        check_vma=False,
    )
```

```python
import functools

import jax
import jax.numpy as jnp
from jax import lax
from jax.experimental import pallas as pl
from jax.experimental.pallas import tpu as pltpu
from jax.sharding import PartitionSpec as P

MESH = pl.DeviceIdType.MESH

BANDS = 2
BLK = 16
BATCHES = 2
CAP = 8


PRODUCT = lax.Precision.HIGH


def gc_weight(first, second, nblocks, length):
    block_gap = jnp.abs(first - second)
    block_gap = jnp.minimum(block_gap, nblocks - block_gap)
    scaled_gap = block_gap.astype(jnp.float32) / length
    near_part = (
        ((-0.25 * scaled_gap + 0.5) * scaled_gap + 0.625) * scaled_gap**3
        - 5.0 / 3.0 * scaled_gap**2
        + 1.0
    )
    floored = jnp.maximum(scaled_gap, 1.0)
    far_part = (
        (
            (((scaled_gap / 12.0 - 0.5) * scaled_gap + 0.625) * scaled_gap + 5.0 / 3.0) * scaled_gap
            - 5.0
        )
        * scaled_gap
        + 4.0
        - 2.0 / (3.0 * floored)
    )
    return jnp.where(scaled_gap <= 1.0, near_part, jnp.where(scaled_gap < 2.0, far_part, 0.0))


def obs_statistics(current, values, variances, members):
    banded = current.reshape(current.shape[0], BANDS, members)
    whole_obs = jnp.sum(banded, axis=1)
    centre = jnp.mean(whole_obs, axis=1, keepdims=True)
    spread = jnp.sum((whole_obs - centre) ** 2, axis=1) / (members - 1) + 1e-06
    post_var = 1.0 / (1.0 / spread + 1.0 / variances)
    post_mean = post_var * (centre[:, 0] / spread + values / variances)
    increments = (post_mean - centre[:, 0])[:, None] + (jnp.sqrt(post_var / spread) - 1.0)[
        :, None
    ] * (whole_obs - centre)
    deviations = banded - jnp.mean(banded, axis=2, keepdims=True)
    return (deviations, spread, increments)


def update_pool(pool, pool_homes, deviations, spread, increments, obs_homes, nblocks, decays):
    members = deviations.shape[2]
    banded = pool.reshape(pool.shape[0], BANDS, members)
    pool_dev = banded - jnp.mean(banded, axis=2, keepdims=True)
    weights = jnp.stack(
        [gc_weight(pool_homes[:, None], obs_homes[None, :], nblocks, decay) for decay in decays]
    ) / ((members - 1) * spread)[None, None, :]
    crossed = jnp.einsum("pbm,kbm->bpk", pool_dev, deviations, precision=PRODUCT)
    change = jnp.einsum("bpk,km->pbm", crossed * weights, increments, precision=PRODUCT)
    return (banded + change).reshape(pool.shape)


def update_state(ensemble, col_blocks, deviations, spread, increments, obs_homes, valid, nblocks, decays):
    members = ensemble.shape[2]
    layer_dev = ensemble - jnp.mean(ensemble, axis=2, keepdims=True)
    weights = jnp.stack(
        [gc_weight(col_blocks[:, None], obs_homes[None, :], nblocks, decay) for decay in decays]
    ) / ((members - 1) * spread)[None, None, :]
    weights = jnp.where(valid[None, None, :], weights, 0.0)
    crossed = jnp.einsum("blmc,kbm->blck", layer_dev, deviations, precision=PRODUCT)
    change = jnp.einsum("blck,km->blmc", crossed * weights[:, None], increments, precision=PRODUCT)
    return ensemble + change


def pick(stacked, chosen):
    weights = chosen.astype(stacked.dtype).reshape((-1,) + (1,) * (stacked.ndim - 1))
    return jnp.sum(stacked * weights, axis=0)


def slot_table(owners, slot_rank, slab_number, capacity, columns):
    obs_count = owners.shape[1]
    matches = (owners == slab_number)[:, None, :] & (
        slot_rank[:, None, :] == jnp.arange(capacity, dtype=jnp.int32)[None, :, None]
    )
    slot_obs = jnp.sum(
        jnp.where(matches, jnp.arange(obs_count, dtype=jnp.int32)[None, None, :], 0), axis=2
    )
    slot_valid = jnp.any(matches, axis=2)
    slot_column = jnp.sum(jnp.where(matches, columns[:, None, :], 0), axis=2)
    return (slot_obs, slot_valid, slot_column)


def gather_kernel(n_row, picked_ref, out_ref, part_ref, sem0, send0, sem_a, send_a, sem_b, send_b, sem_c, send_c):
    n_slab = lax.axis_size("slab")
    n_sub = lax.axis_size("sub")
    s = lax.axis_index("slab")
    u = lax.axis_index("sub")
    n_rows = n_slab // n_row
    row, loc = s // n_row, s % n_row

    def copy(src, dst, send, recv, dev):
        return pltpu.make_async_remote_copy(
            src_ref=src, dst_ref=dst, send_sem=send, recv_sem=recv, device_id=dev, device_id_type=MESH
        )

    def to_sub(d):
        q = (u + d) % n_sub
        return copy(picked_ref.at[q], part_ref.at[u], send0.at[q], sem0.at[u], (s, q))

    def from_sub(d):
        q = (u + d) % n_sub
        return copy(picked_ref.at[q], part_ref.at[q], send0.at[q], sem0.at[q], (s, q))

    barrier = pltpu.get_barrier_semaphore()
    for d in range(1, n_sub):
        pl.semaphore_signal(barrier, 1, device_id=(s, (u + d) % n_sub), device_id_type=MESH)

    def greet(d, c):
        dev = (row * n_row + (loc + d) % n_row, u)
        pl.semaphore_signal(barrier, 1, device_id=dev, device_id_type=MESH)
        return c

    lax.fori_loop(1, n_row, greet, 0)
    for d in range(1, n_rows):
        dev = (((row + d) % n_rows) * n_row + loc, u)
        pl.semaphore_signal(barrier, 1, device_id=dev, device_id_type=MESH)
    pl.semaphore_wait(barrier, (n_sub - 1) + (n_row - 1) + (n_rows - 1))

    for d in range(1, n_sub):
        to_sub(d).start()
    total = picked_ref[pl.ds(u, 1), :]
    for d in range(1, n_sub):
        from_sub(d).wait_recv()
        total = total + part_ref[pl.ds((u + d) % n_sub, 1), :]
    half = n_row // 2

    def own(t):
        j = t % n_row
        return out_ref.at[u, t // n_row, j // half, pl.ds(j % half, 1)]

    own(s)[...] = total

    def to_a(d):
        j = (loc + d) % n_row
        return copy(own(s), own(s), send_a.at[j], sem_a.at[loc], (row * n_row + j, u))

    def from_a(d):
        j = (loc + d) % n_row
        src = row * n_row + j
        return copy(own(src), own(src), send_a.at[j], sem_a.at[j], (src, u))

    def start_a(d, c):
        to_a(d).start()
        return c

    def wait_a(d, c):
        from_a(d).wait_recv()
        return c

    lax.fori_loop(1, n_row, start_a, 0)
    lax.fori_loop(1, n_row, wait_a, 0)

    def peer_x(d):
        r = (row + d) % n_rows
        return r, (r * n_row + loc, u)

    def peer_y(d):
        q = (u + d) % n_sub
        return q, (s, q)

    def to_b1(d):
        r, dev = peer_x(d)
        return copy(out_ref.at[u, row, 0], out_ref.at[u, row, 0], send_b.at[0, r], sem_b.at[0, row], dev)

    def from_b1(d):
        r, dev = peer_x(d)
        return copy(out_ref.at[u, r, 0], out_ref.at[u, r, 0], send_b.at[0, r], sem_b.at[0, r], dev)

    def to_c1(d):
        q, dev = peer_y(d)
        return copy(out_ref.at[u, row, 1], out_ref.at[u, row, 1], send_c.at[0, q], sem_c.at[0, u], dev)

    def from_c1(d):
        q, dev = peer_y(d)
        return copy(out_ref.at[q, row, 1], out_ref.at[q, row, 1], send_c.at[0, q], sem_c.at[0, q], dev)

    def to_b2(d):
        r, dev = peer_x(d)
        return copy(out_ref.at[:, row, 1], out_ref.at[:, row, 1], send_b.at[1, r], sem_b.at[1, row], dev)

    def from_b2(d):
        r, dev = peer_x(d)
        return copy(out_ref.at[:, r, 1], out_ref.at[:, r, 1], send_b.at[1, r], sem_b.at[1, r], dev)

    def to_c2(d):
        q, dev = peer_y(d)
        return copy(out_ref.at[u, :, 0], out_ref.at[u, :, 0], send_c.at[1, q], sem_c.at[1, u], dev)

    def from_c2(d):
        q, dev = peer_y(d)
        return copy(out_ref.at[q, :, 0], out_ref.at[q, :, 0], send_c.at[1, q], sem_c.at[1, q], dev)

    for d in range(1, n_rows):
        to_b1(d).start()
    for d in range(1, n_sub):
        to_c1(d).start()
    for d in range(1, n_sub):
        from_c1(d).wait_recv()
    for d in range(1, n_rows):
        to_b2(d).start()
    for d in range(1, n_rows):
        from_b1(d).wait_recv()
    for d in range(1, n_sub):
        to_c2(d).start()
    for d in range(1, n_rows):
        from_b2(d).wait_recv()
    for d in range(1, n_sub):
        from_c2(d).wait_recv()

    for d in range(1, n_sub):
        to_sub(d).wait_send()
    lax.fori_loop(1, n_row, lambda d, c: (to_a(d).wait_send(), c)[1], 0)
    for d in range(1, n_rows):
        to_b1(d).wait_send()
        to_b2(d).wait_send()
    for d in range(1, n_sub):
        to_c1(d).wait_send()
        to_c2(d).wait_send()


def gather_slots(picked, n_slab, n_sub, n_row):
    rows, width = picked.shape
    lanes = rows // n_sub * width
    n_rows = n_slab // n_row
    gathered = pl.pallas_call(
        functools.partial(gather_kernel, n_row),
        out_shape=jax.ShapeDtypeStruct((n_sub, n_rows, 2, n_row // 2, lanes), jnp.float32),
        in_specs=[pl.BlockSpec(memory_space=pltpu.VMEM)],
        out_specs=pl.BlockSpec(memory_space=pltpu.VMEM),
        scratch_shapes=[
            pltpu.VMEM((n_sub, lanes), jnp.float32),
            pltpu.SemaphoreType.DMA((n_sub,)),
            pltpu.SemaphoreType.DMA((n_sub,)),
            pltpu.SemaphoreType.DMA((n_row,)),
            pltpu.SemaphoreType.DMA((n_row,)),
            pltpu.SemaphoreType.DMA((2, n_rows)),
            pltpu.SemaphoreType.DMA((2, n_rows)),
            pltpu.SemaphoreType.DMA((2, n_sub)),
            pltpu.SemaphoreType.DMA((2, n_sub)),
        ],
        compiler_params=pltpu.CompilerParams(has_side_effects=True, collective_id=0),
    )(picked.reshape(n_sub, lanes))
    return gathered.reshape(n_sub, n_slab, lanes)


def per_device(ensemble, obs_value, obs_var, obs_owner, obs_column, home_block, batch_order):
    members = ensemble.shape[2]
    levels_count = ensemble.shape[1]
    cols_dev = ensemble.shape[3]
    slab_count = lax.axis_size("slab")
    sub_count = lax.axis_size("sub")
    slab_index = lax.axis_index("slab")
    sub_index = lax.axis_index("sub")
    capacity = CAP
    cols_slab = cols_dev * sub_count
    nblocks = cols_slab * slab_count // BLK
    span_broad = cols_slab // (4 * BLK)
    span_narrow = max(span_broad // 4, 1)
    decays = (float(span_broad), float(span_narrow))
    assert 2 * span_broad + 1 <= cols_slab // BLK and slab_count >= 3
    owners = obs_owner[:, :, 0]
    obs_home = jnp.mod((owners * cols_slab + obs_column) // BLK + home_block, nblocks)
    onehot = (owners[:, :, None] == jnp.arange(slab_count, dtype=jnp.int32)[None, None, :]).astype(
        jnp.int32
    )
    running = jnp.cumsum(onehot, axis=1) - 1
    slot_rank = jnp.sum(onehot * running, axis=2)
    slot_obs, slot_valid, slot_column = slot_table(owners, slot_rank, slab_index, capacity, obs_column)
    slot_level = slot_obs % levels_count
    holder = slot_column // cols_dev
    local_col = slot_column % cols_dev
    levels = ensemble.at[:, slot_level.reshape(-1)].get(mode="promise_in_bounds")
    retain = (slot_valid & (holder == sub_index)).reshape(-1)
    chosen = (jnp.arange(cols_dev, dtype=jnp.int32)[None, :] == local_col.reshape(-1, 1)) & retain[:, None]
    picked = jnp.sum(jnp.where(chosen[None, :, None, :], levels, 0.0), axis=3)
    picked = jnp.transpose(picked, (1, 0, 2)).reshape(BATCHES * capacity, BANDS * members)
    n_row = 32 if slab_count % 32 == 0 else slab_count
    gathered = gather_slots(picked, slab_count, sub_count, n_row)
    q_rows = BATCHES * capacity // sub_count
    width = BANDS * members
    row_of = jnp.arange(BATCHES, dtype=jnp.int32)[:, None] * capacity + slot_rank
    turns = batch_order[:, None] == jnp.arange(BATCHES, dtype=jnp.int32)[None, :]
    first, second = turns[0], turns[1]
    line_of = (row_of // q_rows) * slab_count + owners
    part_of = row_of % q_rows
    turn_line = jnp.stack([pick(line_of, turns[t]) for t in range(BATCHES)])
    turn_part = jnp.stack([pick(part_of, turns[t]) for t in range(BATCHES)])
    lines = gathered.reshape(sub_count * slab_count, q_rows * width).at[
        turn_line.reshape(-1)
    ].get(mode="promise_in_bounds")
    part = turn_part.reshape(-1, 1)
    flat_priors = lines[:, :width]
    for r in range(1, q_rows):
        flat_priors = jnp.where(part == r, lines[:, r * width : (r + 1) * width], flat_priors)
    turn_priors = flat_priors.reshape(BATCHES, -1, width)

    y0 = turn_priors[0]
    home0 = pick(obs_home, first)
    home1 = pick(obs_home, second)
    stats0 = obs_statistics(y0, pick(obs_value, first), pick(obs_var, first), members)
    y1 = update_pool(turn_priors[1], home1, *stats0, home0, nblocks, decays)
    stats1 = obs_statistics(y1, pick(obs_value, second), pick(obs_var, second), members)
    recorded = jnp.sum(
        jnp.stack([y0, y1])[:, None] * turns.astype(jnp.float32)[:, :, None, None], axis=0
    )

    col_blocks = ((slab_index * sub_count + sub_index) * cols_dev + jnp.arange(
        cols_dev, dtype=jnp.int32
    )) // BLK
    near = jnp.mod(slab_index + jnp.arange(-1, 2, dtype=jnp.int32), slab_count)
    matches = (owners[:, None, None, :] == near[None, :, None, None]) & (
        slot_rank[:, None, None, :] == jnp.arange(capacity, dtype=jnp.int32)[None, None, :, None]
    )
    near_obs = jnp.sum(
        jnp.where(matches, jnp.arange(owners.shape[1], dtype=jnp.int32), 0), axis=3
    ).reshape(BATCHES, -1)
    near_valid = jnp.any(matches, axis=3).reshape(BATCHES, -1)
    for batch_id, homes, stats in ((first, home0, stats0), (second, home1, stats1)):
        deviations, spread, increments = stats
        table = jnp.concatenate(
            [
                deviations.reshape(-1, width),
                increments,
                spread[:, None],
                homes[:, None].astype(jnp.float32),
            ],
            axis=1,
        )
        rows = table.at[pick(near_obs, batch_id)].get(mode="promise_in_bounds")
        ensemble = update_state(
            ensemble,
            col_blocks,
            rows[:, :width].reshape(-1, BANDS, members),
            rows[:, width + members],
            rows[:, width : width + members],
            rows[:, width + members + 1].astype(jnp.int32),
            pick(near_valid.astype(jnp.int32), batch_id) > 0,
            nblocks,
            decays,
        )
    return (ensemble, recorded)


def solution(mesh):
    placed = (P(None, None, None, ("slab", "sub")), P(), P(), P(), P(), P(), P())
    return jax.shard_map(
        per_device,
        mesh=mesh,
        in_specs=placed,
        out_specs=(P(None, None, None, ("slab", "sub")), P()),
        check_vma=False,
    )
```

```python
import functools

import jax
import jax.numpy as jnp
from jax import lax
from jax.experimental import pallas as pl
from jax.experimental.pallas import tpu as pltpu
from jax.sharding import PartitionSpec as P

MESH = pl.DeviceIdType.MESH

BANDS = 2
BLK = 16
BATCHES = 2
CAP = 8


PRODUCT = lax.Precision.HIGH


def gc_weight(first, second, nblocks, length):
    block_gap = jnp.abs(first - second)
    block_gap = jnp.minimum(block_gap, nblocks - block_gap)
    scaled_gap = block_gap.astype(jnp.float32) / length
    near_part = (
        ((-0.25 * scaled_gap + 0.5) * scaled_gap + 0.625) * scaled_gap**3
        - 5.0 / 3.0 * scaled_gap**2
        + 1.0
    )
    floored = jnp.maximum(scaled_gap, 1.0)
    far_part = (
        (
            (((scaled_gap / 12.0 - 0.5) * scaled_gap + 0.625) * scaled_gap + 5.0 / 3.0) * scaled_gap
            - 5.0
        )
        * scaled_gap
        + 4.0
        - 2.0 / (3.0 * floored)
    )
    return jnp.where(scaled_gap <= 1.0, near_part, jnp.where(scaled_gap < 2.0, far_part, 0.0))


def obs_statistics(current, values, variances, members):
    banded = current.reshape(current.shape[0], BANDS, members)
    whole_obs = jnp.sum(banded, axis=1)
    centre = jnp.mean(whole_obs, axis=1, keepdims=True)
    spread = jnp.sum((whole_obs - centre) ** 2, axis=1) / (members - 1) + 1e-06
    post_var = 1.0 / (1.0 / spread + 1.0 / variances)
    post_mean = post_var * (centre[:, 0] / spread + values / variances)
    increments = (post_mean - centre[:, 0])[:, None] + (jnp.sqrt(post_var / spread) - 1.0)[
        :, None
    ] * (whole_obs - centre)
    deviations = banded - jnp.mean(banded, axis=2, keepdims=True)
    return (deviations, spread, increments)


def update_pool(pool, pool_homes, deviations, spread, increments, obs_homes, nblocks, decays):
    members = deviations.shape[2]
    banded = pool.reshape(pool.shape[0], BANDS, members)
    pool_dev = banded - jnp.mean(banded, axis=2, keepdims=True)
    weights = jnp.stack(
        [gc_weight(pool_homes[:, None], obs_homes[None, :], nblocks, decay) for decay in decays]
    ) / ((members - 1) * spread)[None, None, :]
    crossed = jnp.einsum("pbm,kbm->bpk", pool_dev, deviations, precision=PRODUCT)
    change = jnp.einsum("bpk,km->pbm", crossed * weights, increments, precision=PRODUCT)
    return (banded + change).reshape(pool.shape)


def update_state(ensemble, col_blocks, deviations, spread, increments, obs_homes, valid, nblocks, decays):
    members = ensemble.shape[2]
    layer_dev = ensemble - jnp.mean(ensemble, axis=2, keepdims=True)
    weights = jnp.stack(
        [gc_weight(col_blocks[:, None], obs_homes[None, :], nblocks, decay) for decay in decays]
    ) / ((members - 1) * spread)[None, None, :]
    weights = jnp.where(valid[None, None, :], weights, 0.0)
    crossed = jnp.einsum("blmc,kbm->blck", layer_dev, deviations, precision=PRODUCT)
    change = jnp.einsum("blck,km->blmc", crossed * weights[:, None], increments, precision=PRODUCT)
    return ensemble + change


def pick(stacked, chosen):
    weights = chosen.astype(stacked.dtype).reshape((-1,) + (1,) * (stacked.ndim - 1))
    return jnp.sum(stacked * weights, axis=0)


def slot_table(owners, slot_rank, slab_number, capacity, columns):
    obs_count = owners.shape[1]
    matches = (owners == slab_number)[:, None, :] & (
        slot_rank[:, None, :] == jnp.arange(capacity, dtype=jnp.int32)[None, :, None]
    )
    slot_obs = jnp.sum(
        jnp.where(matches, jnp.arange(obs_count, dtype=jnp.int32)[None, None, :], 0), axis=2
    )
    slot_valid = jnp.any(matches, axis=2)
    slot_column = jnp.sum(jnp.where(matches, columns[:, None, :], 0), axis=2)
    return (slot_obs, slot_valid, slot_column)


def gather_kernel(n_row, picked_ref, out_ref, part_ref, sem0, send0, sem_a, send_a, sem_b, send_b, sem_c, send_c):
    n_slab = lax.axis_size("slab")
    n_sub = lax.axis_size("sub")
    s = lax.axis_index("slab")
    u = lax.axis_index("sub")
    n_rows = n_slab // n_row
    row, loc = s // n_row, s % n_row

    def copy(src, dst, send, recv, dev):
        return pltpu.make_async_remote_copy(
            src_ref=src, dst_ref=dst, send_sem=send, recv_sem=recv, device_id=dev, device_id_type=MESH
        )

    def to_sub(d):
        q = (u + d) % n_sub
        return copy(picked_ref.at[q], part_ref.at[u], send0.at[q], sem0.at[u], (s, q))

    def from_sub(d):
        q = (u + d) % n_sub
        return copy(picked_ref.at[q], part_ref.at[q], send0.at[q], sem0.at[q], (s, q))

    barrier = pltpu.get_barrier_semaphore()
    for d in range(1, n_sub):
        pl.semaphore_signal(barrier, 1, device_id=(s, (u + d) % n_sub), device_id_type=MESH)

    def greet(d, c):
        dev = (row * n_row + (loc + d) % n_row, u)
        pl.semaphore_signal(barrier, 1, device_id=dev, device_id_type=MESH)
        return c

    lax.fori_loop(1, n_row, greet, 0)
    for d in range(1, n_rows):
        dev = (((row + d) % n_rows) * n_row + loc, u)
        pl.semaphore_signal(barrier, 1, device_id=dev, device_id_type=MESH)
    pl.semaphore_wait(barrier, (n_sub - 1) + (n_row - 1) + (n_rows - 1))

    for d in range(1, n_sub):
        to_sub(d).start()
    total = picked_ref[pl.ds(u, 1), :]
    for d in range(1, n_sub):
        from_sub(d).wait_recv()
        total = total + part_ref[pl.ds((u + d) % n_sub, 1), :]
    half = n_row // 2

    def own(t):
        j = t % n_row
        return out_ref.at[u, t // n_row, j // half, pl.ds(j % half, 1)]

    own(s)[...] = total

    def to_a(d):
        j = (loc + d) % n_row
        return copy(own(s), own(s), send_a.at[j], sem_a.at[loc], (row * n_row + j, u))

    def from_a(d):
        j = (loc + d) % n_row
        src = row * n_row + j
        return copy(own(src), own(src), send_a.at[j], sem_a.at[j], (src, u))

    def start_a(d, c):
        to_a(d).start()
        return c

    def wait_a(d, c):
        from_a(d).wait_recv()
        return c

    lax.fori_loop(1, n_row, start_a, 0)
    lax.fori_loop(1, n_row, wait_a, 0)

    def peer_x(d):
        r = (row + d) % n_rows
        return r, (r * n_row + loc, u)

    def peer_y(d):
        q = (u + d) % n_sub
        return q, (s, q)

    def to_b1(d):
        r, dev = peer_x(d)
        return copy(out_ref.at[u, row, 0], out_ref.at[u, row, 0], send_b.at[0, r], sem_b.at[0, row], dev)

    def from_b1(d):
        r, dev = peer_x(d)
        return copy(out_ref.at[u, r, 0], out_ref.at[u, r, 0], send_b.at[0, r], sem_b.at[0, r], dev)

    def to_c1(d):
        q, dev = peer_y(d)
        return copy(out_ref.at[u, row, 1], out_ref.at[u, row, 1], send_c.at[0, q], sem_c.at[0, u], dev)

    def from_c1(d):
        q, dev = peer_y(d)
        return copy(out_ref.at[q, row, 1], out_ref.at[q, row, 1], send_c.at[0, q], sem_c.at[0, q], dev)

    def to_b2(d):
        r, dev = peer_x(d)
        return copy(out_ref.at[:, row, 1], out_ref.at[:, row, 1], send_b.at[1, r], sem_b.at[1, row], dev)

    def from_b2(d):
        r, dev = peer_x(d)
        return copy(out_ref.at[:, r, 1], out_ref.at[:, r, 1], send_b.at[1, r], sem_b.at[1, r], dev)

    def to_c2(d):
        q, dev = peer_y(d)
        return copy(out_ref.at[u, :, 0], out_ref.at[u, :, 0], send_c.at[1, q], sem_c.at[1, u], dev)

    def from_c2(d):
        q, dev = peer_y(d)
        return copy(out_ref.at[q, :, 0], out_ref.at[q, :, 0], send_c.at[1, q], sem_c.at[1, q], dev)

    for d in range(1, n_rows):
        to_b1(d).start()
    for d in range(1, n_sub):
        to_c1(d).start()
    for d in range(1, n_sub):
        from_c1(d).wait_recv()
    for d in range(1, n_rows):
        to_b2(d).start()
    for d in range(1, n_rows):
        from_b1(d).wait_recv()
    for d in range(1, n_sub):
        to_c2(d).start()
    for d in range(1, n_rows):
        from_b2(d).wait_recv()
    for d in range(1, n_sub):
        from_c2(d).wait_recv()

    for d in range(1, n_sub):
        to_sub(d).wait_send()
    lax.fori_loop(1, n_row, lambda d, c: (to_a(d).wait_send(), c)[1], 0)
    for d in range(1, n_rows):
        to_b1(d).wait_send()
        to_b2(d).wait_send()
    for d in range(1, n_sub):
        to_c1(d).wait_send()
        to_c2(d).wait_send()


def gather_slots(picked, n_slab, n_sub, n_row):
    rows, width = picked.shape
    lanes = rows // n_sub * width
    n_rows = n_slab // n_row
    gathered = pl.pallas_call(
        functools.partial(gather_kernel, n_row),
        out_shape=jax.ShapeDtypeStruct((n_sub, n_rows, 2, n_row // 2, lanes), jnp.float32),
        in_specs=[pl.BlockSpec(memory_space=pltpu.VMEM)],
        out_specs=pl.BlockSpec(memory_space=pltpu.VMEM),
        scratch_shapes=[
            pltpu.VMEM((n_sub, lanes), jnp.float32),
            pltpu.SemaphoreType.DMA((n_sub,)),
            pltpu.SemaphoreType.DMA((n_sub,)),
            pltpu.SemaphoreType.DMA((n_row,)),
            pltpu.SemaphoreType.DMA((n_row,)),
            pltpu.SemaphoreType.DMA((2, n_rows)),
            pltpu.SemaphoreType.DMA((2, n_rows)),
            pltpu.SemaphoreType.DMA((2, n_sub)),
            pltpu.SemaphoreType.DMA((2, n_sub)),
        ],
        compiler_params=pltpu.CompilerParams(has_side_effects=True, collective_id=0),
    )(picked.reshape(n_sub, lanes))
    return gathered.reshape(n_sub, n_slab, lanes)


def per_device(ensemble, obs_value, obs_var, obs_owner, obs_column, home_block, batch_order):
    members = ensemble.shape[2]
    levels_count = ensemble.shape[1]
    cols_dev = ensemble.shape[3]
    slab_count = lax.axis_size("slab")
    sub_count = lax.axis_size("sub")
    slab_index = lax.axis_index("slab")
    sub_index = lax.axis_index("sub")
    capacity = CAP
    cols_slab = cols_dev * sub_count
    nblocks = cols_slab * slab_count // BLK
    span_broad = cols_slab // (4 * BLK)
    span_narrow = max(span_broad // 4, 1)
    decays = (float(span_broad), float(span_narrow))
    assert 2 * span_broad + 1 <= cols_slab // BLK and slab_count >= 3
    owners = obs_owner[:, :, 0]
    obs_home = jnp.mod((owners * cols_slab + obs_column) // BLK + home_block, nblocks)
    onehot = (owners[:, :, None] == jnp.arange(slab_count, dtype=jnp.int32)[None, None, :]).astype(
        jnp.int32
    )
    running = jnp.cumsum(onehot, axis=1) - 1
    slot_rank = jnp.sum(onehot * running, axis=2)
    slot_obs, slot_valid, slot_column = slot_table(owners, slot_rank, slab_index, capacity, obs_column)
    slot_level = slot_obs % levels_count
    holder = slot_column // cols_dev
    local_col = slot_column % cols_dev
    levels = ensemble.at[:, slot_level.reshape(-1)].get(mode="promise_in_bounds")
    retain = (slot_valid & (holder == sub_index)).reshape(-1)
    chosen = (jnp.arange(cols_dev, dtype=jnp.int32)[None, :] == local_col.reshape(-1, 1)) & retain[:, None]
    picked = jnp.sum(jnp.where(chosen[None, :, None, :], levels, 0.0), axis=3)
    picked = jnp.transpose(picked, (1, 0, 2)).reshape(BATCHES * capacity, BANDS * members)
    n_row = 32 if slab_count % 32 == 0 else slab_count
    gathered = gather_slots(picked, slab_count, sub_count, n_row)
    q_rows = BATCHES * capacity // sub_count
    width = BANDS * members
    row_of = jnp.arange(BATCHES, dtype=jnp.int32)[:, None] * capacity + slot_rank
    turns = batch_order[:, None] == jnp.arange(BATCHES, dtype=jnp.int32)[None, :]
    first, second = turns[0], turns[1]
    line_of = (row_of // q_rows) * slab_count + owners
    part_of = row_of % q_rows
    turn_line = jnp.stack([pick(line_of, turns[t]) for t in range(BATCHES)])
    turn_part = jnp.stack([pick(part_of, turns[t]) for t in range(BATCHES)])
    lines = gathered.reshape(sub_count * slab_count, q_rows * width).at[
        turn_line.reshape(-1)
    ].get(mode="promise_in_bounds")
    part = turn_part.reshape(-1, 1)
    flat_priors = lines[:, :width]
    for r in range(1, q_rows):
        flat_priors = jnp.where(part == r, lines[:, r * width : (r + 1) * width], flat_priors)
    turn_priors = flat_priors.reshape(BATCHES, -1, width)

    y0 = turn_priors[0]
    home0 = pick(obs_home, first)
    home1 = pick(obs_home, second)
    stats0 = obs_statistics(y0, pick(obs_value, first), pick(obs_var, first), members)
    y1 = update_pool(turn_priors[1], home1, *stats0, home0, nblocks, decays)
    stats1 = obs_statistics(y1, pick(obs_value, second), pick(obs_var, second), members)
    recorded = jnp.where(first[:, None, None], y0[None], y1[None])

    col_blocks = ((slab_index * sub_count + sub_index) * cols_dev + jnp.arange(
        cols_dev, dtype=jnp.int32
    )) // BLK
    near = jnp.mod(slab_index + jnp.arange(-1, 2, dtype=jnp.int32), slab_count)
    matches = (owners[:, None, None, :] == near[None, :, None, None]) & (
        slot_rank[:, None, None, :] == jnp.arange(capacity, dtype=jnp.int32)[None, None, :, None]
    )
    near_obs = jnp.sum(
        jnp.where(matches, jnp.arange(owners.shape[1], dtype=jnp.int32), 0), axis=3
    ).reshape(BATCHES, -1)
    near_valid = jnp.any(matches, axis=3).reshape(BATCHES, -1)
    for batch_id, homes, stats in ((first, home0, stats0), (second, home1, stats1)):
        deviations, spread, increments = stats
        table = jnp.concatenate(
            [
                deviations.reshape(-1, width),
                increments,
                spread[:, None],
                homes[:, None].astype(jnp.float32),
            ],
            axis=1,
        )
        rows = table.at[pick(near_obs, batch_id)].get(mode="promise_in_bounds")
        ensemble = update_state(
            ensemble,
            col_blocks,
            rows[:, :width].reshape(-1, BANDS, members),
            rows[:, width + members],
            rows[:, width : width + members],
            rows[:, width + members + 1].astype(jnp.int32),
            pick(near_valid.astype(jnp.int32), batch_id) > 0,
            nblocks,
            decays,
        )
    return (ensemble, recorded)


def solution(mesh):
    placed = (P(None, None, None, ("slab", "sub")), P(), P(), P(), P(), P(), P())
    return jax.shard_map(
        per_device,
        mesh=mesh,
        in_specs=placed,
        out_specs=(P(None, None, None, ("slab", "sub")), P()),
        check_vma=False,
    )
```
